128 devices in a mesh: coef: 8 (over z, core), track: 16 (over y, x).
Axes of the slice: x: 4, y: 4, z: 4, core: 2. Of those that a mesh axis runs over, the one named last changes fastest.
Arguments:
- probes: bfloat16 [2, 640, 128, 1200], P(None, 'coef', 'track'), may hold values from -6 to 6
- legendre: bfloat16 [640, 64, 1200], P('coef'), may hold values from -0.1875 to 0.1875
- order_map: int32 [640], replicated, may hold values from 0 to 639, each once
- tile_index: int32 [8, 16, 24], P('coef'), may hold values from 0 to 79
- tile_count: int32 [8, 16], P('coef'), may hold values from 1 to 24, 192 in all within a row
- base_offset: int32 [8, 16, 24, 512], P('coef', 'track'), may hold values from 0 to 127
- stencil_weight: bfloat16 [8, 16, 24, 4, 512], P('coef', 'track'), may hold values from -0.5 to 1.5
- obs_weight: float32 [8, 16, 24, 512], P('coef', 'track'), may hold values from 0.1 to 10
Outputs:
- panel: float32 [2, 640, 128, 1200], P(None, ('coef', 'track'))
- factor: float32 [128, 128], replicated
The draws below stay inside these ranges and needn't reach their ends.
Inputs may be any that keep to these rules, and one draw needn't show every extreme that they name: `tile_count`: in each coef row the counts sum to 192; slots of an owner at or past its count are unused. `order_map`: each order appears in exactly one slot.
All inputs are finite; a program needn't handle non-finite values.
Results may differ from the reference program's by a relative error of at most 0.0045.
Values may be sent and summed in bfloat16 or wider, within the bound.
A program may use at most 128 MiB of HBM per device.

```python
import math
import jax
import jax.numpy as jnp
import numpy as np
from jax import lax

NDEG = 1200
ORDERS = 640
NLON = 1280
PROBES = 128
LAT_DEV = 8
CAP = 24
OBS = 512
NLAT = 64
TILES_BAND = 80
N_COEF = 8
N_TRACK = 16


def touch_ends(drawn, key, low, top_value):
    dims = drawn.shape
    spot = [jax.random.randint(jax.random.fold_in(key, axis), (), 0, dims[axis]) for axis in range(len(dims))]
    drawn = drawn.at[tuple(spot)].set(low)
    longest = dims.index(max(dims))
    spot[longest] = (spot[longest] + 1) % dims[longest]
    return drawn.at[tuple(spot)].set(top_value)


def steps_of(key, dims, shards, smallest, top_value):
    gain, own = 1.0, jax.random.fold_in(key, 6)
    for dim, blocks in shards:
        steps = jnp.exp(jax.random.uniform(jax.random.fold_in(own, dim), (blocks,), jnp.float32, smallest / len(shards), top_value / len(shards)))
        gain = gain * jnp.repeat(steps, dims[dim] // blocks).reshape([-1 if axis == dim else 1 for axis in range(len(dims))])
    return gain


def length_profile(number_of, total, bound, skew):
    weights = [(1 << 20) // math.isqrt(rank ** skew) + 1 for rank in range(2, number_of + 1)]
    spare, holding = total - bound - (number_of - 1), [1] * (number_of - 1)
    while spare > 0:
        movable = [i for i in range(number_of - 1) if holding[i] < bound]
        mass, budget = sum([weights[i] for i in movable]), spare
        for i in movable:
            addition = min(bound - holding[i], max(1, budget * weights[i] // mass), spare)
            holding[i] = holding[i] + addition
            spare = spare - addition
    return np.array([bound] + holding)


def uneven(stream_key, amount, total, bound, lean):
    if amount == 2:
        one = jax.random.randint(stream_key, (), max(1, total - bound), min(bound, total - 1) + 1)
        return jnp.stack([one, total - one])
    sizes = jnp.asarray(length_profile(amount, total, bound, lean), jnp.int32)
    twos = (amount - 1) // 2
    giver, taker = sizes[1:1 + 2 * twos:2], sizes[2:2 + 2 * twos:2]
    margin = jnp.minimum(giver - 1, bound - taker)
    moved = jax.random.randint(jax.random.fold_in(stream_key, 1), (twos,), 0, 1 << 20) % (margin + 1)
    sizes = sizes.at[1:1 + 2 * twos:2].set(giver - moved).at[2:2 + 2 * twos:2].set(taker + moved)
    return sizes[jax.random.permutation(jax.random.fold_in(stream_key, 2), amount)]


def normal_values(rng, extent, scale, reach, split=(), kind=jnp.bfloat16):
    drawn = scale * jax.random.normal(rng, extent, jnp.float32)
    if split:
        drawn = drawn * steps_of(rng, extent, split, -0.22, 0.18)
    return jnp.clip(drawn, -reach, reach).astype(kind)


def setup_inputs(seed: int = 0) -> dict:
    streams_of = jax.random.split(jax.random.key(seed), 9)
    probes = normal_values(streams_of[0], (2, ORDERS, PROBES, NDEG), 1.0, 6.0, ((1, 8), (2, 16)))
    legendre = normal_values(streams_of[1], (ORDERS, NLAT, NDEG), NDEG ** -0.5, 0.1875, ((0, 8),))
    order_map = jax.random.permutation(streams_of[2], ORDERS).astype(jnp.int32)
    tile_index = touch_ends(jax.random.randint(streams_of[3], (N_COEF, N_TRACK, CAP), 0, TILES_BAND), jax.random.fold_in(streams_of[3], 1), 0, TILES_BAND - 1).astype(jnp.int32)
    tile_count = jax.vmap(lambda own: uneven(own, N_TRACK, N_TRACK * CAP // 2, CAP, 2))(jax.random.split(streams_of[4], N_COEF)).reshape((N_COEF, N_TRACK)).astype(jnp.int32)
    base_offset = touch_ends(jax.random.randint(streams_of[5], (N_COEF, N_TRACK, CAP, OBS), 0, 128), jax.random.fold_in(streams_of[5], 1), 0, 127).astype(jnp.int32)
    stencil_weight = jnp.clip(-0.5 + 2.0 * jax.random.uniform(streams_of[6], (N_COEF, N_TRACK, CAP, 4, OBS), jnp.float32) ** steps_of(streams_of[6], (N_COEF, N_TRACK, CAP, 4, OBS), ((0, 8), (1, 16)), -0.2, 0.2), -0.5, 1.5).astype(jnp.bfloat16)
    obs_weight = jnp.clip(jnp.exp(math.log(10.0) - 4.6051702 * jax.random.uniform(streams_of[7], (N_COEF, N_TRACK, CAP, OBS), jnp.float32) ** steps_of(streams_of[7], (N_COEF, N_TRACK, CAP, OBS), ((0, 8), (1, 16)), -0.2, 0.2)), 0.1, 10.0)
    return {"probes": probes, "legendre": legendre, "order_map": order_map, "tile_index": tile_index, "tile_count": tile_count, "base_offset": base_offset, "stencil_weight": stencil_weight, "obs_weight": obs_weight}


HIGHEST = lax.Precision.HIGHEST

def trig_tables(order_slots):
    longitude = jnp.arange(NLON, dtype=jnp.int32)
    phase = order_slots.astype(jnp.int32)[:, None] * longitude[None, :] % NLON
    angle = phase.astype(jnp.float32) * jnp.float32(2.0 * math.pi / NLON)
    scale = jnp.float32(1.0 / math.sqrt(ORDERS))
    return jnp.stack([jnp.cos(angle) * scale, jnp.sin(angle) * scale])

def stencil_matrix(base, weights):
    points = jnp.arange(128, dtype=jnp.int32)
    summed = jnp.zeros(base.shape + (128,), jnp.float32)
    for i in range(4):
        matches = (((base + i) % 128)[..., None] == points).astype(jnp.float32)
        summed = summed + weights[..., i, :, None].astype(jnp.float32) * matches
    return summed.astype(jnp.bfloat16)

def owner_row(inputs):
    band_tiles, index_rows, count_row, base_row, weight_row, noise_row = inputs
    picked = band_tiles[index_rows].astype(jnp.float32)
    stencil = stencil_matrix(base_row, weight_row).astype(jnp.float32)
    values = jnp.einsum('tsoq,tspq->tsop', stencil, picked)
    live = (jnp.arange(CAP, dtype=jnp.int32)[None, :] < count_row[:, None]).astype(jnp.float32)
    resid = (values * noise_row[..., None] * live[:, :, None, None]).astype(jnp.bfloat16)
    adjoint = jnp.einsum('tsoq,tsop->tspq', stencil, resid.astype(jnp.float32)).astype(jnp.bfloat16)
    selector = (index_rows[..., None] == jnp.arange(TILES_BAND, dtype=jnp.int32)).astype(jnp.float32)
    return jnp.einsum('tsj,tspq->jpq', selector, adjoint.astype(jnp.float32))

def reference(probes, legendre, order_map, tile_index, tile_count, base_offset, stencil_weight, obs_weight):
    tables = trig_tables(order_map)
    lat_coef = jnp.einsum('cmpl,mal->cmpa', probes.astype(jnp.float32), legendre.astype(jnp.float32))
    grid = jnp.einsum('cmpa,cmn->apn', lat_coef, tables, precision=HIGHEST)
    blocks = NLON // 128
    tiles = grid.astype(jnp.bfloat16).reshape(N_COEF, LAT_DEV, PROBES, blocks, 128)
    tiles = tiles.transpose(0, 1, 3, 2, 4).reshape(N_COEF, LAT_DEV * blocks, PROBES, 128)
    adjoint_tiles = lax.map(owner_row, (tiles, tile_index, tile_count, base_offset, stencil_weight, obs_weight))
    adjoint_grid = adjoint_tiles.reshape(N_COEF * LAT_DEV, blocks, PROBES, 128)
    shaped_tables = tables.reshape(2, ORDERS, blocks, 128)
    spectra = jnp.einsum('cmbq,abpq->cmpa', shaped_tables, adjoint_grid, precision=HIGHEST).astype(jnp.bfloat16)
    panel_rows = jnp.einsum('cmpa,mal->cmpl', spectra.astype(jnp.float32), legendre.astype(jnp.float32))
    gram = jnp.einsum('cmpl,cmql->pq', panel_rows, panel_rows, precision=HIGHEST) / (2 * ORDERS * NDEG)
    lower = jnp.linalg.cholesky(gram)
    inverse = jax.scipy.linalg.solve_triangular(lower, jnp.eye(PROBES, dtype=jnp.float32), lower=True)
    panel = jnp.einsum('pq,cmql->cmpl', inverse, panel_rows, precision=HIGHEST)
    return (panel, lower.T)
```

```python
import math

import jax
import jax.numpy as jnp
from jax import lax
from jax.experimental import pallas as pl
from jax.experimental.pallas import tpu as pltpu
from jax.sharding import PartitionSpec as P

NDEG = 1200
ORDERS = 640
NLON = 1280
NC = 8
NT = 16
ND = NC * NT
OWN = 5
UNITS = 40
PIECE = 3

BF = jnp.bfloat16
F32 = jnp.float32
HIGHEST = lax.Precision.HIGHEST
MESH = pl.DeviceIdType.MESH
VM = pl.BlockSpec(memory_space=pltpu.VMEM)
SM = pl.BlockSpec(memory_space=pltpu.SMEM)


def mm(a, b):
    return lax.dot_general(a, b, (((1,), (0,)), ((), ())), preferred_element_type=F32)


def mm_nt(a, b):
    return lax.dot_general(a, b, (((1,), (1,)), ((), ())), preferred_element_type=F32)


def mm_tn(a, b):
    return lax.dot_general(a, b, (((0,), (0,)), ((), ())), preferred_element_type=F32)


def split(x):
    hi = x.astype(BF)
    return hi, (x - hi.astype(F32)).astype(BF)


def normal_kernel(index_ref, count_ref, base_ref, coef_ref, weight_ref, out_ref, prod_ref, diag_ref):
    slots, obs = base_ref.shape
    live = lax.broadcasted_iota(jnp.int32, (slots, obs), 0) < count_ref[0]
    weight = jnp.where(live, weight_ref[...], 0.0)
    row = 0
    for d in range(4):
        for i in range(4 - d):
            left = coef_ref[:, i, :].astype(F32)
            right = coef_ref[:, i + d, :].astype(F32)
            prod_ref[:, row, :] = left * right * weight
            row += 1
    points = lax.broadcasted_iota(jnp.int32, (128, obs), 0)

    def slot(s, carry):
        hot = jnp.where(points == base_ref[pl.ds(s, 1), :], 1.0, 0.0).astype(BF)
        full = prod_ref[s]
        hi, mid = split(full)
        low = (full - hi.astype(F32) - mid.astype(F32)).astype(BF)
        hist = mm_nt(hi, hot) + mm_nt(mid, hot) + mm_nt(low, hot)
        row = 0
        for d in range(4):
            total = hist[row : row + 1, :]
            row += 1
            for i in range(1, 4 - d):
                total = total + pltpu.roll(hist[row : row + 1, :], i, axis=1)
                row += 1
            diag_ref[s, d : d + 1, :] = total
        return carry

    prod_ref[:, 10:16, :] = jnp.zeros((slots, 6, obs), F32)
    lax.fori_loop(0, slots, slot, 0)
    rows = lax.broadcasted_iota(jnp.int32, (80, slots), 0)
    tile = (rows % 8) * 10 + rows // 8
    pick = jnp.where(tile == index_ref[...], 1.0, 0.0).astype(F32)
    tables = [
        lax.dot_general(
            pick, diag_ref[:, d, :], (((1,), (0,)), ((), ())), precision=HIGHEST, preferred_element_type=F32
        )
        for d in range(4)
    ]
    for u in range(NT * PIECE):
        if u < UNITS:
            b, d = u // 4, u % 4
            block = tables[d][b * 8 : (b + 1) * 8, :]
        else:
            block = jnp.zeros((8, 128), F32)
        out_ref[u // PIECE, u % PIECE] = block


def normal_tables(index_row, count, base, coef, weight):
    slots, obs = base.shape
    return pl.pallas_call(
        normal_kernel,
        name="normal_tables",
        out_shape=jax.ShapeDtypeStruct((NT, PIECE, 8, 128), F32),
        in_specs=[VM, SM, VM, VM, VM],
        out_specs=VM,
        scratch_shapes=[pltpu.VMEM((slots, 16, obs), F32), pltpu.VMEM((slots, 4, 128), F32)],
    )(index_row, count, base, coef, weight)


def exchange_kernel(
    lat_ref, norm_ref, lat_out, norm_out, part, lat_send, lat_recv, rs_send, rs_recv, ag_send, ag_recv
):
    c = lax.axis_index("coef")
    t = lax.axis_index("track")
    barrier = pltpu.get_barrier_semaphore()
    for i in range(1, NC):
        pl.semaphore_signal(barrier, 1, device_id=((c + i) % NC, t), device_id_type=MESH)
    for i in range(1, NT):
        pl.semaphore_signal(barrier, 1, device_id=(c, (t + i) % NT), device_id_type=MESH)
    pl.semaphore_wait(barrier, NC + NT - 2)

    def lat_copy(i):
        peer = (c + i) % NC
        return pltpu.make_async_remote_copy(
            lat_ref.at[peer], lat_out.at[c], lat_send, lat_recv, device_id=(peer, t), device_id_type=MESH
        )

    def rs_copy(i):
        peer = (t + i) % NT
        return pltpu.make_async_remote_copy(
            norm_ref.at[peer], part.at[t], rs_send, rs_recv, device_id=(c, peer), device_id_type=MESH
        )

    def ag_copy(i):
        peer = (t + i) % NT
        return pltpu.make_async_remote_copy(
            norm_out.at[t], norm_out.at[t], ag_send, ag_recv, device_id=(c, peer), device_id_type=MESH
        )

    for i in range(1, NT):
        rs_copy(i).start()
    for i in range(1, NC):
        lat_copy(i).start()
    lat_out[c] = lat_ref[c]
    part[t] = norm_ref[t]
    pltpu.make_async_copy(part.at[pl.ds(0, NT - 1)], part.at[pl.ds(0, NT - 1)], rs_recv).wait()
    total = part[0]
    for s in range(1, NT):
        total = total + part[s]
    norm_out[t] = total
    for i in range(1, NT):
        ag_copy(i).start()
    pltpu.make_async_copy(lat_out.at[pl.ds(0, NC - 1)], lat_out.at[pl.ds(0, NC - 1)], lat_recv).wait()
    pltpu.make_async_copy(norm_out.at[pl.ds(0, NT - 1)], norm_out.at[pl.ds(0, NT - 1)], ag_recv).wait()
    pltpu.make_async_copy(part.at[pl.ds(0, NT - 1)], part.at[pl.ds(0, NT - 1)], rs_send).wait()
    pltpu.make_async_copy(lat_ref.at[pl.ds(0, NC - 1)], lat_ref.at[pl.ds(0, NC - 1)], lat_send).wait()
    pltpu.make_async_copy(norm_out.at[pl.ds(0, NT - 1)], norm_out.at[pl.ds(0, NT - 1)], ag_send).wait()


def exchange(lat, norm):
    return pl.pallas_call(
        exchange_kernel,
        name="exchange",
        out_shape=(jax.ShapeDtypeStruct(lat.shape, lat.dtype), jax.ShapeDtypeStruct(norm.shape, norm.dtype)),
        in_specs=[VM, VM],
        out_specs=(VM, VM),
        scratch_shapes=[pltpu.VMEM(norm.shape, F32)] + [pltpu.SemaphoreType.DMA] * 6,
        compiler_params=pltpu.CompilerParams(collective_id=0, has_side_effects=True),
    )(lat, norm)


def grid_kernel(lat_ref, norm_ref, trig_ref, out_ref, hi_ref, lo_ref, adj_ref, spec_ref, turn_ref):
    def make(j, carry):
        cos_q, sin_q, cos_b, sin_b = (trig_ref[k, pl.ds(j * 128, 128), :] for k in range(4))
        for b in range(10):
            ca, sa = cos_b[:, b : b + 1], sin_b[:, b : b + 1]
            cols = slice(b * 128, (b + 1) * 128)
            hi, lo = split(ca * cos_q - sa * sin_q)
            hi_ref[j, :, cols] = hi
            lo_ref[j, :, cols] = lo
            hi, lo = split(sa * cos_q + ca * sin_q)
            hi_ref[OWN + j, :, cols] = hi
            lo_ref[OWN + j, :, cols] = lo
        return carry

    lax.fori_loop(0, OWN, make, 0)
    grid = jnp.zeros((64, NLON), F32)
    for s in range(NC):
        rows = slice(s * NT, (s + 1) * NT)
        grid = grid + mm(lat_ref[s], hi_ref[:, rows, :].reshape(160, NLON))
        grid = grid + mm(lat_ref[s], lo_ref[:, rows, :].reshape(160, NLON))
    for b in range(10):
        x = grid[:, b * 128 : (b + 1) * 128]

        def diagonal(d):
            unit = b * 4 + d
            block = norm_ref[unit // PIECE, unit % PIECE]
            return jnp.broadcast_to(block[None], (8, 8, 128)).reshape(64, 128)

        adj = diagonal(0) * x
        for d in range(1, 4):
            m = diagonal(d)
            adj = adj + m * pltpu.roll(x, 128 - d, axis=1) + pltpu.roll(m * x, d, axis=1)
        hi, lo = split(adj)
        adj_ref[:64, b * 128 : (b + 1) * 128] = hi
        adj_ref[64:, b * 128 : (b + 1) * 128] = lo
    for i in range(10):
        both = mm_nt(adj_ref[...], hi_ref[i])
        spec_ref[i] = both[:64] + both[64:] + mm_nt(adj_ref[:64, :], lo_ref[i])
    spec_ref[10:] = jnp.zeros((6, 64, 128), F32)
    for p in range(8):
        block = spec_ref[:, p * 8 : (p + 1) * 8, :].reshape(128, 128)
        turn_ref[pl.ds(p, 128, stride=8), :] = block.T
    out_ref[...] = turn_ref[...].reshape(128, 8, 128).astype(BF)


def grid_stage(lat, norm, trig):
    return pl.pallas_call(
        grid_kernel,
        name="grid_stage",
        out_shape=jax.ShapeDtypeStruct((ND, 8, 128), BF),
        in_specs=[VM, VM, VM],
        out_specs=VM,
        scratch_shapes=[
            pltpu.VMEM((10, 128, NLON), BF),
            pltpu.VMEM((10, 128, NLON), BF),
            pltpu.VMEM((128, NLON), BF),
            pltpu.VMEM((16, 64, 128), F32),
            pltpu.VMEM((1024, 128), F32),
        ],
        compiler_params=pltpu.CompilerParams(vmem_limit_bytes=48 * 1024 * 1024),
    )(lat, norm, trig)


def gram_kernel(
    spec_ref, leg_ref, rows_out, gram_out, recv, perm, normal, g_part, g_coef, g_track,
    a_send, a_recv, b_send, b_recv, c_send, c_recv, d_send, d_recv,
):
    c = lax.axis_index("coef")
    t = lax.axis_index("track")
    me = c * NT + t
    barrier = pltpu.get_barrier_semaphore()

    def greet(i, carry):
        peer = (me + i) % ND
        pl.semaphore_signal(barrier, 1, device_id=(peer // NT, peer % NT), device_id_type=MESH)
        return carry

    lax.fori_loop(1, ND, greet, 0)
    pl.semaphore_wait(barrier, ND - 1)

    def send(i, carry):
        peer = (me + i) % ND
        pltpu.make_async_remote_copy(
            spec_ref.at[peer], recv.at[me], a_send, a_recv,
            device_id=(peer // NT, peer % NT), device_id_type=MESH,
        ).start()
        return carry

    lax.fori_loop(1, ND, send, 0)
    recv[me] = spec_ref[me]
    same = (lax.broadcasted_iota(jnp.int32, (128, 128), 0) < 64) == (
        lax.broadcasted_iota(jnp.int32, (128, 128), 1) < 64
    )
    for j in range(OWN):
        one = leg_ref[j]
        two = jnp.concatenate([one, one], axis=0)
        hi, lo = split(jnp.where(same, mm_nt(two, two), 0.0))
        normal[0, j] = hi
        normal[1, j] = lo
    row = lax.broadcasted_iota(jnp.int32, (1024, 640), 0)
    col = lax.broadcasted_iota(jnp.int32, (1024, 640), 1)
    src_band, src_i, src_a = row // 128, (row % 128) // 8, row % 8
    dst_j, dst_half, dst_band, dst_a = col // 128, (col % 128) // 64, (col % 64) // 8, col % 8
    hit = (src_band == dst_band) & (src_a == dst_a) & (src_i == dst_half * OWN + dst_j)
    perm[...] = jnp.where(hit, 1.0, 0.0).astype(BF)
    pltpu.make_async_copy(recv.at[pl.ds(0, ND - 1)], recv.at[pl.ds(0, ND - 1)], a_recv).wait()
    gathered = jnp.zeros((128, 640), F32)
    for s in range(NC):
        block = recv[s * NT : (s + 1) * NT].astype(F32).reshape(128, 128).astype(BF)
        gathered = gathered + mm(block, perm[s * 128 : (s + 1) * 128, :])
    gram = jnp.zeros((128, 128), F32)
    for j in range(OWN):
        rows = gathered[:, j * 128 : (j + 1) * 128].astype(BF)
        rows_out[j] = rows
        hi, lo = split(mm(rows, normal[0, j]) + mm(rows, normal[1, j]))
        gram = gram + mm_nt(hi, rows) + mm_nt(lo, rows)
    g_part[...] = gram.reshape(NC, 16, 128)

    def to_coef(ref, dst, sems, peer):
        return pltpu.make_async_remote_copy(ref, dst, *sems, device_id=(peer, t), device_id_type=MESH)

    for i in range(1, NC):
        peer = (c + i) % NC
        to_coef(g_part.at[peer], g_coef.at[c], (b_send, b_recv), peer).start()
    g_coef[c] = g_part[c]
    pltpu.make_async_copy(g_coef.at[pl.ds(0, NC - 1)], g_coef.at[pl.ds(0, NC - 1)], b_recv).wait()
    total = g_coef[0]
    for s in range(1, NC):
        total = total + g_coef[s]
    g_track[t] = total
    for i in range(1, NT):
        peer = (t + i) % NT
        pltpu.make_async_remote_copy(
            g_track.at[t], g_track.at[t], c_send, c_recv, device_id=(c, peer), device_id_type=MESH
        ).start()
    pltpu.make_async_copy(g_track.at[pl.ds(0, NT - 1)], g_track.at[pl.ds(0, NT - 1)], c_recv).wait()
    total = g_track[0]
    for s in range(1, NT):
        total = total + g_track[s]
    gram_out[c] = total * (1.0 / (2 * ORDERS * NDEG))
    for i in range(1, NC):
        peer = (c + i) % NC
        to_coef(gram_out.at[c], gram_out.at[c], (d_send, d_recv), peer).start()
    pltpu.make_async_copy(gram_out.at[pl.ds(0, NC - 1)], gram_out.at[pl.ds(0, NC - 1)], d_recv).wait()
    pltpu.make_async_copy(recv.at[pl.ds(0, ND - 1)], recv.at[pl.ds(0, ND - 1)], a_send).wait()
    pltpu.make_async_copy(g_part.at[pl.ds(0, NC - 1)], g_part.at[pl.ds(0, NC - 1)], b_send).wait()
    pltpu.make_async_copy(g_track.at[pl.ds(0, NT - 1)], g_track.at[pl.ds(0, NT - 1)], c_send).wait()
    pltpu.make_async_copy(gram_out.at[pl.ds(0, NC - 1)], gram_out.at[pl.ds(0, NC - 1)], d_send).wait()


def gram_stage(spec, own_table):
    return pl.pallas_call(
        gram_kernel,
        name="gram_stage",
        out_shape=(jax.ShapeDtypeStruct((OWN, 128, 128), BF), jax.ShapeDtypeStruct((NC, 16, 128), F32)),
        in_specs=[VM, VM],
        out_specs=(VM, VM),
        scratch_shapes=[
            pltpu.VMEM((ND, 8, 128), BF),
            pltpu.VMEM((1024, 640), BF),
            pltpu.VMEM((2, OWN, 128, 128), BF),
            pltpu.VMEM((NC, 16, 128), F32),
            pltpu.VMEM((NC, 16, 128), F32),
            pltpu.VMEM((NT, 16, 128), F32),
        ]
        + [pltpu.SemaphoreType.DMA] * 8,
        compiler_params=pltpu.CompilerParams(collective_id=1, has_side_effects=True),
    )(spec, own_table)


def panel_kernel(inv_ref, rows_ref, leg_ref, out_ref):
    hi, lo = split(inv_ref[...])
    z = mm(hi, rows_ref[0]) + mm(lo, rows_ref[0])
    z_hi, z_lo = split(z)
    left = lax.broadcasted_iota(jnp.int32, (128, 128), 1) < 64
    hi_f, lo_f = z_hi.astype(F32), z_lo.astype(F32)
    cosine = jnp.where(left, hi_f, pltpu.roll(lo_f, 64, axis=1)).astype(BF)
    sine = jnp.where(left, pltpu.roll(hi_f, 64, axis=1), lo_f).astype(BF)
    one = leg_ref[0]
    two = jnp.concatenate([one, one], axis=0)
    contract = (((0,), (1,)), ((), ()))
    out_ref[0, 0] = lax.dot_general(two, cosine, contract, preferred_element_type=F32)
    out_ref[1, 0] = lax.dot_general(two, sine, contract, preferred_element_type=F32)


def panel_stage(inverse, rows, own_table):
    return pl.pallas_call(
        panel_kernel,
        name="panel_stage",
        grid=(OWN,),
        out_shape=jax.ShapeDtypeStruct((2, OWN, NDEG, 128), F32),
        in_specs=[
            pl.BlockSpec((128, 128), lambda j: (0, 0)),
            pl.BlockSpec((1, 128, 128), lambda j: (j, 0, 0)),
            pl.BlockSpec((1, 64, NDEG), lambda j: (j, 0, 0)),
        ],
        out_specs=pl.BlockSpec((2, 1, NDEG, 128), lambda j: (0, j, 0, 0)),
    )(inverse, rows, own_table)


def trig_factors(order_map):
    order = order_map.reshape(NC, NT, OWN).transpose(2, 0, 1).reshape(ORDERS, 1)
    lane = jnp.arange(128, dtype=jnp.int32)[None, :]
    unit = F32(2.0 * math.pi / NLON)
    point = (order * lane % NLON).astype(F32) * unit
    offset = (order * (lane * 128) % NLON).astype(F32) * unit
    scale = F32(1.0 / math.sqrt(ORDERS))
    return jnp.stack([jnp.cos(point), jnp.sin(point), jnp.cos(offset) * scale, jnp.sin(offset) * scale])


def on_device(
    probes, legendre, order_map, tile_index, tile_count, base_offset, stencil_weight, obs_weight
):
    t = lax.axis_index("track")
    lat = jnp.einsum("cmpl,mal->mcpa", probes, legendre, preferred_element_type=F32)
    lat = lat.reshape(NT, OWN, 2, 8, NC, 8).transpose(4, 3, 5, 2, 1, 0)
    lat = lat.astype(BF).reshape(NC, 64, 160)
    index_row = lax.dynamic_slice_in_dim(tile_index[0], t, 1, 0)
    count = lax.dynamic_slice_in_dim(tile_count[0], t, 1, 0)
    norm = normal_tables(index_row, count, base_offset[0, 0], stencil_weight[0, 0], obs_weight[0, 0])
    lat, norm = exchange(lat, norm)
    spec = grid_stage(lat, norm, trig_factors(order_map))
    own_table = lax.dynamic_slice_in_dim(legendre, t * OWN, OWN, 0)
    rows, gram = gram_stage(spec, own_table)
    lower = jnp.linalg.cholesky(gram.reshape(128, 128))
    inverse = jax.scipy.linalg.solve_triangular(lower, jnp.eye(128, dtype=F32), lower=True)
    panel = panel_stage(inverse, rows, own_table)
    return (jnp.swapaxes(panel, 2, 3), lower.T)


def solution(mesh):
    return jax.shard_map(
        on_device,
        mesh=mesh,
        in_specs=(
            P(None, "coef", "track", None),
            P("coef", None, None),
            P(),
            P("coef", None, None),
            P("coef", None),
            P("coef", "track", None, None),
            P("coef", "track", None, None, None),
            P("coef", "track", None, None),
        ),
        out_specs=(P(None, ("coef", "track"), None, None), P()),
        check_vma=False,
    )
```

```python
import math

import jax
import jax.numpy as jnp
from jax import lax
from jax.experimental import pallas as pl
from jax.experimental.pallas import tpu as pltpu
from jax.sharding import PartitionSpec as P

NDEG = 1200
ORDERS = 640
NLON = 1280
NC = 8
NT = 16
ND = NC * NT
OWN = 5
UNITS = 40
PIECE = 3

BF = jnp.bfloat16
F32 = jnp.float32
HIGHEST = lax.Precision.HIGHEST
MESH = pl.DeviceIdType.MESH
VM = pl.BlockSpec(memory_space=pltpu.VMEM)
SM = pl.BlockSpec(memory_space=pltpu.SMEM)


def mm(a, b):
    return lax.dot_general(a, b, (((1,), (0,)), ((), ())), preferred_element_type=F32)


def mm_nt(a, b):
    return lax.dot_general(a, b, (((1,), (1,)), ((), ())), preferred_element_type=F32)


def mm_tn(a, b):
    return lax.dot_general(a, b, (((0,), (0,)), ((), ())), preferred_element_type=F32)


def split(x):
    hi = x.astype(BF)
    return hi, (x - hi.astype(F32)).astype(BF)


def normal_kernel(index_ref, count_ref, base_ref, coef_ref, weight_ref, out_ref, prod_ref, diag_ref):
    slots, obs = base_ref.shape
    live = lax.broadcasted_iota(jnp.int32, (slots, obs), 0) < count_ref[0]
    weight = jnp.where(live, weight_ref[...], 0.0)
    row = 0
    for d in range(4):
        for i in range(4 - d):
            left = coef_ref[:, i, :].astype(F32)
            right = coef_ref[:, i + d, :].astype(F32)
            prod_ref[:, row, :] = left * right * weight
            row += 1
    points = lax.broadcasted_iota(jnp.int32, (128, obs), 0)

    def slot(s, carry):
        hot = jnp.where(points == base_ref[pl.ds(s, 1), :], 1.0, 0.0).astype(BF)
        full = prod_ref[s]
        hi, mid = split(full)
        low = (full - hi.astype(F32) - mid.astype(F32)).astype(BF)
        hist = mm_nt(hi, hot) + mm_nt(mid, hot) + mm_nt(low, hot)
        row = 0
        for d in range(4):
            total = hist[row : row + 1, :]
            row += 1
            for i in range(1, 4 - d):
                total = total + pltpu.roll(hist[row : row + 1, :], i, axis=1)
                row += 1
            diag_ref[s, d : d + 1, :] = total
        return carry

    prod_ref[:, 10:16, :] = jnp.zeros((slots, 6, obs), F32)
    lax.fori_loop(0, slots, slot, 0)
    rows = lax.broadcasted_iota(jnp.int32, (80, slots), 0)
    tile = (rows % 8) * 10 + rows // 8
    pick = jnp.where(tile == index_ref[...], 1.0, 0.0).astype(F32)
    tables = [
        lax.dot_general(
            pick, diag_ref[:, d, :], (((1,), (0,)), ((), ())), precision=HIGHEST, preferred_element_type=F32
        )
        for d in range(4)
    ]
    for u in range(NT * PIECE):
        if u < UNITS:
            b, d = u // 4, u % 4
            block = tables[d][b * 8 : (b + 1) * 8, :]
        else:
            block = jnp.zeros((8, 128), F32)
        out_ref[u // PIECE, u % PIECE] = block


def normal_tables(index_row, count, base, coef, weight):
    slots, obs = base.shape
    return pl.pallas_call(
        normal_kernel,
        name="normal_tables",
        out_shape=jax.ShapeDtypeStruct((NT, PIECE, 8, 128), F32),
        in_specs=[VM, SM, VM, VM, VM],
        out_specs=VM,
        scratch_shapes=[pltpu.VMEM((slots, 16, obs), F32), pltpu.VMEM((slots, 4, 128), F32)],
    )(index_row, count, base, coef, weight)


def exchange_kernel(
    lat_ref, norm_ref, lat_out, norm_out, part, lat_send, lat_recv, rs_send, rs_recv, ag_send, ag_recv
):
    c = lax.axis_index("coef")
    t = lax.axis_index("track")
    barrier = pltpu.get_barrier_semaphore()
    for i in range(1, NC):
        pl.semaphore_signal(barrier, 1, device_id=((c + i) % NC, t), device_id_type=MESH)
    for i in range(1, NT):
        pl.semaphore_signal(barrier, 1, device_id=(c, (t + i) % NT), device_id_type=MESH)
    pl.semaphore_wait(barrier, NC + NT - 2)

    def lat_copy(i):
        peer = (c + i) % NC
        return pltpu.make_async_remote_copy(
            lat_ref.at[peer], lat_out.at[c], lat_send, lat_recv, device_id=(peer, t), device_id_type=MESH
        )

    def rs_copy(i):
        peer = (t + i) % NT
        return pltpu.make_async_remote_copy(
            norm_ref.at[peer], part.at[t], rs_send, rs_recv, device_id=(c, peer), device_id_type=MESH
        )

    def ag_copy(i):
        peer = (t + i) % NT
        return pltpu.make_async_remote_copy(
            norm_out.at[t], norm_out.at[t], ag_send, ag_recv, device_id=(c, peer), device_id_type=MESH
        )

    for i in range(1, NT):
        rs_copy(i).start()
    for i in range(1, NC):
        lat_copy(i).start()
    lat_out[c] = lat_ref[c]
    part[t] = norm_ref[t]
    pltpu.make_async_copy(part.at[pl.ds(0, NT - 1)], part.at[pl.ds(0, NT - 1)], rs_recv).wait()
    total = part[0]
    for s in range(1, NT):
        total = total + part[s]
    norm_out[t] = total
    for i in range(1, NT):
        ag_copy(i).start()
    pltpu.make_async_copy(lat_out.at[pl.ds(0, NC - 1)], lat_out.at[pl.ds(0, NC - 1)], lat_recv).wait()
    pltpu.make_async_copy(norm_out.at[pl.ds(0, NT - 1)], norm_out.at[pl.ds(0, NT - 1)], ag_recv).wait()
    pltpu.make_async_copy(part.at[pl.ds(0, NT - 1)], part.at[pl.ds(0, NT - 1)], rs_send).wait()
    pltpu.make_async_copy(lat_ref.at[pl.ds(0, NC - 1)], lat_ref.at[pl.ds(0, NC - 1)], lat_send).wait()
    pltpu.make_async_copy(norm_out.at[pl.ds(0, NT - 1)], norm_out.at[pl.ds(0, NT - 1)], ag_send).wait()


def exchange(lat, norm):
    return pl.pallas_call(
        exchange_kernel,
        name="exchange",
        out_shape=(jax.ShapeDtypeStruct(lat.shape, lat.dtype), jax.ShapeDtypeStruct(norm.shape, norm.dtype)),
        in_specs=[VM, VM],
        out_specs=(VM, VM),
        scratch_shapes=[pltpu.VMEM(norm.shape, F32)] + [pltpu.SemaphoreType.DMA] * 6,
        compiler_params=pltpu.CompilerParams(collective_id=0, has_side_effects=True),
    )(lat, norm)


def grid_kernel(lat_ref, norm_ref, trig_ref, out_ref, hi_ref, lo_ref, adj_ref, spec_ref, turn_ref):
    def make(j, carry):
        cos_q, sin_q, cos_b, sin_b = (trig_ref[k, pl.ds(j * 128, 128), :] for k in range(4))
        for b in range(10):
            ca, sa = cos_b[:, b : b + 1], sin_b[:, b : b + 1]
            cols = slice(b * 128, (b + 1) * 128)
            hi, lo = split(ca * cos_q - sa * sin_q)
            hi_ref[j, :, cols] = hi
            lo_ref[j, :, cols] = lo
            hi, lo = split(sa * cos_q + ca * sin_q)
            hi_ref[OWN + j, :, cols] = hi
            lo_ref[OWN + j, :, cols] = lo
        return carry

    lax.fori_loop(0, OWN, make, 0)
    grid = jnp.zeros((64, NLON), F32)
    for s in range(NC):
        rows = slice(s * NT, (s + 1) * NT)
        grid = grid + mm(lat_ref[s], hi_ref[:, rows, :].reshape(160, NLON))
        grid = grid + mm(lat_ref[s], lo_ref[:, rows, :].reshape(160, NLON))
    for b in range(10):
        x = grid[:, b * 128 : (b + 1) * 128]

        def diagonal(d):
            unit = b * 4 + d
            block = norm_ref[unit // PIECE, unit % PIECE]
            return jnp.broadcast_to(block[None], (8, 8, 128)).reshape(64, 128)

        adj = diagonal(0) * x
        for d in range(1, 4):
            m = diagonal(d)
            adj = adj + m * pltpu.roll(x, 128 - d, axis=1) + pltpu.roll(m * x, d, axis=1)
        hi, lo = split(adj)
        adj_ref[:64, b * 128 : (b + 1) * 128] = hi
        adj_ref[64:, b * 128 : (b + 1) * 128] = lo
    for i in range(10):
        both = mm_nt(adj_ref[...], hi_ref[i])
        spec_ref[i] = both[:64] + both[64:] + mm_nt(adj_ref[:64, :], lo_ref[i])
    spec_ref[10:] = jnp.zeros((6, 64, 128), F32)
    for p in range(8):
        block = spec_ref[:, p * 8 : (p + 1) * 8, :].reshape(128, 128)
        turn_ref[pl.ds(p, 128, stride=8), :] = block.T
    out_ref[...] = turn_ref[...].reshape(128, 8, 128).astype(BF)


def grid_stage(lat, norm, trig):
    return pl.pallas_call(
        grid_kernel,
        name="grid_stage",
        out_shape=jax.ShapeDtypeStruct((ND, 8, 128), BF),
        in_specs=[VM, VM, VM],
        out_specs=VM,
        scratch_shapes=[
            pltpu.VMEM((10, 128, NLON), BF),
            pltpu.VMEM((10, 128, NLON), BF),
            pltpu.VMEM((128, NLON), BF),
            pltpu.VMEM((16, 64, 128), F32),
            pltpu.VMEM((1024, 128), F32),
        ],
        compiler_params=pltpu.CompilerParams(vmem_limit_bytes=48 * 1024 * 1024),
    )(lat, norm, trig)


def gram_kernel(
    spec_ref, leg_ref, rows_out, gram_out, recv, perm, normal, g_part, g_coef, g_track,
    a_send, a_recv, b_send, b_recv, c_send, c_recv, d_send, d_recv,
):
    c = lax.axis_index("coef")
    t = lax.axis_index("track")
    me = c * NT + t
    barrier = pltpu.get_barrier_semaphore()

    def greet(i, carry):
        peer = (me + i) % ND
        pl.semaphore_signal(barrier, 1, device_id=(peer // NT, peer % NT), device_id_type=MESH)
        return carry

    lax.fori_loop(1, ND, greet, 0)
    pl.semaphore_wait(barrier, ND - 1)

    def send(i, carry):
        peer = (me + i) % ND
        pltpu.make_async_remote_copy(
            spec_ref.at[peer], recv.at[me], a_send, a_recv,
            device_id=(peer // NT, peer % NT), device_id_type=MESH,
        ).start()
        return carry

    lax.fori_loop(1, ND, send, 0)
    recv[me] = spec_ref[me]
    same = (lax.broadcasted_iota(jnp.int32, (128, 128), 0) < 64) == (
        lax.broadcasted_iota(jnp.int32, (128, 128), 1) < 64
    )
    for j in range(OWN):
        one = leg_ref[j]
        two = jnp.concatenate([one, one], axis=0)
        hi, lo = split(jnp.where(same, mm_nt(two, two), 0.0))
        normal[0, j] = hi
        normal[1, j] = lo
    row = lax.broadcasted_iota(jnp.int32, (1024, 640), 0)
    col = lax.broadcasted_iota(jnp.int32, (1024, 640), 1)
    src_band, src_i, src_a = row // 128, (row % 128) // 8, row % 8
    dst_j, dst_half, dst_band, dst_a = col // 128, (col % 128) // 64, (col % 64) // 8, col % 8
    hit = (src_band == dst_band) & (src_a == dst_a) & (src_i == dst_half * OWN + dst_j)
    perm[...] = jnp.where(hit, 1.0, 0.0).astype(BF)
    pltpu.make_async_copy(recv.at[pl.ds(0, ND - 1)], recv.at[pl.ds(0, ND - 1)], a_recv).wait()
    gathered = jnp.zeros((128, 640), F32)
    for s in range(NC):
        block = recv[s * NT : (s + 1) * NT].astype(F32).reshape(128, 128).astype(BF)
        gathered = gathered + mm(block, perm[s * 128 : (s + 1) * 128, :])
    gram = jnp.zeros((128, 128), F32)
    for j in range(OWN):
        rows = gathered[:, j * 128 : (j + 1) * 128].astype(BF)
        rows_out[j] = rows
        hi, lo = split(mm(rows, normal[0, j]) + mm(rows, normal[1, j]))
        gram = gram + mm_nt(hi, rows) + mm_nt(lo, rows)
    g_part[...] = gram.reshape(NC, 16, 128)

    def to_coef(ref, dst, sems, peer):
        return pltpu.make_async_remote_copy(ref, dst, *sems, device_id=(peer, t), device_id_type=MESH)

    for i in range(1, NC):
        peer = (c + i) % NC
        to_coef(g_part.at[peer], g_coef.at[c], (b_send, b_recv), peer).start()
    g_coef[c] = g_part[c]
    pltpu.make_async_copy(g_coef.at[pl.ds(0, NC - 1)], g_coef.at[pl.ds(0, NC - 1)], b_recv).wait()
    total = g_coef[0]
    for s in range(1, NC):
        total = total + g_coef[s]
    g_track[t] = total
    for i in range(1, NT):
        peer = (t + i) % NT
        pltpu.make_async_remote_copy(
            g_track.at[t], g_track.at[t], c_send, c_recv, device_id=(c, peer), device_id_type=MESH
        ).start()
    pltpu.make_async_copy(g_track.at[pl.ds(0, NT - 1)], g_track.at[pl.ds(0, NT - 1)], c_recv).wait()
    total = g_track[0]
    for s in range(1, NT):
        total = total + g_track[s]
    gram_out[c] = total * (1.0 / (2 * ORDERS * NDEG))
    for i in range(1, NC):
        peer = (c + i) % NC
        to_coef(gram_out.at[c], gram_out.at[c], (d_send, d_recv), peer).start()
    pltpu.make_async_copy(gram_out.at[pl.ds(0, NC - 1)], gram_out.at[pl.ds(0, NC - 1)], d_recv).wait()
    pltpu.make_async_copy(recv.at[pl.ds(0, ND - 1)], recv.at[pl.ds(0, ND - 1)], a_send).wait()
    pltpu.make_async_copy(g_part.at[pl.ds(0, NC - 1)], g_part.at[pl.ds(0, NC - 1)], b_send).wait()
    pltpu.make_async_copy(g_track.at[pl.ds(0, NT - 1)], g_track.at[pl.ds(0, NT - 1)], c_send).wait()
    pltpu.make_async_copy(gram_out.at[pl.ds(0, NC - 1)], gram_out.at[pl.ds(0, NC - 1)], d_send).wait()


def gram_stage(spec, own_table):
    return pl.pallas_call(
        gram_kernel,
        name="gram_stage",
        out_shape=(jax.ShapeDtypeStruct((OWN, 128, 128), BF), jax.ShapeDtypeStruct((NC, 16, 128), F32)),
        in_specs=[VM, VM],
        out_specs=(VM, VM),
        scratch_shapes=[
            pltpu.VMEM((ND, 8, 128), BF),
            pltpu.VMEM((1024, 640), BF),
            pltpu.VMEM((2, OWN, 128, 128), BF),
            pltpu.VMEM((NC, 16, 128), F32),
            pltpu.VMEM((NC, 16, 128), F32),
            pltpu.VMEM((NT, 16, 128), F32),
        ]
        + [pltpu.SemaphoreType.DMA] * 8,
        compiler_params=pltpu.CompilerParams(collective_id=1, has_side_effects=True),
    )(spec, own_table)


def exact(a, b, dims):
    return lax.dot_general(a, b, (dims, ((), ())), precision=HIGHEST, preferred_element_type=F32)


NN = ((1,), (0,))
NT_DIMS = ((1,), (1,))


def factorize(gram, upper_ref, inv_ref):
    n = gram.shape[0]
    row = lax.broadcasted_iota(jnp.int32, (n, n), 0)
    col = lax.broadcasted_iota(jnp.int32, (n, n), 1)
    eye = jnp.where(row == col, 1.0, 0.0)
    half = jnp.where(row > col, 1.0, 0.5 * eye)
    diag = jnp.where(row == col, gram, 0.0)
    r_col = lax.rsqrt(jnp.sum(diag, axis=1, keepdims=True))
    r_row = lax.rsqrt(jnp.sum(diag, axis=0, keepdims=True))
    inverse = (eye - half * (gram * r_col * r_row - eye)) * r_row
    error = eye
    for _ in range(3):
        error = exact(exact(inverse, gram, NN), inverse, NT_DIMS) - eye
        inverse = inverse - exact(half * error, inverse, NN)
    inv_ref[...] = inverse
    upper_ref[...] = jnp.where(row <= col, exact(inverse, gram, NN), 0.0)
    worst = jnp.max(jnp.abs(error))

    @pl.when(jnp.logical_not(worst < 1e-4))
    def _():
        def column(j, state):
            left, upper, inv = state
            at_row, at_col = row == j, col == j
            line = jnp.sum(jnp.where(at_row, left, 0.0), axis=0, keepdims=True)
            down = jnp.sum(jnp.where(at_col, left, 0.0), axis=1, keepdims=True)
            pivot = jnp.sum(jnp.where(at_row & at_col, left, 0.0), keepdims=True)
            scale = 1.0 / jnp.sqrt(pivot)
            line = jnp.where(col[:1] >= j, line * scale, 0.0)
            below = jnp.where(row[:, :1] > j, down * scale, 0.0)
            inv_line = jnp.sum(jnp.where(at_row, inv, 0.0), axis=0, keepdims=True) * scale
            inv = jnp.where(at_row, inv_line, inv - below * inv_line)
            upper = jnp.where(at_row, line, upper)
            return left - below * line, upper, inv

        _, upper, inv = lax.fori_loop(0, n, column, (gram, jnp.zeros_like(gram), eye))
        upper_ref[...] = upper
        inv_ref[...] = inv


def panel_kernel(gram_ref, rows_ref, leg_ref, out_ref, upper_ref, inv_ref):
    @pl.when(pl.program_id(0) == 0)
    def _():
        factorize(gram_ref[...].reshape(128, 128), upper_ref, inv_ref)

    hi, lo = split(inv_ref[...])
    z = mm(hi, rows_ref[0]) + mm(lo, rows_ref[0])
    z_hi, z_lo = split(z)
    left = lax.broadcasted_iota(jnp.int32, (128, 128), 1) < 64
    hi_f, lo_f = z_hi.astype(F32), z_lo.astype(F32)
    cosine = jnp.where(left, hi_f, pltpu.roll(lo_f, 64, axis=1)).astype(BF)
    sine = jnp.where(left, pltpu.roll(hi_f, 64, axis=1), lo_f).astype(BF)
    one = leg_ref[0]
    two = jnp.concatenate([one, one], axis=0)
    contract = (((0,), (1,)), ((), ()))
    out_ref[0, 0] = lax.dot_general(two, cosine, contract, preferred_element_type=F32)
    out_ref[1, 0] = lax.dot_general(two, sine, contract, preferred_element_type=F32)


def panel_stage(gram, rows, own_table):
    return pl.pallas_call(
        panel_kernel,
        name="panel_stage",
        grid=(OWN,),
        out_shape=(
            jax.ShapeDtypeStruct((2, OWN, NDEG, 128), F32),
            jax.ShapeDtypeStruct((128, 128), F32),
        ),
        in_specs=[
            pl.BlockSpec((NC, 16, 128), lambda j: (0, 0, 0)),
            pl.BlockSpec((1, 128, 128), lambda j: (j, 0, 0)),
            pl.BlockSpec((1, 64, NDEG), lambda j: (j, 0, 0)),
        ],
        out_specs=(
            pl.BlockSpec((2, 1, NDEG, 128), lambda j: (0, j, 0, 0)),
            pl.BlockSpec((128, 128), lambda j: (0, 0)),
        ),
        scratch_shapes=[pltpu.VMEM((128, 128), F32)],
    )(gram, rows, own_table)


def trig_factors(order_map):
    order = order_map.reshape(NC, NT, OWN).transpose(2, 0, 1).reshape(ORDERS, 1)
    lane = jnp.arange(128, dtype=jnp.int32)[None, :]
    unit = F32(2.0 * math.pi / NLON)
    point = (order * lane % NLON).astype(F32) * unit
    offset = (order * (lane * 128) % NLON).astype(F32) * unit
    scale = F32(1.0 / math.sqrt(ORDERS))
    return jnp.stack([jnp.cos(point), jnp.sin(point), jnp.cos(offset) * scale, jnp.sin(offset) * scale])


def on_device(
    probes, legendre, order_map, tile_index, tile_count, base_offset, stencil_weight, obs_weight
):
    t = lax.axis_index("track")
    lat = jnp.einsum("cmpl,mal->mcpa", probes, legendre, preferred_element_type=F32)
    lat = lat.reshape(NT, OWN, 2, 8, NC, 8).transpose(4, 3, 5, 2, 1, 0)
    lat = lat.astype(BF).reshape(NC, 64, 160)
    index_row = lax.dynamic_slice_in_dim(tile_index[0], t, 1, 0)
    count = lax.dynamic_slice_in_dim(tile_count[0], t, 1, 0)
    norm = normal_tables(index_row, count, base_offset[0, 0], stencil_weight[0, 0], obs_weight[0, 0])
    lat, norm = exchange(lat, norm)
    spec = grid_stage(lat, norm, trig_factors(order_map))
    own_table = lax.dynamic_slice_in_dim(legendre, t * OWN, OWN, 0)
    rows, gram = gram_stage(spec, own_table)
    panel, upper = panel_stage(gram, rows, own_table)
    return (jnp.swapaxes(panel, 2, 3), upper)


def solution(mesh):
    return jax.shard_map(
        on_device,
        mesh=mesh,
        in_specs=(
            P(None, "coef", "track", None),
            P("coef", None, None),
            P(),
            P("coef", None, None),
            P("coef", None),
            P("coef", "track", None, None),
            P("coef", "track", None, None, None),
            P("coef", "track", None, None),
        ),
        out_specs=(P(None, ("coef", "track"), None, None), P()),
        check_vma=False,
    )
```

```python
import math

import jax
import jax.numpy as jnp
from jax import lax
from jax.experimental import pallas as pl
from jax.experimental.pallas import tpu as pltpu
from jax.sharding import PartitionSpec as P

NDEG = 1200
ORDERS = 640
NLON = 1280
NC = 8
NT = 16
ND = NC * NT
OWN = 5
UNITS = 40
PIECE = 3
STEP = 8
CHUNKS = 10

BF = jnp.bfloat16
F32 = jnp.float32
HIGHEST = lax.Precision.HIGHEST
MESH = pl.DeviceIdType.MESH
VM = pl.BlockSpec(memory_space=pltpu.VMEM)


def mm(a, b):
    return lax.dot_general(a, b, (((1,), (0,)), ((), ())), preferred_element_type=F32)


def mm_nt(a, b):
    return lax.dot_general(a, b, (((1,), (1,)), ((), ())), preferred_element_type=F32)


def split(x):
    hi = x.astype(BF)
    return hi, (x - hi.astype(F32)).astype(BF)


def front_kernel(
    probes_ref, leg_ref, order_ref, index_ref, count_ref, base_ref, coef_ref, weight_ref,
    rows_out, gram_out,
    leg, prob, base, coef, weight, live, hist, norm, part, table, lat_rows, lat_pack, lat_send, lat_recv,
    cos_q, sin_q, cos_b, sin_b, tab_hi, tab_lo, adj_ref, spec_ref, turn_ref, spec, recv, perm, normal,
    g_part, g_coef, g_track, in_sem, leg_sem, prob_sem, comm,
):
    c = lax.axis_index("coef")
    t = lax.axis_index("track")
    me = c * NT + t

    def send(src, dst, k, pc, pt):
        pltpu.make_async_remote_copy(
            src, dst, comm.at[2 * k], comm.at[2 * k + 1], device_id=(pc, pt), device_id_type=MESH
        ).start()

    def arrived(ref, n, k):
        pltpu.make_async_copy(ref.at[pl.ds(0, n)], ref.at[pl.ds(0, n)], comm.at[2 * k + 1]).wait()

    def sent(ref, n, k):
        pltpu.make_async_copy(ref.at[pl.ds(0, n)], ref.at[pl.ds(0, n)], comm.at[2 * k]).wait()

    small = [
        pltpu.make_async_copy(src, dst, in_sem.at[k])
        for k, (src, dst) in enumerate(((base_ref, base), (coef_ref, coef), (weight_ref, weight)))
    ]
    for copy in small:
        copy.start()

    def fetch(k):
        orders = pl.ds(k * STEP, STEP)
        return (
            pltpu.make_async_copy(leg_ref.at[orders], leg.at[orders], leg_sem.at[k]),
            pltpu.make_async_copy(probes_ref.at[:, orders], prob.at[:, orders], prob_sem.at[k]),
        )

    for k in range(CHUNKS):
        for copy in fetch(k):
            copy.start()
    barrier = pltpu.get_barrier_semaphore()

    def greet(i, carry):
        peer = (me + i) % ND
        pl.semaphore_signal(barrier, 1, device_id=(peer // NT, peer % NT), device_id_type=MESH)
        return carry

    lax.fori_loop(1, ND, greet, 0)

    for copy in small:
        copy.wait()
    slots, obs = base.shape
    lane16 = lax.broadcasted_iota(jnp.int32, (1, NT), 1)
    count = jnp.sum(jnp.where(lane16 == t, count_ref[...].astype(F32), 0.0), axis=1, keepdims=True)
    slot_id = lax.broadcasted_iota(jnp.int32, (slots, obs), 0).astype(F32)
    live[...] = jnp.where(slot_id < count, weight[...], 0.0)
    points = lax.broadcasted_iota(jnp.int32, (128, obs), 0)

    def slot(group, carry):
        for u in range(4):
            s = group * 4 + u
            hot = jnp.where(points == base[pl.ds(s, 1), :], 1.0, 0.0).astype(BF)
            four = coef[s].astype(F32)
            eight = jnp.concatenate([four, jnp.zeros_like(four)], axis=0)
            scaled = eight * live[pl.ds(s, 1), :]
            full = jnp.concatenate(
                [scaled * eight] + [scaled * pltpu.roll(eight, 8 - d, axis=0) for d in range(1, 4)], axis=0
            )
            hi, mid = split(full)
            low = (full - hi.astype(F32) - mid.astype(F32)).astype(BF)
            sums = mm_nt(jnp.concatenate([hi, mid, low], axis=0), hot)
            hist[s] = sums[:32] + sums[32:64] + sums[64:]
        return carry

    lax.fori_loop(0, slots // 4, slot, 0)
    diagonals = []
    for d in range(4):
        total = hist[:, 8 * d, :]
        for i in range(1, 4 - d):
            total = total + pltpu.roll(hist[:, 8 * d + i, :], i, axis=1)
        diagonals.append(total)
    rows = lax.broadcasted_iota(jnp.int32, (80, slots), 0)
    tile = (rows & 7) * 10 + lax.shift_right_logical(rows, 3)
    pick = jnp.where(tile == index_ref[pl.ds(t, 1), :], 1.0, 0.0)
    summed = exact(pick, jnp.concatenate(diagonals, axis=1), NN)
    for u in range(NT * PIECE):
        if u < UNITS:
            b, d = u // 4, u % 4
            block = summed[b * 8 : (b + 1) * 8, d * 128 : (d + 1) * 128]
        else:
            block = jnp.zeros((8, 128), F32)
        norm[u // PIECE, u % PIECE] = block
    pl.semaphore_wait(barrier, ND - 1)
    for i in range(1, NT):
        peer = (t + i) % NT
        send(norm.at[peer], part.at[t], 0, c, peer)
    part[t] = norm[t]

    def lat_step(k, carry):
        for copy in fetch(k):
            copy.wait()
        for u in range(STEP):
            order = k * STEP + u
            both = mm_nt(prob[:, order].reshape(16, NDEG), leg[order])
            owner = order // OWN
            row = ((order - owner * OWN) * NT + owner) * 8
            lat_rows[pl.ds(pl.multiple_of(row, 8), 8), :] = jnp.concatenate([both[:8], both[8:]], axis=1)
        return carry

    lax.fori_loop(0, CHUNKS, lat_step, 0)
    for p in range(8):
        turned = lat_rows[pl.ds(p, 80, stride=8), :].T
        for half in range(2):
            for s in range(NC):
                start = half * 64 + s * 8
                lat_pack[s, half, p * 8 : (p + 1) * 8, :] = turned[start : start + 8, :]
    lat_send[...] = lat_pack[...].astype(BF)
    for i in range(1, NC):
        peer = (c + i) % NC
        send(lat_send.at[peer], lat_recv.at[c], 1, peer, t)
    lat_recv[c] = lat_send[c]
    arrived(part, NT - 1, 0)
    total = part[0]
    for s in range(1, NT):
        total = total + part[s]
    table[t] = total
    for i in range(1, NT):
        peer = (t + i) % NT
        send(table.at[t], table.at[t], 2, c, peer)

    orders = jnp.concatenate([order_ref[r : r + 1, :] for r in range(OWN)], axis=1)
    coarse = jnp.broadcast_to(lax.shift_right_logical(orders, 5).astype(F32).astype(BF), (128, ORDERS))
    fine = jnp.broadcast_to((orders & 31).astype(F32).astype(BF), (128, ORDERS))
    owner_row = lax.broadcasted_iota(jnp.int32, (128, ORDERS), 0) * OWN
    slot_lane = lax.broadcasted_iota(jnp.int32, (128, ORDERS), 1)
    lane = lax.broadcasted_iota(jnp.int32, (128, 128), 1).astype(F32)

    def trig(j, carry):
        hot = jnp.where(owner_row + j == slot_lane, 1.0, 0.0).astype(BF)
        order = 32.0 * mm_nt(hot, coarse) + mm_nt(hot, fine)
        cos_q[j], sin_q[j] = circle(order * lane)
        cosine, sine = circle(order * (lane * 128.0))
        cos_b[j] = cosine * (1.0 / math.sqrt(ORDERS))
        sin_b[j] = sine * (1.0 / math.sqrt(ORDERS))
        cq, sq, cb, sb = cos_q[j], sin_q[j], cos_b[j], sin_b[j]
        for b in range(10):
            ca, sa = cb[:, b : b + 1], sb[:, b : b + 1]
            cols = slice(b * 128, (b + 1) * 128)
            hi, lo = split(ca * cq - sa * sq)
            tab_hi[j, :, cols] = hi
            tab_lo[j, :, cols] = lo
            hi, lo = split(sa * cq + ca * sq)
            tab_hi[OWN + j, :, cols] = hi
            tab_lo[OWN + j, :, cols] = lo
        return carry

    lax.fori_loop(0, OWN, trig, 0)

    arrived(lat_recv, NC - 1, 1)
    grid = jnp.zeros((64, NLON), F32)
    for s in range(NC):
        own = slice(s * NT, (s + 1) * NT)
        for half in range(2):
            js = slice(half * OWN, (half + 1) * OWN)
            grid = grid + mm(lat_recv[s, half], tab_hi[js, own, :].reshape(80, NLON))
            grid = grid + mm(lat_recv[s, half], tab_lo[js, own, :].reshape(80, NLON))
    arrived(table, NT - 1, 2)
    for b in range(10):
        x = grid[:, b * 128 : (b + 1) * 128]

        def diagonal(d):
            unit = b * 4 + d
            block = table[unit // PIECE, unit % PIECE]
            return jnp.broadcast_to(block[None], (8, 8, 128)).reshape(64, 128)

        adj = diagonal(0) * x
        for d in range(1, 4):
            m = diagonal(d)
            adj = adj + m * pltpu.roll(x, 128 - d, axis=1) + pltpu.roll(m * x, d, axis=1)
        hi, lo = split(adj)
        adj_ref[:64, b * 128 : (b + 1) * 128] = hi
        adj_ref[64:, b * 128 : (b + 1) * 128] = lo
    for i in range(10):
        both = mm_nt(adj_ref[...], tab_hi[i])
        spec_ref[i] = both[:64] + both[64:] + mm_nt(adj_ref[:64, :], tab_lo[i])
    spec_ref[10:] = jnp.zeros((6, 64, 128), F32)
    for p in range(8):
        block = spec_ref[:, p * 8 : (p + 1) * 8, :].reshape(128, 128)
        turn_ref[pl.ds(p, 128, stride=8), :] = block.T
    spec[...] = turn_ref[...].reshape(128, 8, 128).astype(BF)

    def scatter(i, carry):
        peer = (me + i) % ND
        send(spec.at[peer], recv.at[me], 3, peer // NT, peer % NT)
        return carry

    lax.fori_loop(1, ND, scatter, 0)
    recv[me] = spec[me]

    same = (lax.broadcasted_iota(jnp.int32, (128, 128), 0) < 64) == (
        lax.broadcasted_iota(jnp.int32, (128, 128), 1) < 64
    )
    for j in range(OWN):
        one = leg[t * OWN + j]
        two = jnp.concatenate([one, one], axis=0)
        hi, lo = split(jnp.where(same, mm_nt(two, two), 0.0))
        normal[0, j] = hi
        normal[1, j] = lo
    row = lax.broadcasted_iota(jnp.int32, (128, 640), 0)
    col = lax.broadcasted_iota(jnp.int32, (128, 640), 1)
    src_i, src_a = lax.shift_right_logical(row, 3), row & 7
    dst_i = (lax.shift_right_logical(col, 6) & 1) * OWN + lax.shift_right_logical(col, 7)
    dst_band, dst_a = lax.shift_right_logical(col, 3) & 7, col & 7
    hit = (src_a == dst_a) & (src_i == dst_i)
    for s in range(NC):
        perm[s * 128 : (s + 1) * 128, :] = jnp.where(hit & (dst_band == s), 1.0, 0.0).astype(BF)
    arrived(recv, ND - 1, 3)
    gathered = jnp.zeros((128, 640), F32)
    for s in range(NC):
        block = recv[s * NT : (s + 1) * NT].astype(F32).reshape(128, 128).astype(BF)
        gathered = gathered + mm(block, perm[s * 128 : (s + 1) * 128, :])
    gram = jnp.zeros((128, 128), F32)
    for j in range(OWN):
        mine = gathered[:, j * 128 : (j + 1) * 128].astype(BF)
        rows_out[j] = mine
        hi, lo = split(mm(mine, normal[0, j]) + mm(mine, normal[1, j]))
        gram = gram + mm_nt(hi, mine) + mm_nt(lo, mine)
    g_part[...] = gram.reshape(NC, 16, 128)
    for i in range(1, NC):
        peer = (c + i) % NC
        send(g_part.at[peer], g_coef.at[c], 4, peer, t)
    g_coef[c] = g_part[c]
    arrived(g_coef, NC - 1, 4)
    total = g_coef[0]
    for s in range(1, NC):
        total = total + g_coef[s]
    g_track[t] = total
    for i in range(1, NT):
        peer = (t + i) % NT
        send(g_track.at[t], g_track.at[t], 5, c, peer)
    arrived(g_track, NT - 1, 5)
    total = g_track[0]
    for s in range(1, NT):
        total = total + g_track[s]
    gram_out[c] = total * (1.0 / (2 * ORDERS * NDEG))
    for i in range(1, NC):
        peer = (c + i) % NC
        send(gram_out.at[c], gram_out.at[c], 6, peer, t)
    arrived(gram_out, NC - 1, 6)
    for ref, n, k in (
        (part, NT - 1, 0), (lat_send, NC - 1, 1), (table, NT - 1, 2), (spec, ND - 1, 3),
        (g_part, NC - 1, 4), (g_track, NT - 1, 5), (gram_out, NC - 1, 6),
    ):
        sent(ref, n, k)


def circle(x):
    quarter = jnp.floor(x * (1.0 / 320.0) + 0.5)
    y = (x - quarter * 320.0) * (2.0 * math.pi / NLON)
    turn = quarter - 4.0 * jnp.floor(quarter * 0.25)
    z = y * y
    sine = y * (1.0 + z * (-1.0 / 6 + z * (1.0 / 120 + z * (-1.0 / 5040 + z * (1.0 / 362880)))))
    cosine = 1.0 + z * (-0.5 + z * (1.0 / 24 + z * (-1.0 / 720 + z * (1.0 / 40320 - z * (1.0 / 3628800)))))
    odd = (turn == 1.0) | (turn == 3.0)
    cos_x = jnp.where(odd, sine, cosine)
    sin_x = jnp.where(odd, cosine, sine)
    cos_x = jnp.where((turn == 1.0) | (turn == 2.0), -cos_x, cos_x)
    sin_x = jnp.where(turn >= 2.0, -sin_x, sin_x)
    return cos_x, sin_x


def front_stage(probes, legendre, orders, index, count, base, coef, weight):
    slots, obs = base.shape
    vm = pltpu.VMEM
    any_space = pl.BlockSpec(memory_space=pl.ANY)
    return pl.pallas_call(
        front_kernel,
        name="front_stage",
        out_shape=(jax.ShapeDtypeStruct((OWN, 128, 128), BF), jax.ShapeDtypeStruct((NC, 16, 128), F32)),
        in_specs=[any_space, any_space, VM, VM, VM, any_space, any_space, any_space],
        out_specs=(VM, VM),
        scratch_shapes=[
            vm(legendre.shape, BF), vm(probes.shape, BF),
            vm(base.shape, jnp.int32), vm(coef.shape, BF), vm(weight.shape, F32), vm(weight.shape, F32),
            vm((slots, 32, 128), F32),
            vm((NT, PIECE, 8, 128), F32), vm((NT, PIECE, 8, 128), F32), vm((NT, PIECE, 8, 128), F32),
            vm((640, 128), F32),
            vm((NC, 2, 64, 80), F32), vm((NC, 2, 64, 80), BF), vm((NC, 2, 64, 80), BF),
            vm((OWN, 128, 128), F32), vm((OWN, 128, 128), F32), vm((OWN, 128, 128), F32), vm((OWN, 128, 128), F32),
            vm((10, 128, NLON), BF), vm((10, 128, NLON), BF),
            vm((128, NLON), BF), vm((16, 64, 128), F32), vm((1024, 128), F32),
            vm((ND, 8, 128), BF), vm((ND, 8, 128), BF), vm((1024, 640), BF), vm((2, OWN, 128, 128), BF),
            vm((NC, 16, 128), F32), vm((NC, 16, 128), F32), vm((NT, 16, 128), F32),
            pltpu.SemaphoreType.DMA((3,)), pltpu.SemaphoreType.DMA((CHUNKS,)),
            pltpu.SemaphoreType.DMA((CHUNKS,)), pltpu.SemaphoreType.DMA((14,)),
        ],
        compiler_params=pltpu.CompilerParams(
            collective_id=0, has_side_effects=True, vmem_limit_bytes=56 * 1024 * 1024
        ),
    )(probes, legendre, orders, index, count, base, coef, weight)


def exact(a, b, dims):
    return lax.dot_general(a, b, (dims, ((), ())), precision=HIGHEST, preferred_element_type=F32)


NN = ((1,), (0,))
NT_DIMS = ((1,), (1,))


def factorize(gram, upper_ref, inv_ref):
    n = gram.shape[0]
    row = lax.broadcasted_iota(jnp.int32, (n, n), 0)
    col = lax.broadcasted_iota(jnp.int32, (n, n), 1)
    eye = jnp.where(row == col, 1.0, 0.0)
    half = jnp.where(row > col, 1.0, 0.5 * eye)
    diag = jnp.where(row == col, gram, 0.0)
    r_col = lax.rsqrt(jnp.sum(diag, axis=1, keepdims=True))
    r_row = lax.rsqrt(jnp.sum(diag, axis=0, keepdims=True))
    inverse = (eye - half * (gram * r_col * r_row - eye)) * r_row
    error = eye
    for _ in range(3):
        error = exact(exact(inverse, gram, NN), inverse, NT_DIMS) - eye
        inverse = inverse - exact(half * error, inverse, NN)
    inv_ref[...] = inverse
    upper_ref[...] = jnp.where(row <= col, exact(inverse, gram, NN), 0.0)
    worst = jnp.max(jnp.abs(error))

    @pl.when(jnp.logical_not(worst < 1e-4))
    def _():
        def column(j, state):
            left, upper, inv = state
            at_row, at_col = row == j, col == j
            line = jnp.sum(jnp.where(at_row, left, 0.0), axis=0, keepdims=True)
            down = jnp.sum(jnp.where(at_col, left, 0.0), axis=1, keepdims=True)
            pivot = jnp.sum(jnp.where(at_row & at_col, left, 0.0), keepdims=True)
            scale = 1.0 / jnp.sqrt(pivot)
            line = jnp.where(col[:1] >= j, line * scale, 0.0)
            below = jnp.where(row[:, :1] > j, down * scale, 0.0)
            inv_line = jnp.sum(jnp.where(at_row, inv, 0.0), axis=0, keepdims=True) * scale
            inv = jnp.where(at_row, inv_line, inv - below * inv_line)
            upper = jnp.where(at_row, line, upper)
            return left - below * line, upper, inv

        _, upper, inv = lax.fori_loop(0, n, column, (gram, jnp.zeros_like(gram), eye))
        upper_ref[...] = upper
        inv_ref[...] = inv


def panel_kernel(first_ref, gram_ref, rows_ref, leg_ref, out_ref, upper_ref, inv_ref):
    @pl.when(pl.program_id(0) == 0)
    def _():
        factorize(gram_ref[...].reshape(128, 128), upper_ref, inv_ref)

    hi, lo = split(inv_ref[...])
    z = mm(hi, rows_ref[0]) + mm(lo, rows_ref[0])
    z_hi, z_lo = split(z)
    left = lax.broadcasted_iota(jnp.int32, (128, 128), 1) < 64
    hi_f, lo_f = z_hi.astype(F32), z_lo.astype(F32)
    cosine = jnp.where(left, hi_f, pltpu.roll(lo_f, 64, axis=1)).astype(BF)
    sine = jnp.where(left, pltpu.roll(hi_f, 64, axis=1), lo_f).astype(BF)
    one = leg_ref[0]
    two = jnp.concatenate([one, one], axis=0)
    contract = (((0,), (1,)), ((), ()))
    out_ref[0, 0] = lax.dot_general(two, cosine, contract, preferred_element_type=F32)
    out_ref[1, 0] = lax.dot_general(two, sine, contract, preferred_element_type=F32)


def panel_stage(first, gram, rows, legendre):
    return pl.pallas_call(
        panel_kernel,
        name="panel_stage",
        out_shape=(
            jax.ShapeDtypeStruct((2, OWN, NDEG, 128), F32),
            jax.ShapeDtypeStruct((128, 128), F32),
        ),
        grid_spec=pltpu.PrefetchScalarGridSpec(
            num_scalar_prefetch=1,
            grid=(OWN,),
            in_specs=[
                pl.BlockSpec((NC, 16, 128), lambda j, first: (0, 0, 0)),
                pl.BlockSpec((1, 128, 128), lambda j, first: (j, 0, 0)),
                pl.BlockSpec((1, 64, NDEG), lambda j, first: (first[0] + j, 0, 0)),
            ],
            out_specs=(
                pl.BlockSpec((2, 1, NDEG, 128), lambda j, first: (0, j, 0, 0)),
                pl.BlockSpec((128, 128), lambda j, first: (0, 0)),
            ),
            scratch_shapes=[pltpu.VMEM((128, 128), F32)],
        ),
    )(first, gram, rows, legendre)


def on_device(
    probes, legendre, order_map, tile_index, tile_count, base_offset, stencil_weight, obs_weight
):
    rows, gram = front_stage(
        probes, legendre, order_map.reshape(OWN, 128), tile_index[0], tile_count,
        base_offset[0, 0], stencil_weight[0, 0], obs_weight[0, 0],
    )
    first = jnp.reshape(lax.axis_index("track") * OWN, (1,))
    panel, upper = panel_stage(first, gram, rows, legendre)
    return (jnp.swapaxes(panel, 2, 3), upper)


def solution(mesh):
    return jax.shard_map(
        on_device,
        mesh=mesh,
        in_specs=(
            P(None, "coef", "track", None),
            P("coef", None, None),
            P(),
            P("coef", None, None),
            P("coef", None),
            P("coef", "track", None, None),
            P("coef", "track", None, None, None),
            P("coef", "track", None, None),
        ),
        out_specs=(P(None, ("coef", "track"), None, None), P()),
        check_vma=False,
    )
```

```python
import math

import jax
import jax.numpy as jnp
from jax import lax
from jax.experimental import pallas as pl
from jax.experimental.pallas import tpu as pltpu
from jax.sharding import PartitionSpec as P

NDEG = 1200
ORDERS = 640
NLON = 1280
NC = 8
NT = 16
ND = NC * NT
OWN = 5
UNITS = 40
PIECE = 3
STEP = 16
CHUNKS = 5

BF = jnp.bfloat16
F32 = jnp.float32
HIGHEST = lax.Precision.HIGHEST
MESH = pl.DeviceIdType.MESH
VM = pl.BlockSpec(memory_space=pltpu.VMEM)


def mm(a, b):
    return lax.dot_general(a, b, (((1,), (0,)), ((), ())), preferred_element_type=F32)


def mm_nt(a, b):
    return lax.dot_general(a, b, (((1,), (1,)), ((), ())), preferred_element_type=F32)


def split(x):
    hi = x.astype(BF)
    return hi, (x - hi.astype(F32)).astype(BF)


def front_kernel(
    probes_ref, leg_ref, order_ref, index_ref, count_ref, base_ref, coef_ref, weight_ref,
    rows_out, gram_out, turned_out,
    leg, prob, base, coef, weight, live, hist, norm, part, table, lat_rows, lat_pack, lat_send, lat_recv,
    cos_q, sin_q, cos_b, sin_b, tab_hi, tab_lo, adj_ref, spec_ref, turn_ref, spec, recv, perm, normal,
    g_part, g_coef, g_track, turned_leg, in_sem, leg_sem, prob_sem, turn_sem, comm, ready,
):
    c = lax.axis_index("coef")
    t = lax.axis_index("track")
    me = c * NT + t

    def send(src, dst, k, pc, pt):
        pltpu.make_async_remote_copy(
            src, dst, comm.at[2 * k], comm.at[2 * k + 1], device_id=(pc, pt), device_id_type=MESH
        ).start()

    def arrived(ref, n, k):
        pltpu.make_async_copy(ref.at[pl.ds(0, n)], ref.at[pl.ds(0, n)], comm.at[2 * k + 1]).wait()

    def sent(ref, n, k):
        pltpu.make_async_copy(ref.at[pl.ds(0, n)], ref.at[pl.ds(0, n)], comm.at[2 * k]).wait()

    z, core = lax.div(c, 2), lax.rem(c, 2)
    y, x = lax.div(t, 4), lax.rem(t, 4)
    far = (0, 1, 2, 1)
    bands = {(dz, dk): lax.rem(z + dz, 4) * 2 + lax.rem(core + dk, 2) for dz in range(4) for dk in range(2)}
    tracks = {(dy, dx): lax.rem(y + dy, 4) * 4 + lax.rem(x + dx, 4) for dy in range(4) for dx in range(4)}
    steps = [(dz, dk, dy, dx) for dz in range(4) for dk in range(2) for dy in range(4) for dx in range(4)]
    steps.sort(key=lambda d: -(far[d[0]] + far[d[2]] + far[d[3]]) * 2 - d[1])
    peers = [(bands[d[:2]], tracks[d[2:]]) for d in steps if any(d)]

    small = [
        pltpu.make_async_copy(src, dst, in_sem.at[k])
        for k, (src, dst) in enumerate(((base_ref, base), (coef_ref, coef), (weight_ref, weight)))
    ]
    for copy in small:
        copy.start()

    def fetch(k):
        orders = pl.ds(k * STEP, STEP)
        return (
            pltpu.make_async_copy(leg_ref.at[orders], leg.at[orders], leg_sem.at[k]),
            pltpu.make_async_copy(probes_ref.at[:, orders], prob.at[:, orders], prob_sem.at[k]),
        )

    barrier = pltpu.get_barrier_semaphore()

    for i in range(1, NC):
        pl.semaphore_signal(barrier, 1, device_id=(lax.rem(c + i, NC), t), device_id_type=MESH)
    for i in range(1, NT):
        pl.semaphore_signal(barrier, 1, device_id=(c, lax.rem(t + i, NT)), device_id_type=MESH)

    for copy in small:
        copy.wait()
    for k in range(CHUNKS):
        for copy in fetch(k):
            copy.start()
    slots, obs = base.shape
    lane16 = lax.broadcasted_iota(jnp.int32, (1, NT), 1)
    count = jnp.sum(jnp.where(lane16 == t, count_ref[...].astype(F32), 0.0), axis=1, keepdims=True)
    slot_id = lax.broadcasted_iota(jnp.int32, (slots, obs), 0).astype(F32)
    live[...] = jnp.where(slot_id < count, weight[...], 0.0)
    points = lax.broadcasted_iota(jnp.int32, (128, obs), 0)

    def slot(group, carry):
        for u in range(4):
            s = group * 4 + u
            hot = jnp.where(points == base[pl.ds(s, 1), :], 1.0, 0.0).astype(BF)
            four = coef[s].astype(F32)
            eight = jnp.concatenate([four, jnp.zeros_like(four)], axis=0)
            scaled = eight * live[pl.ds(s, 1), :]
            full = jnp.concatenate(
                [scaled * eight] + [scaled * pltpu.roll(eight, 8 - d, axis=0) for d in range(1, 4)], axis=0
            )
            hi, mid = split(full)
            low = (full - hi.astype(F32) - mid.astype(F32)).astype(BF)
            sums = mm_nt(jnp.concatenate([hi, mid, low], axis=0), hot)
            hist[s] = sums[:32] + sums[32:64] + sums[64:]
        return carry

    lax.fori_loop(0, slots // 4, slot, 0)
    diagonals = []
    for d in range(4):
        total = hist[:, 8 * d, :]
        for i in range(1, 4 - d):
            total = total + pltpu.roll(hist[:, 8 * d + i, :], i, axis=1)
        diagonals.append(total)
    rows = lax.broadcasted_iota(jnp.int32, (80, slots), 0)
    tile = (rows & 7) * 10 + lax.shift_right_logical(rows, 3)
    pick = jnp.where(tile == index_ref[pl.ds(t, 1), :], 1.0, 0.0)
    summed = exact(pick, jnp.concatenate(diagonals, axis=1), NN)
    for u in range(NT * PIECE):
        if u < UNITS:
            b, d = u // 4, u % 4
            block = summed[b * 8 : (b + 1) * 8, d * 128 : (d + 1) * 128]
        else:
            block = jnp.zeros((8, 128), F32)
        norm[u // PIECE, u % PIECE] = block
    pl.semaphore_wait(barrier, NC + NT - 2)
    for i in range(1, NT):
        pl.semaphore_signal(ready, 1, device_id=(c, lax.rem(t + i, NT)), device_id_type=MESH)
    for i in range(1, NT):
        peer = (t + i) % NT
        send(norm.at[peer], part.at[t], 0, c, peer)
    part[t] = norm[t]

    def lat_step(k, carry):
        for copy in fetch(k):
            copy.wait()
        for u in range(STEP):
            order = k * STEP + u
            both = mm_nt(prob[:, order].reshape(16, NDEG), leg[order])
            owner = order // OWN
            row = ((order - owner * OWN) * NT + owner) * 8
            lat_rows[pl.ds(pl.multiple_of(row, 8), 8), :] = jnp.concatenate([both[:8], both[8:]], axis=1)
        return carry

    lax.fori_loop(0, CHUNKS, lat_step, 0)
    for p in range(8):
        turned = lat_rows[pl.ds(p, 80, stride=8), :].T
        for half in range(2):
            for s in range(NC):
                start = half * 64 + s * 8
                lat_pack[s, half, p * 8 : (p + 1) * 8, :] = turned[start : start + 8, :]
    lat_send[...] = lat_pack[...].astype(BF)
    for i in range(1, NC):
        peer = (c + i) % NC
        send(lat_send.at[peer], lat_recv.at[c], 1, peer, t)
    lat_recv[c] = lat_send[c]
    arrived(part, NT - 1, 0)
    total = part[0]
    for s in range(1, NT):
        total = total + part[s]
    table[t] = total
    for i in range(1, NT):
        peer = (t + i) % NT
        send(table.at[t], table.at[t], 2, c, peer)

    orders = jnp.concatenate([order_ref[r : r + 1, :] for r in range(OWN)], axis=1)
    coarse = jnp.broadcast_to(lax.shift_right_logical(orders, 5).astype(F32).astype(BF), (128, ORDERS))
    fine = jnp.broadcast_to((orders & 31).astype(F32).astype(BF), (128, ORDERS))
    owner_row = lax.broadcasted_iota(jnp.int32, (128, ORDERS), 0) * OWN
    slot_lane = lax.broadcasted_iota(jnp.int32, (128, ORDERS), 1)
    lane = lax.broadcasted_iota(jnp.int32, (128, 128), 1).astype(F32)

    def trig(j, carry):
        hot = jnp.where(owner_row + j == slot_lane, 1.0, 0.0).astype(BF)
        order = 32.0 * mm_nt(hot, coarse) + mm_nt(hot, fine)
        cos_q[j], sin_q[j] = circle(order * lane)
        cosine, sine = circle(order * (lane * 128.0))
        cos_b[j] = cosine * (1.0 / math.sqrt(ORDERS))
        sin_b[j] = sine * (1.0 / math.sqrt(ORDERS))
        cq, sq, cb, sb = cos_q[j], sin_q[j], cos_b[j], sin_b[j]
        for b in range(10):
            ca, sa = cb[:, b : b + 1], sb[:, b : b + 1]
            cols = slice(b * 128, (b + 1) * 128)
            hi, lo = split(ca * cq - sa * sq)
            tab_hi[j, :, cols] = hi
            tab_lo[j, :, cols] = lo
            hi, lo = split(sa * cq + ca * sq)
            tab_hi[OWN + j, :, cols] = hi
            tab_lo[OWN + j, :, cols] = lo
        return carry

    lax.fori_loop(0, OWN, trig, 0)

    arrived(lat_recv, NC - 1, 1)
    grid = jnp.zeros((64, NLON), F32)
    for s in range(NC):
        own = slice(s * NT, (s + 1) * NT)
        for half in range(2):
            js = slice(half * OWN, (half + 1) * OWN)
            grid = grid + mm(lat_recv[s, half], tab_hi[js, own, :].reshape(80, NLON))
            grid = grid + mm(lat_recv[s, half], tab_lo[js, own, :].reshape(80, NLON))
    arrived(table, NT - 1, 2)
    for b in range(10):
        x = grid[:, b * 128 : (b + 1) * 128]

        def diagonal(d):
            unit = b * 4 + d
            block = table[unit // PIECE, unit % PIECE]
            return jnp.broadcast_to(block[None], (8, 8, 128)).reshape(64, 128)

        adj = diagonal(0) * x
        for d in range(1, 4):
            m = diagonal(d)
            adj = adj + m * pltpu.roll(x, 128 - d, axis=1) + pltpu.roll(m * x, d, axis=1)
        hi, lo = split(adj)
        adj_ref[:64, b * 128 : (b + 1) * 128] = hi
        adj_ref[64:, b * 128 : (b + 1) * 128] = lo
    for i in range(10):
        both = mm_nt(adj_ref[...], tab_hi[i])
        spec_ref[i] = both[:64] + both[64:] + mm_nt(adj_ref[:64, :], tab_lo[i])
    spec_ref[10:] = jnp.zeros((6, 64, 128), F32)
    for p in range(8):
        block = spec_ref[:, p * 8 : (p + 1) * 8, :].reshape(128, 128)
        turn_ref[pl.ds(p, 128, stride=8), :] = block.T
    spec[...] = turn_ref[...].reshape(128, 8, 128).astype(BF)

    pl.semaphore_wait(ready, NT - 1)
    for pc, pt in peers:
        send(spec.at[pc * NT + pt], recv.at[me], 3, pc, pt)
    recv[me] = spec[me]

    same = (lax.broadcasted_iota(jnp.int32, (128, 128), 0) < 64) == (
        lax.broadcasted_iota(jnp.int32, (128, 128), 1) < 64
    )
    for j in range(OWN):
        one = leg[t * OWN + j]
        two = jnp.concatenate([one, one], axis=0)
        hi, lo = split(jnp.where(same, mm_nt(two, two), 0.0))
        normal[0, j] = hi
        normal[1, j] = lo
    row = lax.broadcasted_iota(jnp.int32, (128, 640), 0)
    col = lax.broadcasted_iota(jnp.int32, (128, 640), 1)
    src_i, src_a = lax.shift_right_logical(row, 3), row & 7
    dst_i = (lax.shift_right_logical(col, 6) & 1) * OWN + lax.shift_right_logical(col, 7)
    dst_band, dst_a = lax.shift_right_logical(col, 3) & 7, col & 7
    hit = (src_a == dst_a) & (src_i == dst_i)
    for s in range(NC):
        perm[s * 128 : (s + 1) * 128, :] = jnp.where(hit & (dst_band == s), 1.0, 0.0).astype(BF)
    arrived(recv, ND - 1, 3)
    gathered = jnp.zeros((128, 640), F32)
    for s in range(NC):
        block = recv[s * NT : (s + 1) * NT].astype(F32).reshape(128, 128).astype(BF)
        gathered = gathered + mm(block, perm[s * 128 : (s + 1) * 128, :])
    gram = jnp.zeros((128, 128), F32)
    for j in range(OWN):
        mine = gathered[:, j * 128 : (j + 1) * 128].astype(BF)
        rows_out[j] = mine
        hi, lo = split(mm(mine, normal[0, j]) + mm(mine, normal[1, j]))
        gram = gram + mm_nt(hi, mine) + mm_nt(lo, mine)
    g_part[...] = gram.reshape(NC, 16, 128)

    def turn(j):
        one = leg[t * OWN + j]
        turned_leg[j] = jnp.concatenate([one, one], axis=0).T
        pltpu.make_async_copy(turned_leg.at[j], turned_out.at[j], turn_sem.at[j]).start()

    for i in range(1, NC):
        peer = (c + i) % NC
        send(g_part.at[peer], g_coef.at[c], 4, peer, t)
    g_coef[c] = g_part[c]
    turn(0)
    turn(1)
    arrived(g_coef, NC - 1, 4)
    total = g_coef[0]
    for s in range(1, NC):
        total = total + g_coef[s]
    g_track[t] = total
    for i in range(1, NT):
        peer = (t + i) % NT
        send(g_track.at[t], g_track.at[t], 5, c, peer)
    turn(2)
    turn(3)
    arrived(g_track, NT - 1, 5)
    total = g_track[0]
    for s in range(1, NT):
        total = total + g_track[s]
    gram_out[c] = total * (1.0 / (2 * ORDERS * NDEG))
    for i in range(1, NC):
        peer = (c + i) % NC
        send(gram_out.at[c], gram_out.at[c], 6, peer, t)
    turn(4)
    arrived(gram_out, NC - 1, 6)
    for j in range(OWN):
        pltpu.make_async_copy(turned_leg.at[j], turned_out.at[j], turn_sem.at[j]).wait()
    for ref, n, k in (
        (part, NT - 1, 0), (lat_send, NC - 1, 1), (table, NT - 1, 2), (spec, ND - 1, 3),
        (g_part, NC - 1, 4), (g_track, NT - 1, 5), (gram_out, NC - 1, 6),
    ):
        sent(ref, n, k)


def circle(x):
    quarter = jnp.floor(x * (1.0 / 320.0) + 0.5)
    y = (x - quarter * 320.0) * (2.0 * math.pi / NLON)
    turn = quarter - 4.0 * jnp.floor(quarter * 0.25)
    z = y * y
    sine = y * (1.0 + z * (-1.0 / 6 + z * (1.0 / 120 + z * (-1.0 / 5040 + z * (1.0 / 362880)))))
    cosine = 1.0 + z * (-0.5 + z * (1.0 / 24 + z * (-1.0 / 720 + z * (1.0 / 40320 - z * (1.0 / 3628800)))))
    odd = (turn == 1.0) | (turn == 3.0)
    cos_x = jnp.where(odd, sine, cosine)
    sin_x = jnp.where(odd, cosine, sine)
    cos_x = jnp.where((turn == 1.0) | (turn == 2.0), -cos_x, cos_x)
    sin_x = jnp.where(turn >= 2.0, -sin_x, sin_x)
    return cos_x, sin_x


def front_stage(probes, legendre, orders, index, count, base, coef, weight):
    slots, obs = base.shape
    vm = pltpu.VMEM
    any_space = pl.BlockSpec(memory_space=pl.ANY)
    return pl.pallas_call(
        front_kernel,
        name="front_stage",
        out_shape=(jax.ShapeDtypeStruct((OWN, 128, 128), BF), jax.ShapeDtypeStruct((NC, 16, 128), F32),
                   jax.ShapeDtypeStruct((OWN, NDEG, 128), BF)),
        in_specs=[any_space, any_space, VM, VM, VM, any_space, any_space, any_space],
        out_specs=(VM, VM, any_space),
        scratch_shapes=[
            vm(legendre.shape, BF), vm(probes.shape, BF),
            vm(base.shape, jnp.int32), vm(coef.shape, BF), vm(weight.shape, F32), vm(weight.shape, F32),
            vm((slots, 32, 128), F32),
            vm((NT, PIECE, 8, 128), F32), vm((NT, PIECE, 8, 128), F32), vm((NT, PIECE, 8, 128), F32),
            vm((640, 128), F32),
            vm((NC, 2, 64, 80), F32), vm((NC, 2, 64, 80), BF), vm((NC, 2, 64, 80), BF),
            vm((OWN, 128, 128), F32), vm((OWN, 128, 128), F32), vm((OWN, 128, 128), F32), vm((OWN, 128, 128), F32),
            vm((10, 128, NLON), BF), vm((10, 128, NLON), BF),
            vm((128, NLON), BF), vm((16, 64, 128), F32), vm((1024, 128), F32),
            vm((ND, 8, 128), BF), vm((ND, 8, 128), BF), vm((1024, 640), BF), vm((2, OWN, 128, 128), BF),
            vm((NC, 16, 128), F32), vm((NC, 16, 128), F32), vm((NT, 16, 128), F32),
            vm((OWN, NDEG, 128), BF),
            pltpu.SemaphoreType.DMA((3,)), pltpu.SemaphoreType.DMA((CHUNKS,)),
            pltpu.SemaphoreType.DMA((CHUNKS,)), pltpu.SemaphoreType.DMA((OWN,)), pltpu.SemaphoreType.DMA((14,)),
            pltpu.SemaphoreType.REGULAR,
        ],
        compiler_params=pltpu.CompilerParams(
            collective_id=0, has_side_effects=True, vmem_limit_bytes=56 * 1024 * 1024
        ),
    )(probes, legendre, orders, index, count, base, coef, weight)


def exact(a, b, dims):
    return lax.dot_general(a, b, (dims, ((), ())), precision=HIGHEST, preferred_element_type=F32)


NN = ((1,), (0,))


def three(a, b, product):
    a_hi, a_lo = split(a)
    b_hi, b_lo = split(b)
    return product(a_hi, b_hi) + product(a_hi, b_lo) + product(a_lo, b_hi)


def factorize(gram, upper_ref, inv_ref):
    n = gram.shape[0]
    row = lax.broadcasted_iota(jnp.int32, (n, n), 0)
    col = lax.broadcasted_iota(jnp.int32, (n, n), 1)
    eye = jnp.where(row == col, 1.0, 0.0)
    half = jnp.where(row > col, 1.0, 0.5 * eye)
    diag = jnp.where(row == col, gram, 0.0)
    r_col = lax.rsqrt(jnp.sum(diag, axis=1, keepdims=True))
    r_row = lax.rsqrt(jnp.sum(diag, axis=0, keepdims=True))
    inverse = (eye - half * (gram * r_col * r_row - eye)) * r_row
    error = eye
    for _ in range(3):
        error = three(three(inverse, gram, mm), inverse, mm_nt) - eye
        inverse = inverse - three(half * error, inverse, mm)
    inv_ref[...] = inverse
    upper_ref[...] = jnp.where(row <= col, three(inverse, gram, mm), 0.0)
    worst = jnp.max(jnp.abs(error))

    @pl.when(jnp.logical_not(worst < 1e-4))
    def _():
        def column(j, state):
            left, upper, inv = state
            at_row, at_col = row == j, col == j
            line = jnp.sum(jnp.where(at_row, left, 0.0), axis=0, keepdims=True)
            down = jnp.sum(jnp.where(at_col, left, 0.0), axis=1, keepdims=True)
            pivot = jnp.sum(jnp.where(at_row & at_col, left, 0.0), keepdims=True)
            scale = 1.0 / jnp.sqrt(pivot)
            line = jnp.where(col[:1] >= j, line * scale, 0.0)
            below = jnp.where(row[:, :1] > j, down * scale, 0.0)
            inv_line = jnp.sum(jnp.where(at_row, inv, 0.0), axis=0, keepdims=True) * scale
            inv = jnp.where(at_row, inv_line, inv - below * inv_line)
            upper = jnp.where(at_row, line, upper)
            return left - below * line, upper, inv

        _, upper, inv = lax.fori_loop(0, n, column, (gram, jnp.zeros_like(gram), eye))
        upper_ref[...] = upper
        inv_ref[...] = inv


def panel_kernel(gram_ref, rows_ref, leg_ref, out_ref, upper_ref, inv_ref):
    @pl.when(pl.program_id(0) == 0)
    def _():
        factorize(gram_ref[...].reshape(128, 128), upper_ref, inv_ref)

    hi, lo = split(inv_ref[...])
    z = mm(hi, rows_ref[0]) + mm(lo, rows_ref[0])
    z_hi, z_lo = split(z)
    left = lax.broadcasted_iota(jnp.int32, (128, 128), 1) < 64
    hi_f, lo_f = z_hi.astype(F32), z_lo.astype(F32)
    cosine = jnp.where(left, hi_f, pltpu.roll(lo_f, 64, axis=1)).astype(BF)
    sine = jnp.where(left, pltpu.roll(hi_f, 64, axis=1), lo_f).astype(BF)
    out_ref[0, 0] = mm_nt(leg_ref[0], cosine)
    out_ref[1, 0] = mm_nt(leg_ref[0], sine)


def panel_stage(gram, rows, turned):
    return pl.pallas_call(
        panel_kernel,
        name="panel_stage",
        grid=(OWN,),
        out_shape=(
            jax.ShapeDtypeStruct((2, OWN, NDEG, 128), F32),
            jax.ShapeDtypeStruct((128, 128), F32),
        ),
        in_specs=[
            pl.BlockSpec((NC, 16, 128), lambda j: (0, 0, 0)),
            pl.BlockSpec((1, 128, 128), lambda j: (j, 0, 0)),
            pl.BlockSpec((1, NDEG, 128), lambda j: (j, 0, 0)),
        ],
        out_specs=(
            pl.BlockSpec((2, 1, NDEG, 128), lambda j: (0, j, 0, 0)),
            pl.BlockSpec((128, 128), lambda j: (0, 0)),
        ),
        scratch_shapes=[pltpu.VMEM((128, 128), F32)],
    )(gram, rows, turned)


def on_device(
    probes, legendre, order_map, tile_index, tile_count, base_offset, stencil_weight, obs_weight
):
    rows, gram, turned = front_stage(
        probes, legendre, order_map.reshape(OWN, 128), tile_index[0], tile_count,
        base_offset[0, 0], stencil_weight[0, 0], obs_weight[0, 0],
    )
    panel, upper = panel_stage(gram, rows, turned)
    return (jnp.swapaxes(panel, 2, 3), upper)


def solution(mesh):
    return jax.shard_map(
        on_device,
        mesh=mesh,
        in_specs=(
            P(None, "coef", "track", None),
            P("coef", None, None),
            P(),
            P("coef", None, None),
            P("coef", None),
            P("coef", "track", None, None),
            P("coef", "track", None, None, None),
            P("coef", "track", None, None),
        ),
        out_specs=(P(None, ("coef", "track"), None, None), P()),
        check_vma=False,
    )
```

```python
import math

import jax
import jax.numpy as jnp
from jax import lax
from jax.experimental import pallas as pl
from jax.experimental.pallas import tpu as pltpu
from jax.sharding import PartitionSpec as P

NDEG = 1200
ORDERS = 640
NLON = 1280
NC = 8
NT = 16
ND = NC * NT
OWN = 5
UNITS = 40
PIECE = 3
STEP = 20
CHUNKS = 4

BF = jnp.bfloat16
F32 = jnp.float32
HIGHEST = lax.Precision.HIGHEST
MESH = pl.DeviceIdType.MESH
VM = pl.BlockSpec(memory_space=pltpu.VMEM)


def mm(a, b):
    return lax.dot_general(a, b, (((1,), (0,)), ((), ())), preferred_element_type=F32)


def mm_nt(a, b):
    return lax.dot_general(a, b, (((1,), (1,)), ((), ())), preferred_element_type=F32)


def split(x):
    hi = x.astype(BF)
    return hi, (x - hi.astype(F32)).astype(BF)


def front_kernel(
    probes_ref, leg_ref, order_ref, index_ref, count_ref, base_ref, coef_ref, weight_ref,
    rows_out, gram_out, turned_out,
    leg, prob, base, coef, weight, live, hist, norm, part, table, lat_rows, lat_pack, lat_send, lat_recv,
    cos_q, sin_q, cos_b, sin_b, tab_hi, tab_lo, adj_ref, spec_ref, turn_ref, spec, recv, perm, normal,
    g_part, g_coef, g_track, turned_leg, in_sem, leg_sem, prob_sem, turn_sem, comm, ready,
):
    c = lax.axis_index("coef")
    t = lax.axis_index("track")
    me = c * NT + t

    def send(src, dst, k, pc, pt):
        pltpu.make_async_remote_copy(
            src, dst, comm.at[2 * k], comm.at[2 * k + 1], device_id=(pc, pt), device_id_type=MESH
        ).start()

    def arrived(ref, n, k):
        pltpu.make_async_copy(ref.at[pl.ds(0, n)], ref.at[pl.ds(0, n)], comm.at[2 * k + 1]).wait()

    def sent(ref, n, k):
        pltpu.make_async_copy(ref.at[pl.ds(0, n)], ref.at[pl.ds(0, n)], comm.at[2 * k]).wait()

    z, core = lax.div(c, 2), lax.rem(c, 2)
    y, x = lax.div(t, 4), lax.rem(t, 4)
    far = (0, 1, 2, 1)
    bands = {(dz, dk): lax.rem(z + dz, 4) * 2 + lax.rem(core + dk, 2) for dz in range(4) for dk in range(2)}
    tracks = {(dy, dx): lax.rem(y + dy, 4) * 4 + lax.rem(x + dx, 4) for dy in range(4) for dx in range(4)}
    steps = [(dz, dk, dy, dx) for dz in range(4) for dk in range(2) for dy in range(4) for dx in range(4)]
    steps.sort(key=lambda d: -(far[d[0]] + far[d[2]] + far[d[3]]) * 2 - d[1])
    peers = [(bands[d[:2]], tracks[d[2:]]) for d in steps if any(d)]

    small = [
        pltpu.make_async_copy(src, dst, in_sem.at[k])
        for k, (src, dst) in enumerate(((base_ref, base), (coef_ref, coef), (weight_ref, weight)))
    ]
    for copy in small:
        copy.start()

    def fetch(k):
        orders = pl.ds(k * STEP, STEP)
        return (
            pltpu.make_async_copy(leg_ref.at[orders], leg.at[orders], leg_sem.at[k]),
            pltpu.make_async_copy(probes_ref.at[:, orders], prob.at[:, orders], prob_sem.at[k]),
        )

    barrier = pltpu.get_barrier_semaphore()

    for i in range(1, NC):
        pl.semaphore_signal(barrier, 1, device_id=(lax.rem(c + i, NC), t), device_id_type=MESH)
    for i in range(1, NT):
        pl.semaphore_signal(barrier, 1, device_id=(c, lax.rem(t + i, NT)), device_id_type=MESH)

    for copy in small:
        copy.wait()
    for k in range(CHUNKS):
        for copy in fetch(k):
            copy.start()
    slots, obs = base.shape
    lane16 = lax.broadcasted_iota(jnp.int32, (1, NT), 1)
    count = jnp.sum(jnp.where(lane16 == t, count_ref[...].astype(F32), 0.0), axis=1, keepdims=True)
    slot_id = lax.broadcasted_iota(jnp.int32, (slots, obs), 0).astype(F32)
    live[...] = jnp.where(slot_id < count, weight[...], 0.0)
    points = lax.broadcasted_iota(jnp.int32, (128, obs), 0)

    def slot(group, carry):
        for u in range(4):
            s = group * 4 + u
            hot = jnp.where(points == base[pl.ds(s, 1), :], 1.0, 0.0).astype(BF)
            four = coef[s].astype(F32)
            eight = jnp.concatenate([four, jnp.zeros_like(four)], axis=0)
            scaled = eight * live[pl.ds(s, 1), :]
            full = jnp.concatenate(
                [scaled * eight] + [scaled * pltpu.roll(eight, 8 - d, axis=0) for d in range(1, 4)], axis=0
            )
            hi, mid = split(full)
            low = (full - hi.astype(F32) - mid.astype(F32)).astype(BF)
            sums = mm_nt(jnp.concatenate([hi, mid, low], axis=0), hot)
            hist[s] = sums[:32] + sums[32:64] + sums[64:]
        return carry

    lax.fori_loop(0, slots // 4, slot, 0)
    diagonals = []
    for d in range(4):
        total = hist[:, 8 * d, :]
        for i in range(1, 4 - d):
            total = total + pltpu.roll(hist[:, 8 * d + i, :], i, axis=1)
        diagonals.append(total)
    rows = lax.broadcasted_iota(jnp.int32, (80, slots), 0)
    tile = (rows & 7) * 10 + lax.shift_right_logical(rows, 3)
    pick = jnp.where(tile == index_ref[pl.ds(t, 1), :], 1.0, 0.0)
    summed = exact(pick, jnp.concatenate(diagonals, axis=1), NN)
    for u in range(NT * PIECE):
        if u < UNITS:
            b, d = u // 4, u % 4
            block = summed[b * 8 : (b + 1) * 8, d * 128 : (d + 1) * 128]
        else:
            block = jnp.zeros((8, 128), F32)
        norm[u // PIECE, u % PIECE] = block
    pl.semaphore_wait(barrier, NC + NT - 2)
    for i in range(1, NT):
        pl.semaphore_signal(ready, 1, device_id=(c, lax.rem(t + i, NT)), device_id_type=MESH)
    for i in range(1, NT):
        peer = (t + i) % NT
        send(norm.at[peer], part.at[t], 0, c, peer)
    part[t] = norm[t]

    def lat_step(k, carry):
        for copy in fetch(k):
            copy.wait()
        for u in range(STEP):
            order = k * STEP + u
            both = mm_nt(prob[:, order].reshape(16, NDEG), leg[order])
            owner = order // OWN
            row = ((order - owner * OWN) * NT + owner) * 8
            lat_rows[pl.ds(pl.multiple_of(row, 8), 8), :] = jnp.concatenate([both[:8], both[8:]], axis=1)
        return carry

    lax.fori_loop(0, CHUNKS, lat_step, 0)
    for p in range(8):
        turned = lat_rows[pl.ds(p, 80, stride=8), :].T
        for half in range(2):
            for s in range(NC):
                start = half * 64 + s * 8
                lat_pack[s, half, p * 8 : (p + 1) * 8, :] = turned[start : start + 8, :]
    lat_send[...] = lat_pack[...].astype(BF)
    for i in range(1, NC):
        peer = (c + i) % NC
        send(lat_send.at[peer], lat_recv.at[c], 1, peer, t)
    lat_recv[c] = lat_send[c]
    arrived(part, NT - 1, 0)
    total = part[0]
    for s in range(1, NT):
        total = total + part[s]
    table[t] = total
    for i in range(1, NT):
        peer = (t + i) % NT
        send(table.at[t], table.at[t], 2, c, peer)

    orders = jnp.concatenate([order_ref[r : r + 1, :] for r in range(OWN)], axis=1)
    coarse = jnp.broadcast_to(lax.shift_right_logical(orders, 5).astype(F32).astype(BF), (128, ORDERS))
    fine = jnp.broadcast_to((orders & 31).astype(F32).astype(BF), (128, ORDERS))
    owner_row = lax.broadcasted_iota(jnp.int32, (128, ORDERS), 0) * OWN
    slot_lane = lax.broadcasted_iota(jnp.int32, (128, ORDERS), 1)
    lane = lax.broadcasted_iota(jnp.int32, (128, 128), 1).astype(F32)

    def trig(j, carry):
        hot = jnp.where(owner_row + j == slot_lane, 1.0, 0.0).astype(BF)
        order = 32.0 * mm_nt(hot, coarse) + mm_nt(hot, fine)
        cos_q[j], sin_q[j] = circle(order * lane)
        cosine, sine = circle(order * (lane * 128.0))
        cos_b[j] = cosine * (1.0 / math.sqrt(ORDERS))
        sin_b[j] = sine * (1.0 / math.sqrt(ORDERS))
        cq, sq, cb, sb = cos_q[j], sin_q[j], cos_b[j], sin_b[j]
        for b in range(10):
            ca, sa = cb[:, b : b + 1], sb[:, b : b + 1]
            cols = slice(b * 128, (b + 1) * 128)
            hi, lo = split(ca * cq - sa * sq)
            tab_hi[j, :, cols] = hi
            tab_lo[j, :, cols] = lo
            hi, lo = split(sa * cq + ca * sq)
            tab_hi[OWN + j, :, cols] = hi
            tab_lo[OWN + j, :, cols] = lo
        return carry

    lax.fori_loop(0, OWN, trig, 0)

    arrived(lat_recv, NC - 1, 1)
    grid = jnp.zeros((64, NLON), F32)
    for s in range(NC):
        own = slice(s * NT, (s + 1) * NT)
        for half in range(2):
            js = slice(half * OWN, (half + 1) * OWN)
            grid = grid + mm(lat_recv[s, half], tab_hi[js, own, :].reshape(80, NLON))
            grid = grid + mm(lat_recv[s, half], tab_lo[js, own, :].reshape(80, NLON))
    arrived(table, NT - 1, 2)
    for b in range(10):
        x = grid[:, b * 128 : (b + 1) * 128]

        def diagonal(d):
            unit = b * 4 + d
            block = table[unit // PIECE, unit % PIECE]
            return jnp.broadcast_to(block[None], (8, 8, 128)).reshape(64, 128)

        adj = diagonal(0) * x
        for d in range(1, 4):
            m = diagonal(d)
            adj = adj + m * pltpu.roll(x, 128 - d, axis=1) + pltpu.roll(m * x, d, axis=1)
        hi, lo = split(adj)
        adj_ref[:64, b * 128 : (b + 1) * 128] = hi
        adj_ref[64:, b * 128 : (b + 1) * 128] = lo
    for i in range(10):
        both = mm_nt(adj_ref[...], tab_hi[i])
        spec_ref[i] = both[:64] + both[64:] + mm_nt(adj_ref[:64, :], tab_lo[i])
    spec_ref[10:] = jnp.zeros((6, 64, 128), F32)
    for p in range(8):
        block = spec_ref[:, p * 8 : (p + 1) * 8, :].reshape(128, 128)
        turn_ref[pl.ds(p, 128, stride=8), :] = block.T
    spec[...] = turn_ref[...].reshape(128, 8, 128).astype(BF)

    pl.semaphore_wait(ready, NT - 1)
    for pc, pt in peers:
        send(spec.at[pc * NT + pt], recv.at[me], 3, pc, pt)
    recv[me] = spec[me]

    same = (lax.broadcasted_iota(jnp.int32, (128, 128), 0) < 64) == (
        lax.broadcasted_iota(jnp.int32, (128, 128), 1) < 64
    )
    for j in range(OWN):
        one = leg[t * OWN + j]
        two = jnp.concatenate([one, one], axis=0)
        hi, lo = split(jnp.where(same, mm_nt(two, two), 0.0))
        normal[0, j] = hi
        normal[1, j] = lo
    row = lax.broadcasted_iota(jnp.int32, (128, 640), 0)
    col = lax.broadcasted_iota(jnp.int32, (128, 640), 1)
    src_i, src_a = lax.shift_right_logical(row, 3), row & 7
    dst_i = (lax.shift_right_logical(col, 6) & 1) * OWN + lax.shift_right_logical(col, 7)
    dst_band, dst_a = lax.shift_right_logical(col, 3) & 7, col & 7
    hit = (src_a == dst_a) & (src_i == dst_i)
    for s in range(NC):
        perm[s * 128 : (s + 1) * 128, :] = jnp.where(hit & (dst_band == s), 1.0, 0.0).astype(BF)
    arrived(recv, ND - 1, 3)
    gathered = jnp.zeros((128, 640), F32)
    for s in range(NC):
        block = recv[s * NT : (s + 1) * NT].astype(F32).reshape(128, 128).astype(BF)
        gathered = gathered + mm(block, perm[s * 128 : (s + 1) * 128, :])
    gram = jnp.zeros((128, 128), F32)
    for j in range(OWN):
        mine = gathered[:, j * 128 : (j + 1) * 128].astype(BF)
        rows_out[j] = mine
        hi, lo = split(mm(mine, normal[0, j]) + mm(mine, normal[1, j]))
        gram = gram + mm_nt(hi, mine) + mm_nt(lo, mine)
    g_part[...] = gram.reshape(NC, 16, 128)

    def turn(j):
        one = leg[t * OWN + j]
        turned_leg[j] = jnp.concatenate([one, one], axis=0).T
        pltpu.make_async_copy(turned_leg.at[j], turned_out.at[j], turn_sem.at[j]).start()

    for i in range(1, NC):
        peer = (c + i) % NC
        send(g_part.at[peer], g_coef.at[c], 4, peer, t)
    g_coef[c] = g_part[c]
    turn(0)
    turn(1)
    arrived(g_coef, NC - 1, 4)
    total = g_coef[0]
    for s in range(1, NC):
        total = total + g_coef[s]
    g_track[t] = total
    for i in range(1, NT):
        peer = (t + i) % NT
        send(g_track.at[t], g_track.at[t], 5, c, peer)
    turn(2)
    turn(3)
    arrived(g_track, NT - 1, 5)
    total = g_track[0]
    for s in range(1, NT):
        total = total + g_track[s]
    gram_out[c] = total * (1.0 / (2 * ORDERS * NDEG))
    for i in range(1, NC):
        peer = (c + i) % NC
        send(gram_out.at[c], gram_out.at[c], 6, peer, t)
    turn(4)
    arrived(gram_out, NC - 1, 6)
    for j in range(OWN):
        pltpu.make_async_copy(turned_leg.at[j], turned_out.at[j], turn_sem.at[j]).wait()
    for ref, n, k in (
        (part, NT - 1, 0), (lat_send, NC - 1, 1), (table, NT - 1, 2), (spec, ND - 1, 3),
        (g_part, NC - 1, 4), (g_track, NT - 1, 5), (gram_out, NC - 1, 6),
    ):
        sent(ref, n, k)


def circle(x):
    quarter = jnp.floor(x * (1.0 / 320.0) + 0.5)
    y = (x - quarter * 320.0) * (2.0 * math.pi / NLON)
    turn = quarter - 4.0 * jnp.floor(quarter * 0.25)
    z = y * y
    sine = y * (1.0 + z * (-1.0 / 6 + z * (1.0 / 120 + z * (-1.0 / 5040 + z * (1.0 / 362880)))))
    cosine = 1.0 + z * (-0.5 + z * (1.0 / 24 + z * (-1.0 / 720 + z * (1.0 / 40320 - z * (1.0 / 3628800)))))
    odd = (turn == 1.0) | (turn == 3.0)
    cos_x = jnp.where(odd, sine, cosine)
    sin_x = jnp.where(odd, cosine, sine)
    cos_x = jnp.where((turn == 1.0) | (turn == 2.0), -cos_x, cos_x)
    sin_x = jnp.where(turn >= 2.0, -sin_x, sin_x)
    return cos_x, sin_x


def front_stage(probes, legendre, orders, index, count, base, coef, weight):
    slots, obs = base.shape
    vm = pltpu.VMEM
    any_space = pl.BlockSpec(memory_space=pl.ANY)
    return pl.pallas_call(
        front_kernel,
        name="front_stage",
        out_shape=(jax.ShapeDtypeStruct((OWN, 128, 128), BF), jax.ShapeDtypeStruct((NC, 16, 128), F32),
                   jax.ShapeDtypeStruct((OWN, NDEG, 128), BF)),
        in_specs=[any_space, any_space, VM, VM, VM, any_space, any_space, any_space],
        out_specs=(VM, VM, any_space),
        scratch_shapes=[
            vm(legendre.shape, BF), vm(probes.shape, BF),
            vm(base.shape, jnp.int32), vm(coef.shape, BF), vm(weight.shape, F32), vm(weight.shape, F32),
            vm((slots, 32, 128), F32),
            vm((NT, PIECE, 8, 128), F32), vm((NT, PIECE, 8, 128), F32), vm((NT, PIECE, 8, 128), F32),
            vm((640, 128), F32),
            vm((NC, 2, 64, 80), F32), vm((NC, 2, 64, 80), BF), vm((NC, 2, 64, 80), BF),
            vm((OWN, 128, 128), F32), vm((OWN, 128, 128), F32), vm((OWN, 128, 128), F32), vm((OWN, 128, 128), F32),
            vm((10, 128, NLON), BF), vm((10, 128, NLON), BF),
            vm((128, NLON), BF), vm((16, 64, 128), F32), vm((1024, 128), F32),
            vm((ND, 8, 128), BF), vm((ND, 8, 128), BF), vm((1024, 640), BF), vm((2, OWN, 128, 128), BF),
            vm((NC, 16, 128), F32), vm((NC, 16, 128), F32), vm((NT, 16, 128), F32),
            vm((OWN, NDEG, 128), BF),
            pltpu.SemaphoreType.DMA((3,)), pltpu.SemaphoreType.DMA((CHUNKS,)),
            pltpu.SemaphoreType.DMA((CHUNKS,)), pltpu.SemaphoreType.DMA((OWN,)), pltpu.SemaphoreType.DMA((14,)),
            pltpu.SemaphoreType.REGULAR,
        ],
        compiler_params=pltpu.CompilerParams(
            collective_id=0, has_side_effects=True, vmem_limit_bytes=56 * 1024 * 1024
        ),
    )(probes, legendre, orders, index, count, base, coef, weight)


def exact(a, b, dims):
    return lax.dot_general(a, b, (dims, ((), ())), precision=HIGHEST, preferred_element_type=F32)


NN = ((1,), (0,))


def three(a, b, product):
    a_hi, a_lo = split(a)
    b_hi, b_lo = split(b)
    return product(a_hi, b_hi) + product(a_hi, b_lo) + product(a_lo, b_hi)


def factorize(gram, upper_ref, inv_ref):
    n = gram.shape[0]
    row = lax.broadcasted_iota(jnp.int32, (n, n), 0)
    col = lax.broadcasted_iota(jnp.int32, (n, n), 1)
    eye = jnp.where(row == col, 1.0, 0.0)
    half = jnp.where(row > col, 1.0, 0.5 * eye)
    diag = jnp.where(row == col, gram, 0.0)
    r_col = lax.rsqrt(jnp.sum(diag, axis=1, keepdims=True))
    r_row = lax.rsqrt(jnp.sum(diag, axis=0, keepdims=True))
    inverse = (eye - half * (gram * r_col * r_row - eye)) * r_row
    upper = three(inverse, gram, mm)
    error = eye
    for _ in range(3):
        error = three(upper, inverse, mm_nt) - eye
        step = three(half * error, jnp.concatenate([inverse, upper], axis=1), mm)
        inverse = inverse - step[:, :n]
        upper = upper - step[:, n:]
    inv_ref[...] = inverse
    upper_ref[...] = jnp.where(row <= col, upper, 0.0)
    failed = jnp.max(jnp.where(jnp.abs(error) < 1e-4, 0.0, 1.0))

    @pl.when(failed > 0.5)
    def _():
        def column(j, state):
            left, full, inv = state
            at_row, at_col = row == j, col == j
            line = jnp.sum(jnp.where(at_row, left, 0.0), axis=0, keepdims=True)
            down = jnp.sum(jnp.where(at_col, left, 0.0), axis=1, keepdims=True)
            pivot = jnp.sum(jnp.where(at_row & at_col, left, 0.0), keepdims=True)
            scale = 1.0 / jnp.sqrt(pivot)
            line = jnp.where(col[:1] >= j, line * scale, 0.0)
            below = jnp.where(row[:, :1] > j, down * scale, 0.0)
            inv_line = jnp.sum(jnp.where(at_row, inv, 0.0), axis=0, keepdims=True) * scale
            inv = jnp.where(at_row, inv_line, inv - below * inv_line)
            return left - below * line, jnp.where(at_row, line, full), inv

        _, full, inv = lax.fori_loop(0, n, column, (gram, jnp.zeros_like(gram), eye))
        upper_ref[...] = full
        inv_ref[...] = inv


def panel_kernel(
    gram_ref, rows_ref, leg_ref, out_ref, upper_ref, inv_ref, rows, leg, block, rows_sem, leg_sem, out_sem
):
    fetch_rows = pltpu.make_async_copy(rows_ref, rows, rows_sem)
    fetch_rows.start()
    fetch_leg = [pltpu.make_async_copy(leg_ref.at[j], leg.at[j], leg_sem.at[j]) for j in range(OWN)]
    for copy in fetch_leg:
        copy.start()
    factorize(gram_ref[...].reshape(128, 128), upper_ref, inv_ref)
    hi, lo = split(inv_ref[...])
    left = lax.broadcasted_iota(jnp.int32, (128, 128), 1) < 64
    fetch_rows.wait()
    every = jnp.concatenate([rows[j] for j in range(OWN)], axis=1)
    z_hi, z_lo = split(mm(hi, every) + mm(lo, every))
    writes = []
    for j in range(OWN):
        cols = slice(j * 128, (j + 1) * 128)
        hi_f, lo_f = z_hi[:, cols].astype(F32), z_lo[:, cols].astype(F32)
        cosine = jnp.where(left, hi_f, pltpu.roll(lo_f, 64, axis=1))
        sine = jnp.where(left, pltpu.roll(hi_f, 64, axis=1), lo_f)
        weights = jnp.concatenate([cosine, sine], axis=0).astype(BF)
        fetch_leg[j].wait()
        for start, stop in ((0, 608), (608, NDEG)):
            both = mm_nt(leg[j, start:stop, :], weights)
            block[0, j, start:stop, :] = both[:, :128]
            block[1, j, start:stop, :] = both[:, 128:]
        for half in range(2):
            write = pltpu.make_async_copy(block.at[half, j], out_ref.at[half, j], out_sem.at[half, j])
            write.start()
            writes.append(write)
    for write in writes:
        write.wait()


def panel_stage(gram, rows, turned):
    any_space = pl.BlockSpec(memory_space=pl.ANY)
    return pl.pallas_call(
        panel_kernel,
        name="panel_stage",
        out_shape=(
            jax.ShapeDtypeStruct((2, OWN, NDEG, 128), F32),
            jax.ShapeDtypeStruct((128, 128), F32),
        ),
        in_specs=[VM, any_space, any_space],
        out_specs=(any_space, VM),
        scratch_shapes=[
            pltpu.VMEM((128, 128), F32),
            pltpu.VMEM(rows.shape, BF),
            pltpu.VMEM(turned.shape, BF),
            pltpu.VMEM((2, OWN, NDEG, 128), F32),
            pltpu.SemaphoreType.DMA,
            pltpu.SemaphoreType.DMA((OWN,)),
            pltpu.SemaphoreType.DMA((2, OWN)),
        ],
    )(gram, rows, turned)


def on_device(
    probes, legendre, order_map, tile_index, tile_count, base_offset, stencil_weight, obs_weight
):
    rows, gram, turned = front_stage(
        probes, legendre, order_map.reshape(OWN, 128), tile_index[0], tile_count,
        base_offset[0, 0], stencil_weight[0, 0], obs_weight[0, 0],
    )
    panel, upper = panel_stage(gram, rows, turned)
    return (jnp.swapaxes(panel, 2, 3), upper)


def solution(mesh):
    return jax.shard_map(
        on_device,
        mesh=mesh,
        in_specs=(
            P(None, "coef", "track", None),
            P("coef", None, None),
            P(),
            P("coef", None, None),
            P("coef", None),
            P("coef", "track", None, None),
            P("coef", "track", None, None, None),
            P("coef", "track", None, None),
        ),
        out_specs=(P(None, ("coef", "track"), None, None), P()),
        check_vma=False,
    )
```

```python
import math

import jax
import jax.numpy as jnp
from jax import lax
from jax.experimental import pallas as pl
from jax.experimental.pallas import tpu as pltpu
from jax.sharding import PartitionSpec as P

NDEG = 1200
ORDERS = 640
NLON = 1280
NC = 8
NT = 16
ND = NC * NT
OWN = 5
UNITS = 40
PIECE = 3
EARLY = 2
GROUP = 32
STEP = 20
CHUNKS = 4

BF = jnp.bfloat16
F32 = jnp.float32
HIGHEST = lax.Precision.HIGHEST
MESH = pl.DeviceIdType.MESH
VM = pl.BlockSpec(memory_space=pltpu.VMEM)


def mm(a, b):
    return lax.dot_general(a, b, (((1,), (0,)), ((), ())), preferred_element_type=F32)


def mm_nt(a, b):
    return lax.dot_general(a, b, (((1,), (1,)), ((), ())), preferred_element_type=F32)


def split(x):
    hi = x.astype(BF)
    return hi, (x - hi.astype(F32)).astype(BF)


def front_kernel(
    probes_ref, leg_ref, order_ref, index_ref, count_ref, base_ref, coef_ref, weight_ref,
    rows_out, gram_out, turned_out,
    leg, prob, base, coef, weight, live, hist, norm, part, table, lat_rows, lat_pack, lat_send, lat_recv,
    cos_q, sin_q, cos_b, sin_b, tab_hi, tab_lo, adj_ref, spec_ref, turn_ref, spec, recv, perm, normal,
    g_part, g_group, g_all, turned_leg, in_sem, leg_sem, prob_sem, turn_sem, comm, ready,
):
    c = lax.axis_index("coef")
    t = lax.axis_index("track")
    me = c * NT + t

    def send(src, dst, k, pc, pt):
        pltpu.make_async_remote_copy(
            src, dst, comm.at[2 * k], comm.at[2 * k + 1], device_id=(pc, pt), device_id_type=MESH
        ).start()

    def arrived(ref, n, k):
        pltpu.make_async_copy(ref.at[pl.ds(0, n)], ref.at[pl.ds(0, n)], comm.at[2 * k + 1]).wait()

    def sent(ref, n, k):
        pltpu.make_async_copy(ref.at[pl.ds(0, n)], ref.at[pl.ds(0, n)], comm.at[2 * k]).wait()

    z, core = lax.div(c, 2), lax.rem(c, 2)
    y_chip, x_chip = lax.div(t, 4), lax.rem(t, 4)
    far = (0, 1, 2, 1)
    bands = {(dz, dk): lax.rem(z + dz, 4) * 2 + lax.rem(core + dk, 2) for dz in range(4) for dk in range(2)}
    tracks = {(dy, dx): lax.rem(y_chip + dy, 4) * 4 + lax.rem(x_chip + dx, 4) for dy in range(4) for dx in range(4)}
    steps = [(dz, dk, dy, dx) for dz in range(4) for dk in range(2) for dy in range(4) for dx in range(4)]
    steps.sort(key=lambda d: -(far[d[0]] + far[d[2]] + far[d[3]]) * 2 - d[1])
    peers = [(bands[d[:2]], tracks[d[2:]]) for d in steps if any(d)]

    small = [
        pltpu.make_async_copy(src, dst, in_sem.at[k])
        for k, (src, dst) in enumerate(((base_ref, base), (coef_ref, coef), (weight_ref, weight)))
    ]
    for copy in small:
        copy.start()

    def fetch(k):
        orders = pl.ds(k * STEP, STEP)
        return (
            pltpu.make_async_copy(leg_ref.at[orders], leg.at[orders], leg_sem.at[k]),
            pltpu.make_async_copy(probes_ref.at[:, orders], prob.at[:, orders], prob_sem.at[k]),
        )

    barrier = pltpu.get_barrier_semaphore()

    for i in range(1, NC):
        pl.semaphore_signal(barrier, 1, device_id=(lax.rem(c + i, NC), t), device_id_type=MESH)
    for i in range(1, NT):
        pl.semaphore_signal(barrier, 1, device_id=(c, lax.rem(t + i, NT)), device_id_type=MESH)

    orders = jnp.concatenate([order_ref[r : r + 1, :] for r in range(OWN)], axis=1)
    coarse = jnp.broadcast_to(lax.shift_right_logical(orders, 5).astype(F32).astype(BF), (128, ORDERS))
    fine = jnp.broadcast_to((orders & 31).astype(F32).astype(BF), (128, ORDERS))
    owner_row = lax.broadcasted_iota(jnp.int32, (128, ORDERS), 0) * OWN
    slot_lane = lax.broadcasted_iota(jnp.int32, (128, ORDERS), 1)
    lane = lax.broadcasted_iota(jnp.int32, (128, 128), 1).astype(F32)

    def trig(j, carry):
        hot = jnp.where(owner_row + j == slot_lane, 1.0, 0.0).astype(BF)
        order = 32.0 * mm_nt(hot, coarse) + mm_nt(hot, fine)
        cos_q[j], sin_q[j] = circle(order * lane)
        cosine, sine = circle(order * (lane * 128.0))
        cos_b[j] = cosine * (1.0 / math.sqrt(ORDERS))
        sin_b[j] = sine * (1.0 / math.sqrt(ORDERS))
        return carry

    lax.fori_loop(0, EARLY, trig, 0)

    for copy in small:
        copy.wait()
    for k in range(CHUNKS):
        for copy in fetch(k):
            copy.start()
    slots, obs = base.shape
    lane16 = lax.broadcasted_iota(jnp.int32, (1, NT), 1)
    count = jnp.sum(jnp.where(lane16 == t, count_ref[...].astype(F32), 0.0), axis=1, keepdims=True)
    slot_id = lax.broadcasted_iota(jnp.int32, (slots, obs), 0).astype(F32)
    live[...] = jnp.where(slot_id < count, weight[...], 0.0)
    points = lax.broadcasted_iota(jnp.int32, (128, obs), 0)

    def slot(group, carry):
        for u in range(4):
            s = group * 4 + u
            hot = jnp.where(points == base[pl.ds(s, 1), :], 1.0, 0.0).astype(BF)
            four = coef[s].astype(F32)
            eight = jnp.concatenate([four, jnp.zeros_like(four)], axis=0)
            scaled = eight * live[pl.ds(s, 1), :]
            full = jnp.concatenate(
                [scaled * eight] + [scaled * pltpu.roll(eight, 8 - d, axis=0) for d in range(1, 4)], axis=0
            )
            hi, mid = split(full)
            low = (full - hi.astype(F32) - mid.astype(F32)).astype(BF)
            sums = mm_nt(jnp.concatenate([hi, mid, low], axis=0), hot)
            hist[s] = sums[:32] + sums[32:64] + sums[64:]
        return carry

    lax.fori_loop(0, slots // 4, slot, 0)
    diagonals = []
    for d in range(4):
        total = hist[:, 8 * d, :]
        for i in range(1, 4 - d):
            total = total + pltpu.roll(hist[:, 8 * d + i, :], i, axis=1)
        diagonals.append(total)
    rows = lax.broadcasted_iota(jnp.int32, (80, slots), 0)
    tile = (rows & 7) * 10 + lax.shift_right_logical(rows, 3)
    pick = jnp.where(tile == index_ref[pl.ds(t, 1), :], 1.0, 0.0)
    summed = exact(pick, jnp.concatenate(diagonals, axis=1), NN)
    for u in range(NT * PIECE):
        if u < UNITS:
            b, d = u // 4, u % 4
            block = summed[b * 8 : (b + 1) * 8, d * 128 : (d + 1) * 128]
        else:
            block = jnp.zeros((8, 128), F32)
        norm[u // PIECE, u % PIECE] = block
    pl.semaphore_wait(barrier, NC + NT - 2)
    for i in range(1, NT):
        pl.semaphore_signal(ready, 1, device_id=(c, lax.rem(t + i, NT)), device_id_type=MESH)
    for i in range(1, NT):
        peer = (t + i) % NT
        send(norm.at[peer], part.at[t], 0, c, peer)
    part[t] = norm[t]

    def lat_step(k, carry):
        for copy in fetch(k):
            copy.wait()
        for u in range(STEP):
            order = k * STEP + u
            both = mm_nt(prob[:, order].reshape(16, NDEG), leg[order])
            owner = order // OWN
            row = ((order - owner * OWN) * NT + owner) * 8
            lat_rows[pl.ds(pl.multiple_of(row, 8), 8), :] = jnp.concatenate([both[:8], both[8:]], axis=1)
        return carry

    lax.fori_loop(0, CHUNKS, lat_step, 0)
    lanes = lax.broadcasted_iota(jnp.int32, (64, 128), 1)
    slot16 = lax.shift_right_logical(lanes, 4)
    rest = [jnp.zeros((64, 128), F32)] * 2
    for p in range(8):
        some = jnp.concatenate([lat_rows[pl.ds(p, 80, stride=8), :], jnp.zeros((48, 128), F32)], axis=0).T
        cosine, sine = some[:64], some[64:]
        main = jnp.where(lanes < 64, cosine, pltpu.roll(sine, 64, axis=1))
        g = p // 2
        rest[p % 2] = jnp.where(slot16 == 2 * g, pltpu.roll(cosine, (32 * g + 64) % 128, axis=1), rest[p % 2])
        rest[p % 2] = jnp.where(slot16 == 2 * g + 1, pltpu.roll(sine, (32 * g + 80) % 128, axis=1), rest[p % 2])
        for s in range(NC):
            lat_pack[s, p * 8 : (p + 1) * 8, :] = main[s * 8 : (s + 1) * 8, :]
    for k in range(2):
        for s in range(NC):
            lat_pack[s, 64 + k * 8 : 72 + k * 8, :] = rest[k][s * 8 : (s + 1) * 8, :]
    lat_send[...] = lat_pack[...].astype(BF)
    for i in range(1, NC):
        peer = (c + i) % NC
        send(lat_send.at[peer], lat_recv.at[c], 1, peer, t)
    lat_recv[c] = lat_send[c]
    arrived(part, NT - 1, 0)
    total = part[0]
    for s in range(1, NT):
        total = total + part[s]
    table[t] = total
    for i in range(1, NT):
        peer = (t + i) % NT
        send(table.at[t], table.at[t], 2, c, peer)

    def make(j, carry):
        cq, sq, cb, sb = cos_q[j], sin_q[j], cos_b[j], sin_b[j]
        for b in range(10):
            ca, sa = cb[:, b : b + 1], sb[:, b : b + 1]
            cols = slice(b * 128, (b + 1) * 128)
            hi, lo = split(ca * cq - sa * sq)
            tab_hi[j, :, cols] = hi
            tab_lo[j, :, cols] = lo
            hi, lo = split(sa * cq + ca * sq)
            tab_hi[OWN + j, :, cols] = hi
            tab_lo[OWN + j, :, cols] = lo
        return carry

    lax.fori_loop(EARLY, OWN, lambda j, carry: make(j, trig(j, carry)), 0)
    lax.fori_loop(0, EARLY, make, 0)

    arrived(lat_recv, NC - 1, 1)
    slot32 = lax.shift_right_logical(lax.broadcasted_iota(jnp.int32, (16, 128), 1), 5)
    tail = []
    for first in (0, 4):
        parts = [jnp.zeros((16, 128), F32)] * 4
        for k in range(4):
            some = lat_recv[first + k, 64:, :].astype(F32)
            for g in range(4):
                moved = pltpu.roll(some, (32 * (k - g)) % 128, axis=1) if k != g else some
                parts[g] = jnp.where(slot32 == k, moved, parts[g])
        tail.append(jnp.concatenate(parts, axis=0).astype(BF))

    def rows_of(tab, s):
        own = slice(s * NT, (s + 1) * NT)
        return [tab[0:4, own, :].reshape(64, NLON), tab[OWN : OWN + 4, own, :].reshape(64, NLON)]

    def rest_of(tab, s):
        own = slice(s * NT, (s + 1) * NT)
        return [tab[4, own, :], tab[OWN + 4, own, :]]

    grid = jnp.zeros((64, NLON), F32)
    for tab in (tab_hi, tab_lo):
        for s in range(0, NC, 2):
            pair = jnp.concatenate([lat_recv[s, :64, :], lat_recv[s + 1, :64, :]], axis=1)
            grid = grid + mm(pair, jnp.concatenate(rows_of(tab, s) + rows_of(tab, s + 1), axis=0))
        rest_rows = [block for s in range(NC) for block in rest_of(tab, s)]
        grid = grid + mm(jnp.concatenate(tail, axis=1), jnp.concatenate(rest_rows, axis=0))
    arrived(table, NT - 1, 2)
    for b in range(10):
        x = grid[:, b * 128 : (b + 1) * 128]

        def diagonal(d):
            unit = b * 4 + d
            block = table[unit // PIECE, unit % PIECE]
            return jnp.broadcast_to(block[None], (8, 8, 128)).reshape(64, 128)

        adj = diagonal(0) * x
        for d in range(1, 4):
            m = diagonal(d)
            adj = adj + m * pltpu.roll(x, 128 - d, axis=1) + pltpu.roll(m * x, d, axis=1)
        hi, lo = split(adj)
        adj_ref[:64, b * 128 : (b + 1) * 128] = hi
        adj_ref[64:, b * 128 : (b + 1) * 128] = lo
    for i in range(10):
        both = mm_nt(adj_ref[...], tab_hi[i])
        spec_ref[i] = both[:64] + both[64:] + mm_nt(adj_ref[:64, :], tab_lo[i])
    spec_ref[10:] = jnp.zeros((6, 64, 128), F32)
    for p in range(8):
        block = spec_ref[:, p * 8 : (p + 1) * 8, :].reshape(128, 128)
        turn_ref[pl.ds(p, 128, stride=8), :] = block.T
    spec[...] = turn_ref[...].reshape(128, 8, 128).astype(BF)

    pl.semaphore_wait(ready, NT - 1)
    for pc, pt in peers:
        send(spec.at[pc * NT + pt], recv.at[me], 3, pc, pt)
    recv[me] = spec[me]

    same = (lax.broadcasted_iota(jnp.int32, (128, 128), 0) < 64) == (
        lax.broadcasted_iota(jnp.int32, (128, 128), 1) < 64
    )
    for j in range(OWN):
        one = leg[t * OWN + j]
        two = jnp.concatenate([one, one], axis=0)
        hi, lo = split(jnp.where(same, mm_nt(two, two), 0.0))
        normal[0, j] = hi
        normal[1, j] = lo
    row = lax.broadcasted_iota(jnp.int32, (128, 640), 0)
    col = lax.broadcasted_iota(jnp.int32, (128, 640), 1)
    src_i, src_a = lax.shift_right_logical(row, 3), row & 7
    dst_i = (lax.shift_right_logical(col, 6) & 1) * OWN + lax.shift_right_logical(col, 7)
    dst_band, dst_a = lax.shift_right_logical(col, 3) & 7, col & 7
    hit = (src_a == dst_a) & (src_i == dst_i)
    for s in range(NC):
        perm[s * 128 : (s + 1) * 128, :] = jnp.where(hit & (dst_band == s), 1.0, 0.0).astype(BF)
    arrived(recv, ND - 1, 3)
    gathered = jnp.zeros((128, 640), F32)
    for s in range(NC):
        block = recv[s * NT : (s + 1) * NT].astype(F32).reshape(128, 128).astype(BF)
        gathered = gathered + mm(block, perm[s * 128 : (s + 1) * 128, :])
    gram = jnp.zeros((128, 128), F32)
    for j in range(OWN):
        mine = gathered[:, j * 128 : (j + 1) * 128].astype(BF)
        rows_out[j] = mine
        hi, lo = split(mm(mine, normal[0, j]) + mm(mine, normal[1, j]))
        gram = gram + mm_nt(hi, mine) + mm_nt(lo, mine)
    for k in range(GROUP):
        g_part[k] = gram[k * 4 : (k + 1) * 4, :]

    def turn(j):
        one = leg[t * OWN + j]
        turned_leg[j] = jnp.concatenate([one, one], axis=0).T
        pltpu.make_async_copy(turned_leg.at[j], turned_out.at[j], turn_sem.at[j]).start()

    seat = c * 4 + x_chip
    for d in steps:
        if d[2] == 0 and any(d):
            pc, px = bands[d[:2]], lax.rem(x_chip + d[3], 4)
            send(g_part.at[pc * 4 + px], g_group.at[seat], 4, pc, y_chip * 4 + px)
    g_group[seat] = g_part[seat]
    turn(0)
    turn(1)
    arrived(g_group, GROUP - 1, 4)
    total = g_group[0]
    for k in range(1, GROUP):
        total = total + g_group[k]
    mine_at = y_chip * GROUP + seat
    g_all[mine_at] = total * (1.0 / (2 * ORDERS * NDEG))
    for pc, pt in peers:
        send(g_all.at[mine_at], g_all.at[mine_at], 5, pc, pt)
    turn(2)
    turn(3)
    turn(4)
    arrived(g_all, ND - 1, 5)
    for k in range(GROUP):
        total = g_all[k]
        for q in range(1, 4):
            total = total + g_all[q * GROUP + k]
        gram_out[k * 4 : (k + 1) * 4, :] = total
    for j in range(OWN):
        pltpu.make_async_copy(turned_leg.at[j], turned_out.at[j], turn_sem.at[j]).wait()
    for ref, n, k in (
        (part, NT - 1, 0), (lat_send, NC - 1, 1), (table, NT - 1, 2), (spec, ND - 1, 3),
        (g_part, GROUP - 1, 4), (g_all, ND - 1, 5),
    ):
        sent(ref, n, k)


def circle(x):
    quarter = jnp.floor(x * (1.0 / 320.0) + 0.5)
    y = (x - quarter * 320.0) * (2.0 * math.pi / NLON)
    turn = quarter - 4.0 * jnp.floor(quarter * 0.25)
    z = y * y
    sine = y * (1.0 + z * (-1.0 / 6 + z * (1.0 / 120 + z * (-1.0 / 5040 + z * (1.0 / 362880)))))
    cosine = 1.0 + z * (-0.5 + z * (1.0 / 24 + z * (-1.0 / 720 + z * (1.0 / 40320 - z * (1.0 / 3628800)))))
    odd = (turn == 1.0) | (turn == 3.0)
    cos_x = jnp.where(odd, sine, cosine)
    sin_x = jnp.where(odd, cosine, sine)
    cos_x = jnp.where((turn == 1.0) | (turn == 2.0), -cos_x, cos_x)
    sin_x = jnp.where(turn >= 2.0, -sin_x, sin_x)
    return cos_x, sin_x


def front_stage(probes, legendre, orders, index, count, base, coef, weight):
    slots, obs = base.shape
    vm = pltpu.VMEM
    any_space = pl.BlockSpec(memory_space=pl.ANY)
    return pl.pallas_call(
        front_kernel,
        name="front_stage",
        out_shape=(jax.ShapeDtypeStruct((OWN, 128, 128), BF), jax.ShapeDtypeStruct((128, 128), F32),
                   jax.ShapeDtypeStruct((OWN, NDEG, 128), BF)),
        in_specs=[any_space, any_space, VM, VM, VM, any_space, any_space, any_space],
        out_specs=(VM, VM, any_space),
        scratch_shapes=[
            vm(legendre.shape, BF), vm(probes.shape, BF),
            vm(base.shape, jnp.int32), vm(coef.shape, BF), vm(weight.shape, F32), vm(weight.shape, F32),
            vm((slots, 32, 128), F32),
            vm((NT, PIECE, 8, 128), F32), vm((NT, PIECE, 8, 128), F32), vm((NT, PIECE, 8, 128), F32),
            vm((640, 128), F32),
            vm((NC, 80, 128), F32), vm((NC, 80, 128), BF), vm((NC, 80, 128), BF),
            vm((OWN, 128, 128), F32), vm((OWN, 128, 128), F32), vm((OWN, 128, 128), F32), vm((OWN, 128, 128), F32),
            vm((10, 128, NLON), BF), vm((10, 128, NLON), BF),
            vm((128, NLON), BF), vm((16, 64, 128), F32), vm((1024, 128), F32),
            vm((ND, 8, 128), BF), vm((ND, 8, 128), BF), vm((1024, 640), BF), vm((2, OWN, 128, 128), BF),
            vm((GROUP, 4, 128), F32), vm((GROUP, 4, 128), F32), vm((ND, 4, 128), F32),
            vm((OWN, NDEG, 128), BF),
            pltpu.SemaphoreType.DMA((3,)), pltpu.SemaphoreType.DMA((CHUNKS,)),
            pltpu.SemaphoreType.DMA((CHUNKS,)), pltpu.SemaphoreType.DMA((OWN,)), pltpu.SemaphoreType.DMA((12,)),
            pltpu.SemaphoreType.REGULAR,
        ],
        compiler_params=pltpu.CompilerParams(
            collective_id=0, has_side_effects=True, vmem_limit_bytes=56 * 1024 * 1024
        ),
    )(probes, legendre, orders, index, count, base, coef, weight)


def exact(a, b, dims):
    return lax.dot_general(a, b, (dims, ((), ())), precision=HIGHEST, preferred_element_type=F32)


NN = ((1,), (0,))


def three(a, b, product):
    a_hi, a_lo = split(a)
    b_hi, b_lo = split(b)
    return product(a_hi, b_hi) + product(a_hi, b_lo) + product(a_lo, b_hi)


def factorize(gram, upper_ref, inv_ref):
    n = gram.shape[0]
    row = lax.broadcasted_iota(jnp.int32, (n, n), 0)
    col = lax.broadcasted_iota(jnp.int32, (n, n), 1)
    eye = jnp.where(row == col, 1.0, 0.0)
    half = jnp.where(row > col, 1.0, 0.5 * eye)
    diag = jnp.where(row == col, gram, 0.0)
    r_col = lax.rsqrt(jnp.sum(diag, axis=1, keepdims=True))
    r_row = lax.rsqrt(jnp.sum(diag, axis=0, keepdims=True))
    inverse = (eye - half * (gram * r_col * r_row - eye)) * r_row
    upper = three(inverse, gram, mm)
    error = eye
    for _ in range(3):
        error = three(upper, inverse, mm_nt) - eye
        step = three(half * error, jnp.concatenate([inverse, upper], axis=1), mm)
        inverse = inverse - step[:, :n]
        upper = upper - step[:, n:]
    inv_ref[...] = inverse
    upper_ref[...] = jnp.where(row <= col, upper, 0.0)
    failed = jnp.max(jnp.where(jnp.abs(error) < 1e-4, 0.0, 1.0))

    @pl.when(failed > 0.5)
    def _():
        def column(j, state):
            left, full, inv = state
            at_row, at_col = row == j, col == j
            line = jnp.sum(jnp.where(at_row, left, 0.0), axis=0, keepdims=True)
            down = jnp.sum(jnp.where(at_col, left, 0.0), axis=1, keepdims=True)
            pivot = jnp.sum(jnp.where(at_row & at_col, left, 0.0), keepdims=True)
            scale = 1.0 / jnp.sqrt(pivot)
            line = jnp.where(col[:1] >= j, line * scale, 0.0)
            below = jnp.where(row[:, :1] > j, down * scale, 0.0)
            inv_line = jnp.sum(jnp.where(at_row, inv, 0.0), axis=0, keepdims=True) * scale
            inv = jnp.where(at_row, inv_line, inv - below * inv_line)
            return left - below * line, jnp.where(at_row, line, full), inv

        _, full, inv = lax.fori_loop(0, n, column, (gram, jnp.zeros_like(gram), eye))
        upper_ref[...] = full
        inv_ref[...] = inv


def panel_kernel(
    gram_ref, rows_ref, leg_ref, out_ref, upper_ref, inv_ref, rows, leg, block, rows_sem, leg_sem, out_sem
):
    fetch_rows = pltpu.make_async_copy(rows_ref, rows, rows_sem)
    fetch_rows.start()
    fetch_leg = [pltpu.make_async_copy(leg_ref.at[j], leg.at[j], leg_sem.at[j]) for j in range(OWN)]
    for copy in fetch_leg:
        copy.start()
    factorize(gram_ref[...], upper_ref, inv_ref)
    hi, lo = split(inv_ref[...])
    left = lax.broadcasted_iota(jnp.int32, (128, 128), 1) < 64
    fetch_rows.wait()
    every = jnp.concatenate([rows[j] for j in range(OWN)], axis=1)
    z_hi, z_lo = split(mm(hi, every) + mm(lo, every))
    writes = []
    for j in range(OWN):
        cols = slice(j * 128, (j + 1) * 128)
        hi_f, lo_f = z_hi[:, cols].astype(F32), z_lo[:, cols].astype(F32)
        cosine = jnp.where(left, hi_f, pltpu.roll(lo_f, 64, axis=1))
        sine = jnp.where(left, pltpu.roll(hi_f, 64, axis=1), lo_f)
        weights = jnp.concatenate([cosine, sine], axis=0).astype(BF)
        fetch_leg[j].wait()
        for start, stop in ((0, 608), (608, NDEG)):
            both = mm_nt(leg[j, start:stop, :], weights)
            block[0, j, start:stop, :] = both[:, :128]
            block[1, j, start:stop, :] = both[:, 128:]
        for half in range(2):
            write = pltpu.make_async_copy(block.at[half, j], out_ref.at[half, j], out_sem.at[half, j])
            write.start()
            writes.append(write)
    for write in writes:
        write.wait()


def panel_stage(gram, rows, turned):
    any_space = pl.BlockSpec(memory_space=pl.ANY)
    return pl.pallas_call(
        panel_kernel,
        name="panel_stage",
        out_shape=(
            jax.ShapeDtypeStruct((2, OWN, NDEG, 128), F32),
            jax.ShapeDtypeStruct((128, 128), F32),
        ),
        in_specs=[VM, any_space, any_space],
        out_specs=(any_space, VM),
        scratch_shapes=[
            pltpu.VMEM((128, 128), F32),
            pltpu.VMEM(rows.shape, BF),
            pltpu.VMEM(turned.shape, BF),
            pltpu.VMEM((2, OWN, NDEG, 128), F32),
            pltpu.SemaphoreType.DMA,
            pltpu.SemaphoreType.DMA((OWN,)),
            pltpu.SemaphoreType.DMA((2, OWN)),
        ],
    )(gram, rows, turned)


def on_device(
    probes, legendre, order_map, tile_index, tile_count, base_offset, stencil_weight, obs_weight
):
    rows, gram, turned = front_stage(
        probes, legendre, order_map.reshape(OWN, 128), tile_index[0], tile_count,
        base_offset[0, 0], stencil_weight[0, 0], obs_weight[0, 0],
    )
    panel, upper = panel_stage(gram, rows, turned)
    return (jnp.swapaxes(panel, 2, 3), upper)


def solution(mesh):
    return jax.shard_map(
        on_device,
        mesh=mesh,
        in_specs=(
            P(None, "coef", "track", None),
            P("coef", None, None),
            P(),
            P("coef", None, None),
            P("coef", None),
            P("coef", "track", None, None),
            P("coef", "track", None, None, None),
            P("coef", "track", None, None),
        ),
        out_specs=(P(None, ("coef", "track"), None, None), P()),
        check_vma=False,
    )
```

```python
import math

import jax
import jax.numpy as jnp
from jax import lax
from jax.experimental import pallas as pl
from jax.experimental.pallas import tpu as pltpu
from jax.sharding import PartitionSpec as P

NDEG = 1200
ORDERS = 640
NLON = 1280
NC = 8
NT = 16
ND = NC * NT
OWN = 5
UNITS = 40
PIECE = 3
GROUP = 32
STEP = 20
CHUNKS = 4

BF = jnp.bfloat16
F32 = jnp.float32
HIGHEST = lax.Precision.HIGHEST
MESH = pl.DeviceIdType.MESH
VM = pl.BlockSpec(memory_space=pltpu.VMEM)


def mm(a, b):
    return lax.dot_general(a, b, (((1,), (0,)), ((), ())), preferred_element_type=F32)


def mm_nt(a, b):
    return lax.dot_general(a, b, (((1,), (1,)), ((), ())), preferred_element_type=F32)


def split(x):
    hi = x.astype(BF)
    return hi, (x - hi.astype(F32)).astype(BF)


def front_kernel(
    probes_ref, leg_ref, order_ref, index_ref, count_ref, base_ref, coef_ref, weight_ref,
    rows_out, gram_out, turned_out,
    leg, prob, base, coef, weight, order_map, tile_index, tile_count, rows, live, hist, norm, part, table, lat_rows, lat_pack, lat_send, lat_recv,
    cos_q, sin_q, cos_b, sin_b, tab_hi, tab_lo, adj_ref, spec_ref, turn_ref, spec, recv, perm, normal,
    g_part, g_group, g_all, turned_leg, in_sem, leg_sem, prob_sem, turn_sem, comm, ready,
):
    c = lax.axis_index("coef")
    t = lax.axis_index("track")
    me = c * NT + t

    def send(src, dst, k, pc, pt):
        pltpu.make_async_remote_copy(
            src, dst, comm.at[2 * k], comm.at[2 * k + 1], device_id=(pc, pt), device_id_type=MESH
        ).start()

    def arrived(ref, n, k):
        pltpu.make_async_copy(ref.at[pl.ds(0, n)], ref.at[pl.ds(0, n)], comm.at[2 * k + 1]).wait()

    def sent(ref, n, k):
        pltpu.make_async_copy(ref.at[pl.ds(0, n)], ref.at[pl.ds(0, n)], comm.at[2 * k]).wait()

    z, core = lax.div(c, 2), lax.rem(c, 2)
    y_chip, x_chip = lax.div(t, 4), lax.rem(t, 4)
    far = (0, 1, 2, 1)
    bands = {(dz, dk): lax.rem(z + dz, 4) * 2 + lax.rem(core + dk, 2) for dz in range(4) for dk in range(2)}
    tracks = {(dy, dx): lax.rem(y_chip + dy, 4) * 4 + lax.rem(x_chip + dx, 4) for dy in range(4) for dx in range(4)}
    steps = [(dz, dk, dy, dx) for dz in range(4) for dk in range(2) for dy in range(4) for dx in range(4)]
    steps.sort(key=lambda d: -(far[d[0]] + far[d[2]] + far[d[3]]) * 2 - d[1])
    peers = [(bands[d[:2]], tracks[d[2:]]) for d in steps if any(d)]

    small = [
        pltpu.make_async_copy(src, dst, in_sem.at[k])
        for k, (src, dst) in enumerate(
            (
                (base_ref, base), (coef_ref, coef), (weight_ref, weight),
                (order_ref, order_map), (index_ref, tile_index), (count_ref, tile_count),
            )
        )
    ]
    for copy in small:
        copy.start()

    def fetch(k):
        orders = pl.ds(k * STEP, STEP)
        return (
            pltpu.make_async_copy(leg_ref.at[orders], leg.at[orders], leg_sem.at[k]),
            pltpu.make_async_copy(probes_ref.at[:, orders], prob.at[:, orders], prob_sem.at[k]),
        )

    barrier = pltpu.get_barrier_semaphore()

    for i in range(1, NC):
        pl.semaphore_signal(barrier, 1, device_id=(lax.rem(c + i, NC), t), device_id_type=MESH)
    for i in range(1, NT):
        pl.semaphore_signal(barrier, 1, device_id=(c, lax.rem(t + i, NT)), device_id_type=MESH)

    for copy in small:
        copy.wait()
    for k in range(CHUNKS):
        for copy in fetch(k):
            copy.start()
    slots, obs = base.shape
    lane16 = lax.broadcasted_iota(jnp.int32, (1, NT), 1)
    count = jnp.sum(jnp.where(lane16 == t, tile_count[...].astype(F32), 0.0), axis=1, keepdims=True)
    slot_id = lax.broadcasted_iota(jnp.int32, (slots, obs), 0).astype(F32)
    live[...] = jnp.where(slot_id < count, weight[...], 0.0)
    points = lax.broadcasted_iota(jnp.int32, (128, obs), 0)

    def slot(group, carry):
        for u in range(12):
            s = group * 12 + u
            hot = jnp.where(points == base[pl.ds(s, 1), :], 1.0, 0.0).astype(BF)
            four = coef[s].astype(F32)
            eight = jnp.concatenate([four, jnp.zeros_like(four)], axis=0)
            scaled = eight * live[pl.ds(s, 1), :]
            full = jnp.concatenate(
                [scaled * eight] + [scaled * pltpu.roll(eight, 8 - d, axis=0) for d in range(1, 4)], axis=0
            )
            hi, mid = split(full)
            low = (full - hi.astype(F32) - mid.astype(F32)).astype(BF)
            sums = mm_nt(jnp.concatenate([hi, mid, low], axis=0), hot)
            hist[s] = sums[:32] + sums[32:64] + sums[64:]
        return carry

    lax.fori_loop(0, slots // 12, slot, 0)
    diagonals = []
    for d in range(4):
        total = hist[:, 8 * d, :]
        for i in range(1, 4 - d):
            total = total + pltpu.roll(hist[:, 8 * d + i, :], i, axis=1)
        diagonals.append(total)
    unit = lax.broadcasted_iota(jnp.int32, (80, slots), 0)
    tile = (unit & 7) * 10 + lax.shift_right_logical(unit, 3)
    pick = jnp.where(tile == tile_index[pl.ds(t, 1), :], 1.0, 0.0)
    summed = exact(pick, jnp.concatenate(diagonals, axis=1), NN)
    for u in range(NT * PIECE):
        if u < UNITS:
            b, d = u // 4, u % 4
            block = summed[b * 8 : (b + 1) * 8, d * 128 : (d + 1) * 128]
        else:
            block = jnp.zeros((8, 128), F32)
        norm[u // PIECE, u % PIECE] = block
    pl.semaphore_wait(barrier, NC + NT - 2)
    for i in range(1, NT):
        pl.semaphore_signal(ready, 1, device_id=(c, lax.rem(t + i, NT)), device_id_type=MESH)
    for i in range(1, NT):
        peer = (t + i) % NT
        send(norm.at[peer], part.at[t], 0, c, peer)
    part[t] = norm[t]

    def lat_step(k, carry):
        for copy in fetch(k):
            copy.wait()
        for u in range(STEP):
            order = k * STEP + u
            both = mm_nt(prob[:, order].reshape(16, NDEG), leg[order])
            owner = order // OWN
            row = ((order - owner * OWN) * NT + owner) * 8
            lat_rows[pl.ds(pl.multiple_of(row, 8), 8), :] = jnp.concatenate([both[:8], both[8:]], axis=1)
        return carry

    lax.fori_loop(0, CHUNKS, lat_step, 0)
    lanes = lax.broadcasted_iota(jnp.int32, (64, 128), 1)
    slot16 = lax.shift_right_logical(lanes, 4)
    rest = [jnp.zeros((64, 128), F32)] * 2
    for p in range(8):
        some = jnp.concatenate([lat_rows[pl.ds(p, 80, stride=8), :], jnp.zeros((48, 128), F32)], axis=0).T
        cosine, sine = some[:64], some[64:]
        main = jnp.where(lanes < 64, cosine, pltpu.roll(sine, 64, axis=1))
        g = p // 2
        rest[p % 2] = jnp.where(slot16 == 2 * g, pltpu.roll(cosine, (32 * g + 64) % 128, axis=1), rest[p % 2])
        rest[p % 2] = jnp.where(slot16 == 2 * g + 1, pltpu.roll(sine, (32 * g + 80) % 128, axis=1), rest[p % 2])
        for s in range(NC):
            lat_pack[s, p * 8 : (p + 1) * 8, :] = main[s * 8 : (s + 1) * 8, :]
    for k in range(2):
        for s in range(NC):
            lat_pack[s, 64 + k * 8 : 72 + k * 8, :] = rest[k][s * 8 : (s + 1) * 8, :]
    lat_send[...] = lat_pack[...].astype(BF)
    for i in range(1, NC):
        peer = (c + i) % NC
        send(lat_send.at[peer], lat_recv.at[c], 1, peer, t)
    lat_recv[c] = lat_send[c]
    arrived(part, NT - 1, 0)
    total = part[0]
    for s in range(1, NT):
        total = total + part[s]
    table[t] = total
    for i in range(1, NT):
        peer = (t + i) % NT
        send(table.at[t], table.at[t], 2, c, peer)

    orders = jnp.concatenate([order_map[r : r + 1, :] for r in range(OWN)], axis=1)
    coarse = jnp.broadcast_to(lax.shift_right_logical(orders, 5).astype(F32).astype(BF), (128, ORDERS))
    fine = jnp.broadcast_to((orders & 31).astype(F32).astype(BF), (128, ORDERS))
    owner_row = lax.broadcasted_iota(jnp.int32, (128, ORDERS), 0) * OWN
    slot_lane = lax.broadcasted_iota(jnp.int32, (128, ORDERS), 1)
    lane = lax.broadcasted_iota(jnp.int32, (128, 128), 1).astype(F32)

    def trig(j, carry):
        hot = jnp.where(owner_row + j == slot_lane, 1.0, 0.0).astype(BF)
        order = 32.0 * mm_nt(hot, coarse) + mm_nt(hot, fine)
        cos_q[j], sin_q[j] = circle(order * lane)
        cosine, sine = circle(order * (lane * 128.0))
        cos_b[j] = cosine * (1.0 / math.sqrt(ORDERS))
        sin_b[j] = sine * (1.0 / math.sqrt(ORDERS))
        return carry

    def make(j, carry):
        cq, sq, cb, sb = cos_q[j], sin_q[j], cos_b[j], sin_b[j]
        for b in range(10):
            ca, sa = cb[:, b : b + 1], sb[:, b : b + 1]
            cols = slice(b * 128, (b + 1) * 128)
            hi, lo = split(ca * cq - sa * sq)
            tab_hi[j, :, cols] = hi
            tab_lo[j, :, cols] = lo
            hi, lo = split(sa * cq + ca * sq)
            tab_hi[OWN + j, :, cols] = hi
            tab_lo[OWN + j, :, cols] = lo
        return carry

    lax.fori_loop(0, OWN, lambda j, carry: make(j, trig(j, carry)), 0)

    arrived(lat_recv, NC - 1, 1)
    slot32 = lax.shift_right_logical(lax.broadcasted_iota(jnp.int32, (16, 128), 1), 5)
    tail = []
    for first in (0, 4):
        parts = [jnp.zeros((16, 128), F32)] * 4
        for k in range(4):
            some = lat_recv[first + k, 64:, :].astype(F32)
            for g in range(4):
                moved = pltpu.roll(some, (32 * (k - g)) % 128, axis=1) if k != g else some
                parts[g] = jnp.where(slot32 == k, moved, parts[g])
        tail.append(jnp.concatenate(parts, axis=0).astype(BF))

    def rows_of(tab, s):
        own = slice(s * NT, (s + 1) * NT)
        return [tab[0:4, own, :].reshape(64, NLON), tab[OWN : OWN + 4, own, :].reshape(64, NLON)]

    def rest_of(tab, s):
        own = slice(s * NT, (s + 1) * NT)
        return [tab[4, own, :], tab[OWN + 4, own, :]]

    grid = jnp.zeros((64, NLON), F32)
    for tab in (tab_hi, tab_lo):
        for s in range(0, NC, 2):
            pair = jnp.concatenate([lat_recv[s, :64, :], lat_recv[s + 1, :64, :]], axis=1)
            grid = grid + mm(pair, jnp.concatenate(rows_of(tab, s) + rows_of(tab, s + 1), axis=0))
        rest_rows = [block for s in range(NC) for block in rest_of(tab, s)]
        grid = grid + mm(jnp.concatenate(tail, axis=1), jnp.concatenate(rest_rows, axis=0))
    arrived(table, NT - 1, 2)
    for b in range(10):
        x = grid[:, b * 128 : (b + 1) * 128]

        def diagonal(d):
            unit = b * 4 + d
            block = table[unit // PIECE, unit % PIECE]
            return jnp.broadcast_to(block[None], (8, 8, 128)).reshape(64, 128)

        adj = diagonal(0) * x
        for d in range(1, 4):
            m = diagonal(d)
            adj = adj + m * pltpu.roll(x, 128 - d, axis=1) + pltpu.roll(m * x, d, axis=1)
        hi, lo = split(adj)
        adj_ref[:64, b * 128 : (b + 1) * 128] = hi
        adj_ref[64:, b * 128 : (b + 1) * 128] = lo
    for i in range(10):
        both = mm_nt(adj_ref[...], tab_hi[i])
        spec_ref[i] = both[:64] + both[64:] + mm_nt(adj_ref[:64, :], tab_lo[i])
    spec_ref[10:] = jnp.zeros((6, 64, 128), F32)
    for p in range(8):
        block = spec_ref[:, p * 8 : (p + 1) * 8, :].reshape(128, 128)
        turn_ref[pl.ds(p, 128, stride=8), :] = block.T
    spec[...] = turn_ref[...].reshape(128, 8, 128).astype(BF)

    pl.semaphore_wait(ready, NT - 1)
    for pc, pt in peers:
        send(spec.at[pc * NT + pt], recv.at[me], 3, pc, pt)
    recv[me] = spec[me]

    same = (lax.broadcasted_iota(jnp.int32, (128, 128), 0) < 64) == (
        lax.broadcasted_iota(jnp.int32, (128, 128), 1) < 64
    )
    for j in range(OWN):
        one = leg[t * OWN + j]
        two = jnp.concatenate([one, one], axis=0)
        hi, lo = split(jnp.where(same, mm_nt(two, two), 0.0))
        normal[j, :128, :] = hi
        normal[j, 128:, :] = lo
    row = lax.broadcasted_iota(jnp.int32, (128, 640), 0)
    col = lax.broadcasted_iota(jnp.int32, (128, 640), 1)
    src_i, src_a = lax.shift_right_logical(row, 3), row & 7
    dst_i = (lax.shift_right_logical(col, 6) & 1) * OWN + lax.shift_right_logical(col, 7)
    dst_band, dst_a = lax.shift_right_logical(col, 3) & 7, col & 7
    hit = (src_a == dst_a) & (src_i == dst_i)
    for s in range(NC):
        perm[s * 128 : (s + 1) * 128, :] = jnp.where(hit & (dst_band == s), 1.0, 0.0).astype(BF)
    arrived(recv, ND - 1, 3)
    blocks = [recv[s * NT : (s + 1) * NT].astype(F32).reshape(128, 128).astype(BF) for s in range(NC)]
    gathered = mm(jnp.concatenate(blocks, axis=1), perm[...])
    left, right = [], []
    for j in range(OWN):
        mine = gathered[:, j * 128 : (j + 1) * 128].astype(BF)
        rows[j] = mine
        left += split(mm(jnp.concatenate([mine, mine], axis=1), normal[j]))
        right += [mine, mine]
    gram = mm_nt(jnp.concatenate(left, axis=1), jnp.concatenate(right, axis=1))
    keep = pltpu.make_async_copy(rows, rows_out, in_sem.at[6])
    keep.start()
    for k in range(GROUP):
        g_part[k] = gram[k * 4 : (k + 1) * 4, :]

    def turn(j):
        one = leg[t * OWN + j]
        turned_leg[j] = jnp.concatenate([one, one], axis=0).T
        pltpu.make_async_copy(turned_leg.at[j], turned_out.at[j], turn_sem.at[j]).start()

    seat = c * 4 + x_chip
    for d in steps:
        if d[2] == 0 and any(d):
            pc, px = bands[d[:2]], lax.rem(x_chip + d[3], 4)
            send(g_part.at[pc * 4 + px], g_group.at[seat], 4, pc, y_chip * 4 + px)
    g_group[seat] = g_part[seat]
    turn(0)
    turn(1)
    arrived(g_group, GROUP - 1, 4)
    total = g_group[0]
    for k in range(1, GROUP):
        total = total + g_group[k]
    mine_at = y_chip * GROUP + seat
    g_all[mine_at] = total * (1.0 / (2 * ORDERS * NDEG))
    for pc, pt in peers:
        send(g_all.at[mine_at], g_all.at[mine_at], 5, pc, pt)
    turn(2)
    turn(3)
    turn(4)
    arrived(g_all, ND - 1, 5)
    for k in range(GROUP):
        total = g_all[k]
        for q in range(1, 4):
            total = total + g_all[q * GROUP + k]
        gram_out[k * 4 : (k + 1) * 4, :] = total
    keep.wait()
    for j in range(OWN):
        pltpu.make_async_copy(turned_leg.at[j], turned_out.at[j], turn_sem.at[j]).wait()
    for ref, n, k in (
        (part, NT - 1, 0), (lat_send, NC - 1, 1), (table, NT - 1, 2), (spec, ND - 1, 3),
        (g_part, GROUP - 1, 4), (g_all, ND - 1, 5),
    ):
        sent(ref, n, k)


def circle(x):
    quarter = jnp.floor(x * (1.0 / 320.0) + 0.5)
    y = (x - quarter * 320.0) * (2.0 * math.pi / NLON)
    turn = quarter - 4.0 * jnp.floor(quarter * 0.25)
    z = y * y
    sine = y * (1.0 + z * (-1.0 / 6 + z * (1.0 / 120 + z * (-1.0 / 5040 + z * (1.0 / 362880)))))
    cosine = 1.0 + z * (-0.5 + z * (1.0 / 24 + z * (-1.0 / 720 + z * (1.0 / 40320 - z * (1.0 / 3628800)))))
    odd = (turn == 1.0) | (turn == 3.0)
    cos_x = jnp.where(odd, sine, cosine)
    sin_x = jnp.where(odd, cosine, sine)
    cos_x = jnp.where((turn == 1.0) | (turn == 2.0), -cos_x, cos_x)
    sin_x = jnp.where(turn >= 2.0, -sin_x, sin_x)
    return cos_x, sin_x


def front_stage(probes, legendre, orders, index, count, base, coef, weight):
    slots, obs = base.shape
    vm = pltpu.VMEM
    any_space = pl.BlockSpec(memory_space=pl.ANY)
    return pl.pallas_call(
        front_kernel,
        name="front_stage",
        out_shape=(jax.ShapeDtypeStruct((OWN, 128, 128), BF), jax.ShapeDtypeStruct((128, 128), F32),
                   jax.ShapeDtypeStruct((OWN, NDEG, 128), BF)),
        in_specs=[any_space] * 8,
        out_specs=(any_space, VM, any_space),
        scratch_shapes=[
            vm(legendre.shape, BF), vm(probes.shape, BF),
            vm(base.shape, jnp.int32), vm(coef.shape, BF), vm(weight.shape, F32),
            vm(orders.shape, jnp.int32), vm(index.shape, jnp.int32), vm(count.shape, jnp.int32),
            vm((OWN, 128, 128), BF), vm(weight.shape, F32),
            vm((slots, 32, 128), F32),
            vm((NT, PIECE, 8, 128), F32), vm((NT, PIECE, 8, 128), F32), vm((NT, PIECE, 8, 128), F32),
            vm((640, 128), F32),
            vm((NC, 80, 128), F32), vm((NC, 80, 128), BF), vm((NC, 80, 128), BF),
            vm((OWN, 128, 128), F32), vm((OWN, 128, 128), F32), vm((OWN, 128, 128), F32), vm((OWN, 128, 128), F32),
            vm((10, 128, NLON), BF), vm((10, 128, NLON), BF),
            vm((128, NLON), BF), vm((16, 64, 128), F32), vm((1024, 128), F32),
            vm((ND, 8, 128), BF), vm((ND, 8, 128), BF), vm((1024, 640), BF), vm((OWN, 256, 128), BF),
            vm((GROUP, 4, 128), F32), vm((GROUP, 4, 128), F32), vm((ND, 4, 128), F32),
            vm((OWN, NDEG, 128), BF),
            pltpu.SemaphoreType.DMA((7,)), pltpu.SemaphoreType.DMA((CHUNKS,)),
            pltpu.SemaphoreType.DMA((CHUNKS,)), pltpu.SemaphoreType.DMA((OWN,)), pltpu.SemaphoreType.DMA((12,)),
            pltpu.SemaphoreType.REGULAR,
        ],
        compiler_params=pltpu.CompilerParams(
            collective_id=0, has_side_effects=True, vmem_limit_bytes=56 * 1024 * 1024
        ),
    )(probes, legendre, orders, index, count, base, coef, weight)


def exact(a, b, dims):
    return lax.dot_general(a, b, (dims, ((), ())), precision=HIGHEST, preferred_element_type=F32)


NN = ((1,), (0,))


def three(a, b, product):
    a_hi, a_lo = split(a)
    b_hi, b_lo = split(b)
    return product(a_hi, b_hi) + product(a_hi, b_lo) + product(a_lo, b_hi)


def factorize(gram, upper_ref, inv_ref):
    n = gram.shape[0]
    row = lax.broadcasted_iota(jnp.int32, (n, n), 0)
    col = lax.broadcasted_iota(jnp.int32, (n, n), 1)
    eye = jnp.where(row == col, 1.0, 0.0)
    half = jnp.where(row > col, 1.0, 0.5 * eye)
    diag = jnp.where(row == col, gram, 0.0)
    r_col = lax.rsqrt(jnp.sum(diag, axis=1, keepdims=True))
    r_row = lax.rsqrt(jnp.sum(diag, axis=0, keepdims=True))
    inverse = (eye - half * (gram * r_col * r_row - eye)) * r_row
    upper = three(inverse, gram, mm)
    error = eye
    for _ in range(3):
        error = three(upper, inverse, mm_nt) - eye
        step = three(half * error, jnp.concatenate([inverse, upper], axis=1), mm)
        inverse = inverse - step[:, :n]
        upper = upper - step[:, n:]
    inv_ref[...] = inverse
    upper_ref[...] = jnp.where(row <= col, upper, 0.0)
    failed = jnp.max(jnp.where(jnp.abs(error) < 1e-4, 0.0, 1.0))

    @pl.when(failed > 0.5)
    def _():
        def column(j, state):
            left, full, inv = state
            at_row, at_col = row == j, col == j
            line = jnp.sum(jnp.where(at_row, left, 0.0), axis=0, keepdims=True)
            down = jnp.sum(jnp.where(at_col, left, 0.0), axis=1, keepdims=True)
            pivot = jnp.sum(jnp.where(at_row & at_col, left, 0.0), keepdims=True)
            scale = 1.0 / jnp.sqrt(pivot)
            line = jnp.where(col[:1] >= j, line * scale, 0.0)
            below = jnp.where(row[:, :1] > j, down * scale, 0.0)
            inv_line = jnp.sum(jnp.where(at_row, inv, 0.0), axis=0, keepdims=True) * scale
            inv = jnp.where(at_row, inv_line, inv - below * inv_line)
            return left - below * line, jnp.where(at_row, line, full), inv

        _, full, inv = lax.fori_loop(0, n, column, (gram, jnp.zeros_like(gram), eye))
        upper_ref[...] = full
        inv_ref[...] = inv


def panel_kernel(
    gram_ref, rows_ref, leg_ref, out_ref, upper_ref, inv_ref, rows, leg, block, rows_sem, leg_sem, out_sem
):
    fetch_rows = pltpu.make_async_copy(rows_ref, rows, rows_sem)
    fetch_rows.start()
    fetch_leg = [pltpu.make_async_copy(leg_ref.at[j], leg.at[j], leg_sem.at[j]) for j in range(OWN)]
    for copy in fetch_leg:
        copy.start()
    factorize(gram_ref[...], upper_ref, inv_ref)
    hi, lo = split(inv_ref[...])
    left = lax.broadcasted_iota(jnp.int32, (128, 128), 1) < 64
    fetch_rows.wait()
    every = jnp.concatenate([rows[j] for j in range(OWN)], axis=1)
    z_hi, z_lo = split(mm(hi, every) + mm(lo, every))
    writes = []
    for j in range(OWN):
        cols = slice(j * 128, (j + 1) * 128)
        hi_f, lo_f = z_hi[:, cols].astype(F32), z_lo[:, cols].astype(F32)
        cosine = jnp.where(left, hi_f, pltpu.roll(lo_f, 64, axis=1))
        sine = jnp.where(left, pltpu.roll(hi_f, 64, axis=1), lo_f)
        weights = jnp.concatenate([cosine, sine], axis=0).astype(BF)
        fetch_leg[j].wait()
        for start, stop in ((0, 608), (608, NDEG)):
            both = mm_nt(leg[j, start:stop, :], weights)
            block[0, j, start:stop, :] = both[:, :128]
            block[1, j, start:stop, :] = both[:, 128:]
        for half in range(2):
            write = pltpu.make_async_copy(block.at[half, j], out_ref.at[half, j], out_sem.at[half, j])
            write.start()
            writes.append(write)
    for write in writes:
        write.wait()


def panel_stage(gram, rows, turned):
    any_space = pl.BlockSpec(memory_space=pl.ANY)
    return pl.pallas_call(
        panel_kernel,
        name="panel_stage",
        out_shape=(
            jax.ShapeDtypeStruct((2, OWN, NDEG, 128), F32),
            jax.ShapeDtypeStruct((128, 128), F32),
        ),
        in_specs=[VM, any_space, any_space],
        out_specs=(any_space, VM),
        scratch_shapes=[
            pltpu.VMEM((128, 128), F32),
            pltpu.VMEM(rows.shape, BF),
            pltpu.VMEM(turned.shape, BF),
            pltpu.VMEM((2, OWN, NDEG, 128), F32),
            pltpu.SemaphoreType.DMA,
            pltpu.SemaphoreType.DMA((OWN,)),
            pltpu.SemaphoreType.DMA((2, OWN)),
        ],
    )(gram, rows, turned)


def on_device(
    probes, legendre, order_map, tile_index, tile_count, base_offset, stencil_weight, obs_weight
):
    rows, gram, turned = front_stage(
        probes, legendre, order_map.reshape(OWN, 128), tile_index[0], tile_count,
        base_offset[0, 0], stencil_weight[0, 0], obs_weight[0, 0],
    )
    panel, upper = panel_stage(gram, rows, turned)
    return (jnp.swapaxes(panel, 2, 3), upper)


def solution(mesh):
    return jax.shard_map(
        on_device,
        mesh=mesh,
        in_specs=(
            P(None, "coef", "track", None),
            P("coef", None, None),
            P(),
            P("coef", None, None),
            P("coef", None),
            P("coef", "track", None, None),
            P("coef", "track", None, None, None),
            P("coef", "track", None, None),
        ),
        out_specs=(P(None, ("coef", "track"), None, None), P()),
        check_vma=False,
    )
```

```python
import math

import jax
import jax.numpy as jnp
from jax import lax
from jax.experimental import pallas as pl
from jax.experimental.pallas import tpu as pltpu
from jax.sharding import PartitionSpec as P

NDEG = 1200
ORDERS = 640
NLON = 1280
NC = 8
NT = 16
ND = NC * NT
OWN = 5
UNITS = 40
PIECE = 3
GROUP = 32
STEP = 20
CHUNKS = 4

BF = jnp.bfloat16
F32 = jnp.float32
HIGHEST = lax.Precision.HIGHEST
MESH = pl.DeviceIdType.MESH
VM = pl.BlockSpec(memory_space=pltpu.VMEM)


def mm(a, b):
    return lax.dot_general(a, b, (((1,), (0,)), ((), ())), preferred_element_type=F32)


def mm_nt(a, b):
    return lax.dot_general(a, b, (((1,), (1,)), ((), ())), preferred_element_type=F32)


def split(x):
    hi = x.astype(BF)
    return hi, (x - hi.astype(F32)).astype(BF)


def front_kernel(
    probes_ref, leg_ref, order_ref, index_ref, count_ref, base_ref, coef_ref, weight_ref,
    rows_out, gram_out, turned_out,
    leg, prob, base, coef, weight, order_map, tile_index, tile_count, live, hist, norm, part, table, lat_rows, lat_pack, lat_send, lat_recv,
    cos_q, sin_q, cos_b, sin_b, tab_hi, tab_lo, adj_ref, spec_ref, turn_ref, spec, recv, perm, normal,
    g_part, g_group, g_all, in_sem, leg_sem, prob_sem, comm, ready,
):
    c = lax.axis_index("coef")
    t = lax.axis_index("track")
    me = c * NT + t

    def send(src, dst, k, pc, pt):
        pltpu.make_async_remote_copy(
            src, dst, comm.at[2 * k], comm.at[2 * k + 1], device_id=(pc, pt), device_id_type=MESH
        ).start()

    def arrived(ref, n, k):
        pltpu.make_async_copy(ref.at[pl.ds(0, n)], ref.at[pl.ds(0, n)], comm.at[2 * k + 1]).wait()

    def sent(ref, n, k):
        pltpu.make_async_copy(ref.at[pl.ds(0, n)], ref.at[pl.ds(0, n)], comm.at[2 * k]).wait()

    z, core = lax.div(c, 2), lax.rem(c, 2)
    y_chip, x_chip = lax.div(t, 4), lax.rem(t, 4)
    far = (0, 1, 2, 1)
    bands = {(dz, dk): lax.rem(z + dz, 4) * 2 + lax.rem(core + dk, 2) for dz in range(4) for dk in range(2)}
    tracks = {(dy, dx): lax.rem(y_chip + dy, 4) * 4 + lax.rem(x_chip + dx, 4) for dy in range(4) for dx in range(4)}
    steps = [(dz, dk, dy, dx) for dz in range(4) for dk in range(2) for dy in range(4) for dx in range(4)]
    steps.sort(key=lambda d: -(far[d[0]] + far[d[2]] + far[d[3]]) * 2 - d[1])
    peers = [(bands[d[:2]], tracks[d[2:]]) for d in steps if any(d)]

    small = [
        pltpu.make_async_copy(src, dst, in_sem.at[k])
        for k, (src, dst) in enumerate(
            (
                (base_ref, base), (coef_ref, coef), (weight_ref, weight),
                (order_ref, order_map), (index_ref, tile_index), (count_ref, tile_count),
            )
        )
    ]
    for copy in small:
        copy.start()

    def fetch(k):
        orders = pl.ds(k * STEP, STEP)
        return (
            pltpu.make_async_copy(leg_ref.at[orders], leg.at[orders], leg_sem.at[k]),
            pltpu.make_async_copy(probes_ref.at[:, orders], prob.at[:, orders], prob_sem.at[k]),
        )

    barrier = pltpu.get_barrier_semaphore()

    for i in range(1, NC):
        pl.semaphore_signal(barrier, 1, device_id=(lax.rem(c + i, NC), t), device_id_type=MESH)
    for i in range(1, NT):
        pl.semaphore_signal(barrier, 1, device_id=(c, lax.rem(t + i, NT)), device_id_type=MESH)

    for copy in small:
        copy.wait()
    for k in range(CHUNKS):
        for copy in fetch(k):
            copy.start()
    slots, obs = base.shape
    lane16 = lax.broadcasted_iota(jnp.int32, (1, NT), 1)
    count = jnp.sum(jnp.where(lane16 == t, tile_count[...].astype(F32), 0.0), axis=1, keepdims=True)
    slot_id = lax.broadcasted_iota(jnp.int32, (slots, obs), 0).astype(F32)
    live[...] = jnp.where(slot_id < count, weight[...], 0.0)
    points = lax.broadcasted_iota(jnp.int32, (128, obs), 0)

    def slot(group, carry):
        for u in range(12):
            s = group * 12 + u
            hot = jnp.where(points == base[pl.ds(s, 1), :], 1.0, 0.0).astype(BF)
            four = coef[s].astype(F32)
            eight = jnp.concatenate([four, jnp.zeros_like(four)], axis=0)
            scaled = eight * live[pl.ds(s, 1), :]
            full = jnp.concatenate(
                [scaled * eight] + [scaled * pltpu.roll(eight, 8 - d, axis=0) for d in range(1, 4)], axis=0
            )
            hi, mid = split(full)
            low = (full - hi.astype(F32) - mid.astype(F32)).astype(BF)
            sums = mm_nt(jnp.concatenate([hi, mid, low], axis=0), hot)
            hist[s] = sums[:32] + sums[32:64] + sums[64:]
        return carry

    lax.fori_loop(0, slots // 12, slot, 0)
    diagonals = []
    for d in range(4):
        total = hist[:, 8 * d, :]
        for i in range(1, 4 - d):
            total = total + pltpu.roll(hist[:, 8 * d + i, :], i, axis=1)
        diagonals.append(total)
    unit = lax.broadcasted_iota(jnp.int32, (80, slots), 0)
    tile = (unit & 7) * 10 + lax.shift_right_logical(unit, 3)
    pick = jnp.where(tile == tile_index[pl.ds(t, 1), :], 1.0, 0.0)
    summed = exact(pick, jnp.concatenate(diagonals, axis=1), NN)
    for u in range(NT * PIECE):
        if u < UNITS:
            b, d = u // 4, u % 4
            block = summed[b * 8 : (b + 1) * 8, d * 128 : (d + 1) * 128]
        else:
            block = jnp.zeros((8, 128), F32)
        norm[u // PIECE, u % PIECE] = block
    pl.semaphore_wait(barrier, NC + NT - 2)
    for i in range(1, NT):
        pl.semaphore_signal(ready, 1, device_id=(c, lax.rem(t + i, NT)), device_id_type=MESH)
    for i in range(1, NT):
        peer = (t + i) % NT
        send(norm.at[peer], part.at[t], 0, c, peer)
    part[t] = norm[t]

    def lat_step(k, carry):
        for copy in fetch(k):
            copy.wait()
        for u in range(STEP):
            order = k * STEP + u
            both = mm_nt(prob[:, order].reshape(16, NDEG), leg[order])
            owner = order // OWN
            row = ((order - owner * OWN) * NT + owner) * 8
            lat_rows[pl.ds(pl.multiple_of(row, 8), 8), :] = jnp.concatenate([both[:8], both[8:]], axis=1)
        return carry

    lax.fori_loop(0, CHUNKS, lat_step, 0)
    lanes = lax.broadcasted_iota(jnp.int32, (64, 128), 1)
    slot16 = lax.shift_right_logical(lanes, 4)
    rest = [jnp.zeros((64, 128), F32)] * 2
    for p in range(8):
        some = jnp.concatenate([lat_rows[pl.ds(p, 80, stride=8), :], jnp.zeros((48, 128), F32)], axis=0).T
        cosine, sine = some[:64], some[64:]
        main = jnp.where(lanes < 64, cosine, pltpu.roll(sine, 64, axis=1))
        g = p // 2
        rest[p % 2] = jnp.where(slot16 == 2 * g, pltpu.roll(cosine, (32 * g + 64) % 128, axis=1), rest[p % 2])
        rest[p % 2] = jnp.where(slot16 == 2 * g + 1, pltpu.roll(sine, (32 * g + 80) % 128, axis=1), rest[p % 2])
        for s in range(NC):
            lat_pack[s, p * 8 : (p + 1) * 8, :] = main[s * 8 : (s + 1) * 8, :]
    for k in range(2):
        for s in range(NC):
            lat_pack[s, 64 + k * 8 : 72 + k * 8, :] = rest[k][s * 8 : (s + 1) * 8, :]
    lat_send[...] = lat_pack[...].astype(BF)
    for i in range(1, NC):
        peer = (c + i) % NC
        send(lat_send.at[peer], lat_recv.at[c], 1, peer, t)
    lat_recv[c] = lat_send[c]
    arrived(part, NT - 1, 0)
    total = part[0]
    for s in range(1, NT):
        total = total + part[s]
    table[t] = total
    for i in range(1, NT):
        peer = (t + i) % NT
        send(table.at[t], table.at[t], 2, c, peer)

    orders = jnp.concatenate([order_map[r : r + 1, :] for r in range(OWN)], axis=1)
    coarse = jnp.broadcast_to(lax.shift_right_logical(orders, 5).astype(F32).astype(BF), (128, ORDERS))
    fine = jnp.broadcast_to((orders & 31).astype(F32).astype(BF), (128, ORDERS))
    owner_row = lax.broadcasted_iota(jnp.int32, (128, ORDERS), 0) * OWN
    slot_lane = lax.broadcasted_iota(jnp.int32, (128, ORDERS), 1)
    lane = lax.broadcasted_iota(jnp.int32, (128, 128), 1).astype(F32)

    def trig(j, carry):
        hot = jnp.where(owner_row + j == slot_lane, 1.0, 0.0).astype(BF)
        order = 32.0 * mm_nt(hot, coarse) + mm_nt(hot, fine)
        cos_q[j], sin_q[j] = circle(order * lane)
        cosine, sine = circle(order * (lane * 128.0))
        cos_b[j] = cosine * (1.0 / math.sqrt(ORDERS))
        sin_b[j] = sine * (1.0 / math.sqrt(ORDERS))
        return carry

    def make(j, carry):
        cq, sq, cb, sb = cos_q[j], sin_q[j], cos_b[j], sin_b[j]
        for b in range(10):
            ca, sa = cb[:, b : b + 1], sb[:, b : b + 1]
            cols = slice(b * 128, (b + 1) * 128)
            hi, lo = split(ca * cq - sa * sq)
            tab_hi[j, :, cols] = hi
            tab_lo[j, :, cols] = lo
            hi, lo = split(sa * cq + ca * sq)
            tab_hi[OWN + j, :, cols] = hi
            tab_lo[OWN + j, :, cols] = lo
        return carry

    lax.fori_loop(0, OWN, lambda j, carry: make(j, trig(j, carry)), 0)

    arrived(lat_recv, NC - 1, 1)
    slot32 = lax.shift_right_logical(lax.broadcasted_iota(jnp.int32, (16, 128), 1), 5)
    tail = []
    for first in (0, 4):
        parts = [jnp.zeros((16, 128), F32)] * 4
        for k in range(4):
            some = lat_recv[first + k, 64:, :].astype(F32)
            for g in range(4):
                moved = pltpu.roll(some, (32 * (k - g)) % 128, axis=1) if k != g else some
                parts[g] = jnp.where(slot32 == k, moved, parts[g])
        tail.append(jnp.concatenate(parts, axis=0).astype(BF))

    def rows_of(tab, s):
        own = slice(s * NT, (s + 1) * NT)
        return [tab[0:4, own, :].reshape(64, NLON), tab[OWN : OWN + 4, own, :].reshape(64, NLON)]

    def rest_of(tab, s):
        own = slice(s * NT, (s + 1) * NT)
        return [tab[4, own, :], tab[OWN + 4, own, :]]

    grid = jnp.zeros((64, NLON), F32)
    for tab in (tab_hi, tab_lo):
        for s in range(0, NC, 2):
            pair = jnp.concatenate([lat_recv[s, :64, :], lat_recv[s + 1, :64, :]], axis=1)
            grid = grid + mm(pair, jnp.concatenate(rows_of(tab, s) + rows_of(tab, s + 1), axis=0))
        rest_rows = [block for s in range(NC) for block in rest_of(tab, s)]
        grid = grid + mm(jnp.concatenate(tail, axis=1), jnp.concatenate(rest_rows, axis=0))
    arrived(table, NT - 1, 2)
    for b in range(10):
        x = grid[:, b * 128 : (b + 1) * 128]

        def diagonal(d):
            unit = b * 4 + d
            block = table[unit // PIECE, unit % PIECE]
            return jnp.broadcast_to(block[None], (8, 8, 128)).reshape(64, 128)

        adj = diagonal(0) * x
        for d in range(1, 4):
            m = diagonal(d)
            adj = adj + m * pltpu.roll(x, 128 - d, axis=1) + pltpu.roll(m * x, d, axis=1)
        hi, lo = split(adj)
        adj_ref[:64, b * 128 : (b + 1) * 128] = hi
        adj_ref[64:, b * 128 : (b + 1) * 128] = lo
    for i in range(10):
        both = mm_nt(adj_ref[...], tab_hi[i])
        spec_ref[i] = both[:64] + both[64:] + mm_nt(adj_ref[:64, :], tab_lo[i])
    spec_ref[10:] = jnp.zeros((6, 64, 128), F32)
    for p in range(8):
        block = spec_ref[:, p * 8 : (p + 1) * 8, :].reshape(128, 128)
        turn_ref[pl.ds(p, 128, stride=8), :] = block.T
    spec[...] = turn_ref[...].reshape(128, 8, 128).astype(BF)

    pl.semaphore_wait(ready, NT - 1)
    for pc, pt in peers:
        send(spec.at[pc * NT + pt], recv.at[me], 3, pc, pt)
    recv[me] = spec[me]

    same = (lax.broadcasted_iota(jnp.int32, (128, 128), 0) < 64) == (
        lax.broadcasted_iota(jnp.int32, (128, 128), 1) < 64
    )
    for j in range(OWN):
        one = leg[t * OWN + j]
        two = jnp.concatenate([one, one], axis=0)
        hi, lo = split(jnp.where(same, mm_nt(two, two), 0.0))
        normal[j, :128, :] = hi
        normal[j, 128:, :] = lo
    row = lax.broadcasted_iota(jnp.int32, (128, 640), 0)
    col = lax.broadcasted_iota(jnp.int32, (128, 640), 1)
    src_i, src_a = lax.shift_right_logical(row, 3), row & 7
    dst_i = (lax.shift_right_logical(col, 6) & 1) * OWN + lax.shift_right_logical(col, 7)
    dst_band, dst_a = lax.shift_right_logical(col, 3) & 7, col & 7
    hit = (src_a == dst_a) & (src_i == dst_i)
    for s in range(NC):
        perm[s * 128 : (s + 1) * 128, :] = jnp.where(hit & (dst_band == s), 1.0, 0.0).astype(BF)
    arrived(recv, ND - 1, 3)
    blocks = [recv[s * NT : (s + 1) * NT].astype(F32).reshape(128, 128).astype(BF) for s in range(NC)]
    gathered = mm(jnp.concatenate(blocks, axis=1), perm[...])
    left, right = [], []
    for j in range(OWN):
        mine = gathered[:, j * 128 : (j + 1) * 128].astype(BF)
        rows_out[j] = mine
        left += split(mm(jnp.concatenate([mine, mine], axis=1), normal[j]))
        right += [mine, mine]
    gram = mm_nt(jnp.concatenate(left, axis=1), jnp.concatenate(right, axis=1))
    for k in range(GROUP):
        g_part[k] = gram[k * 4 : (k + 1) * 4, :]

    def turn(j):
        one = leg[t * OWN + j]
        turned_out[j] = jnp.concatenate([one, one], axis=0).T

    seat = c * 4 + x_chip
    for d in steps:
        if d[2] == 0 and any(d):
            pc, px = bands[d[:2]], lax.rem(x_chip + d[3], 4)
            send(g_part.at[pc * 4 + px], g_group.at[seat], 4, pc, y_chip * 4 + px)
    g_group[seat] = g_part[seat]
    turn(0)
    turn(1)
    arrived(g_group, GROUP - 1, 4)
    total = g_group[0]
    for k in range(1, GROUP):
        total = total + g_group[k]
    mine_at = y_chip * GROUP + seat
    g_all[mine_at] = total * (1.0 / (2 * ORDERS * NDEG))
    for pc, pt in peers:
        send(g_all.at[mine_at], g_all.at[mine_at], 5, pc, pt)
    turn(2)
    turn(3)
    turn(4)
    arrived(g_all, ND - 1, 5)
    for k in range(GROUP):
        total = g_all[k]
        for q in range(1, 4):
            total = total + g_all[q * GROUP + k]
        gram_out[k * 4 : (k + 1) * 4, :] = total
    for ref, n, k in (
        (part, NT - 1, 0), (lat_send, NC - 1, 1), (table, NT - 1, 2), (spec, ND - 1, 3),
        (g_part, GROUP - 1, 4), (g_all, ND - 1, 5),
    ):
        sent(ref, n, k)


def circle(x):
    quarter = jnp.floor(x * (1.0 / 320.0) + 0.5)
    y = (x - quarter * 320.0) * (2.0 * math.pi / NLON)
    turn = quarter - 4.0 * jnp.floor(quarter * 0.25)
    z = y * y
    sine = y * (1.0 + z * (-1.0 / 6 + z * (1.0 / 120 + z * (-1.0 / 5040 + z * (1.0 / 362880)))))
    cosine = 1.0 + z * (-0.5 + z * (1.0 / 24 + z * (-1.0 / 720 + z * (1.0 / 40320 - z * (1.0 / 3628800)))))
    odd = (turn == 1.0) | (turn == 3.0)
    cos_x = jnp.where(odd, sine, cosine)
    sin_x = jnp.where(odd, cosine, sine)
    cos_x = jnp.where((turn == 1.0) | (turn == 2.0), -cos_x, cos_x)
    sin_x = jnp.where(turn >= 2.0, -sin_x, sin_x)
    return cos_x, sin_x


def front_stage(probes, legendre, orders, index, count, base, coef, weight):
    slots, obs = base.shape
    vm = pltpu.VMEM
    any_space = pl.BlockSpec(memory_space=pl.ANY)
    return pl.pallas_call(
        front_kernel,
        name="front_stage",
        out_shape=(jax.ShapeDtypeStruct((OWN, 128, 128), BF), jax.ShapeDtypeStruct((128, 128), F32),
                   jax.ShapeDtypeStruct((OWN, NDEG, 128), BF)),
        in_specs=[any_space] * 8,
        out_specs=(VM, VM, VM),
        scratch_shapes=[
            vm(legendre.shape, BF), vm(probes.shape, BF),
            vm(base.shape, jnp.int32), vm(coef.shape, BF), vm(weight.shape, F32),
            vm(orders.shape, jnp.int32), vm(index.shape, jnp.int32), vm(count.shape, jnp.int32),
            vm(weight.shape, F32),
            vm((slots, 32, 128), F32),
            vm((NT, PIECE, 8, 128), F32), vm((NT, PIECE, 8, 128), F32), vm((NT, PIECE, 8, 128), F32),
            vm((640, 128), F32),
            vm((NC, 80, 128), F32), vm((NC, 80, 128), BF), vm((NC, 80, 128), BF),
            vm((OWN, 128, 128), F32), vm((OWN, 128, 128), F32), vm((OWN, 128, 128), F32), vm((OWN, 128, 128), F32),
            vm((10, 128, NLON), BF), vm((10, 128, NLON), BF),
            vm((128, NLON), BF), vm((16, 64, 128), F32), vm((1024, 128), F32),
            vm((ND, 8, 128), BF), vm((ND, 8, 128), BF), vm((1024, 640), BF), vm((OWN, 256, 128), BF),
            vm((GROUP, 4, 128), F32), vm((GROUP, 4, 128), F32), vm((ND, 4, 128), F32),
            pltpu.SemaphoreType.DMA((6,)), pltpu.SemaphoreType.DMA((CHUNKS,)),
            pltpu.SemaphoreType.DMA((CHUNKS,)), pltpu.SemaphoreType.DMA((12,)),
            pltpu.SemaphoreType.REGULAR,
        ],
        compiler_params=pltpu.CompilerParams(
            collective_id=0, has_side_effects=True, vmem_limit_bytes=44 * 1024 * 1024
        ),
    )(*(pltpu.with_memory_space_constraint(x, pltpu.HBM) for x in (probes, legendre, orders, index, count, base, coef, weight)))


def exact(a, b, dims):
    return lax.dot_general(a, b, (dims, ((), ())), precision=HIGHEST, preferred_element_type=F32)


NN = ((1,), (0,))


def three(a, b, product):
    a_hi, a_lo = split(a)
    b_hi, b_lo = split(b)
    return product(a_hi, b_hi) + product(a_hi, b_lo) + product(a_lo, b_hi)


def factorize(gram, upper_ref, inv_ref):
    n = gram.shape[0]
    row = lax.broadcasted_iota(jnp.int32, (n, n), 0)
    col = lax.broadcasted_iota(jnp.int32, (n, n), 1)
    eye = jnp.where(row == col, 1.0, 0.0)
    half = jnp.where(row > col, 1.0, 0.5 * eye)
    diag = jnp.where(row == col, gram, 0.0)
    r_col = lax.rsqrt(jnp.sum(diag, axis=1, keepdims=True))
    r_row = lax.rsqrt(jnp.sum(diag, axis=0, keepdims=True))
    inverse = (eye - half * (gram * r_col * r_row - eye)) * r_row
    upper = three(inverse, gram, mm)
    error = eye
    for _ in range(3):
        error = three(upper, inverse, mm_nt) - eye
        step = three(half * error, jnp.concatenate([inverse, upper], axis=1), mm)
        inverse = inverse - step[:, :n]
        upper = upper - step[:, n:]
    inv_ref[...] = inverse
    upper_ref[...] = jnp.where(row <= col, upper, 0.0)
    failed = jnp.max(jnp.where(jnp.abs(error) < 1e-4, 0.0, 1.0))

    @pl.when(failed > 0.5)
    def _():
        def column(j, state):
            left, full, inv = state
            at_row, at_col = row == j, col == j
            line = jnp.sum(jnp.where(at_row, left, 0.0), axis=0, keepdims=True)
            down = jnp.sum(jnp.where(at_col, left, 0.0), axis=1, keepdims=True)
            pivot = jnp.sum(jnp.where(at_row & at_col, left, 0.0), keepdims=True)
            scale = 1.0 / jnp.sqrt(pivot)
            line = jnp.where(col[:1] >= j, line * scale, 0.0)
            below = jnp.where(row[:, :1] > j, down * scale, 0.0)
            inv_line = jnp.sum(jnp.where(at_row, inv, 0.0), axis=0, keepdims=True) * scale
            inv = jnp.where(at_row, inv_line, inv - below * inv_line)
            return left - below * line, jnp.where(at_row, line, full), inv

        _, full, inv = lax.fori_loop(0, n, column, (gram, jnp.zeros_like(gram), eye))
        upper_ref[...] = full
        inv_ref[...] = inv


def panel_kernel(gram_ref, rows_ref, leg_ref, out_ref, upper_ref, inv_ref, block, out_sem):
    factorize(gram_ref[...], upper_ref, inv_ref)
    hi, lo = split(inv_ref[...])
    left = lax.broadcasted_iota(jnp.int32, (128, 128), 1) < 64
    every = jnp.concatenate([rows_ref[j] for j in range(OWN)], axis=1)
    z_hi, z_lo = split(mm(hi, every) + mm(lo, every))
    writes = []
    for j in range(OWN):
        cols = slice(j * 128, (j + 1) * 128)
        hi_f, lo_f = z_hi[:, cols].astype(F32), z_lo[:, cols].astype(F32)
        cosine = jnp.where(left, hi_f, pltpu.roll(lo_f, 64, axis=1))
        sine = jnp.where(left, pltpu.roll(hi_f, 64, axis=1), lo_f)
        weights = jnp.concatenate([cosine, sine], axis=0).astype(BF)
        for start, stop in ((0, 608), (608, NDEG)):
            both = mm_nt(leg_ref[j, start:stop, :], weights)
            block[0, j, start:stop, :] = both[:, :128]
            block[1, j, start:stop, :] = both[:, 128:]
        for half in range(2):
            write = pltpu.make_async_copy(block.at[half, j], out_ref.at[half, j], out_sem.at[half, j])
            write.start()
            writes.append(write)
    for write in writes:
        write.wait()


def panel_stage(gram, rows, turned):
    any_space = pl.BlockSpec(memory_space=pl.ANY)
    return pl.pallas_call(
        panel_kernel,
        name="panel_stage",
        out_shape=(
            jax.ShapeDtypeStruct((2, OWN, NDEG, 128), F32),
            jax.ShapeDtypeStruct((128, 128), F32),
        ),
        in_specs=[VM, VM, VM],
        out_specs=(any_space, VM),
        scratch_shapes=[
            pltpu.VMEM((128, 128), F32),
            pltpu.VMEM((2, OWN, NDEG, 128), F32),
            pltpu.SemaphoreType.DMA((2, OWN)),
        ],
        compiler_params=pltpu.CompilerParams(vmem_limit_bytes=16 * 1024 * 1024),
    )(gram, rows, turned)


def on_device(
    probes, legendre, order_map, tile_index, tile_count, base_offset, stencil_weight, obs_weight
):
    rows, gram, turned = front_stage(
        probes, legendre, order_map.reshape(OWN, 128), tile_index[0], tile_count,
        base_offset[0, 0], stencil_weight[0, 0], obs_weight[0, 0],
    )
    panel, upper = panel_stage(gram, rows, turned)
    return (jnp.swapaxes(panel, 2, 3), upper)


def solution(mesh):
    return jax.shard_map(
        on_device,
        mesh=mesh,
        in_specs=(
            P(None, "coef", "track", None),
            P("coef", None, None),
            P(),
            P("coef", None, None),
            P("coef", None),
            P("coef", "track", None, None),
            P("coef", "track", None, None, None),
            P("coef", "track", None, None),
        ),
        out_specs=(P(None, ("coef", "track"), None, None), P()),
        check_vma=False,
    )
```

```python
import math

import jax
import jax.numpy as jnp
from jax import lax
from jax.experimental import pallas as pl
from jax.experimental.pallas import tpu as pltpu
from jax.sharding import PartitionSpec as P

NDEG = 1200
ORDERS = 640
NLON = 1280
NC = 8
NT = 16
ND = NC * NT
OWN = 5
UNITS = 40
PIECE = 3
GROUP = 32
STEP = 20
CHUNKS = 4

BF = jnp.bfloat16
F32 = jnp.float32
HIGHEST = lax.Precision.HIGHEST
MESH = pl.DeviceIdType.MESH
VM = pl.BlockSpec(memory_space=pltpu.VMEM)


def mm(a, b):
    return lax.dot_general(a, b, (((1,), (0,)), ((), ())), preferred_element_type=F32)


def mm_nt(a, b):
    return lax.dot_general(a, b, (((1,), (1,)), ((), ())), preferred_element_type=F32)


def split(x):
    hi = x.astype(BF)
    return hi, (x - hi.astype(F32)).astype(BF)


def front_kernel(
    probes_ref, leg_ref, order_ref, index_ref, count_ref, base_ref, coef_ref, weight_ref,
    rows_out, gram_out, turned_out,
    leg, prob, base, coef, weight, order_map, tile_index, tile_count, live, hist, norm, part, table, lat_rows, lat_pack, lat_send, lat_recv,
    cos_q, sin_q, cos_b, sin_b, tab_hi, tab_lo, adj_ref, spec_ref, turn_ref, spec, recv, perm, normal,
    g_part, g_group, g_all, in_sem, leg_sem, prob_sem, comm, ready,
):
    c = lax.axis_index("coef")
    t = lax.axis_index("track")
    me = c * NT + t

    def send(src, dst, k, pc, pt):
        pltpu.make_async_remote_copy(
            src, dst, comm.at[2 * k], comm.at[2 * k + 1], device_id=(pc, pt), device_id_type=MESH
        ).start()

    def arrived(ref, n, k):
        pltpu.make_async_copy(ref.at[pl.ds(0, n)], ref.at[pl.ds(0, n)], comm.at[2 * k + 1]).wait()

    def sent(ref, n, k):
        pltpu.make_async_copy(ref.at[pl.ds(0, n)], ref.at[pl.ds(0, n)], comm.at[2 * k]).wait()

    z, core = lax.div(c, 2), lax.rem(c, 2)
    y_chip, x_chip = lax.div(t, 4), lax.rem(t, 4)
    far = (0, 1, 2, 1)
    bands = {(dz, dk): lax.rem(z + dz, 4) * 2 + lax.rem(core + dk, 2) for dz in range(4) for dk in range(2)}
    tracks = {(dy, dx): lax.rem(y_chip + dy, 4) * 4 + lax.rem(x_chip + dx, 4) for dy in range(4) for dx in range(4)}
    steps = [(dz, dk, dy, dx) for dz in range(4) for dk in range(2) for dy in range(4) for dx in range(4)]
    steps.sort(key=lambda d: -(far[d[0]] + far[d[2]] + far[d[3]]) * 2 - d[1])
    peers = [(bands[d[:2]], tracks[d[2:]]) for d in steps if any(d)]

    small = [
        pltpu.make_async_copy(src, dst, in_sem.at[k])
        for k, (src, dst) in enumerate(
            (
                (base_ref, base), (coef_ref, coef), (weight_ref, weight),
                (order_ref, order_map), (index_ref, tile_index), (count_ref, tile_count),
            )
        )
    ]
    for copy in small:
        copy.start()

    def fetch(k):
        orders = pl.ds(k * STEP, STEP)
        return (
            pltpu.make_async_copy(leg_ref.at[orders], leg.at[orders], leg_sem.at[k]),
            pltpu.make_async_copy(probes_ref.at[:, orders], prob.at[:, orders], prob_sem.at[k]),
        )

    barrier = pltpu.get_barrier_semaphore()

    for i in range(1, NC):
        pl.semaphore_signal(barrier, 1, device_id=(lax.rem(c + i, NC), t), device_id_type=MESH)
    for i in range(1, NT):
        pl.semaphore_signal(barrier, 1, device_id=(c, lax.rem(t + i, NT)), device_id_type=MESH)

    for copy in small:
        copy.wait()
    for k in range(CHUNKS):
        for copy in fetch(k):
            copy.start()
    slots, obs = base.shape
    lane16 = lax.broadcasted_iota(jnp.int32, (1, NT), 1)
    count = jnp.sum(jnp.where(lane16 == t, tile_count[...].astype(F32), 0.0), axis=1, keepdims=True)
    slot_id = lax.broadcasted_iota(jnp.int32, (slots, obs), 0).astype(F32)
    live[...] = jnp.where(slot_id < count, weight[...], 0.0)
    points = lax.broadcasted_iota(jnp.int32, (128, obs), 0)

    def slot(group, carry):
        for u in range(12):
            s = group * 12 + u
            hot = jnp.where(points == base[pl.ds(s, 1), :], 1.0, 0.0).astype(BF)
            four = coef[s].astype(F32)
            eight = jnp.concatenate([four, jnp.zeros_like(four)], axis=0)
            scaled = eight * live[pl.ds(s, 1), :]
            full = jnp.concatenate(
                [scaled * eight] + [scaled * pltpu.roll(eight, 8 - d, axis=0) for d in range(1, 4)], axis=0
            )
            hi, mid = split(full)
            low = (full - hi.astype(F32) - mid.astype(F32)).astype(BF)
            sums = mm_nt(jnp.concatenate([hi, mid, low], axis=0), hot)
            hist[s] = sums[:32] + sums[32:64] + sums[64:]
        return carry

    lax.fori_loop(0, slots // 12, slot, 0)
    diagonals = []
    for d in range(4):
        total = hist[:, 8 * d, :]
        for i in range(1, 4 - d):
            total = total + pltpu.roll(hist[:, 8 * d + i, :], i, axis=1)
        diagonals.append(total)
    unit = lax.broadcasted_iota(jnp.int32, (80, slots), 0)
    tile = (unit & 7) * 10 + lax.shift_right_logical(unit, 3)
    pick = jnp.where(tile == tile_index[pl.ds(t, 1), :], 1.0, 0.0)
    summed = exact(pick, jnp.concatenate(diagonals, axis=1), NN)
    for u in range(NT * PIECE):
        if u < UNITS:
            b, d = u // 4, u % 4
            block = summed[b * 8 : (b + 1) * 8, d * 128 : (d + 1) * 128]
        else:
            block = jnp.zeros((8, 128), F32)
        norm[u // PIECE, u % PIECE] = block
    pl.semaphore_wait(barrier, NC + NT - 2)
    for i in range(1, NT):
        pl.semaphore_signal(ready, 1, device_id=(c, lax.rem(t + i, NT)), device_id_type=MESH)
    for i in range(1, NT):
        peer = (t + i) % NT
        send(norm.at[peer], part.at[t], 0, c, peer)
    part[t] = norm[t]

    def lat_step(k, carry):
        for copy in fetch(k):
            copy.wait()
        for u in range(STEP):
            order = k * STEP + u
            both = mm_nt(prob[:, order].reshape(16, NDEG), leg[order])
            owner = order // OWN
            row = ((order - owner * OWN) * NT + owner) * 8
            lat_rows[pl.ds(pl.multiple_of(row, 8), 8), :] = jnp.concatenate([both[:8], both[8:]], axis=1)
        return carry

    lax.fori_loop(0, CHUNKS, lat_step, 0)
    lanes = lax.broadcasted_iota(jnp.int32, (64, 128), 1)
    slot16 = lax.shift_right_logical(lanes, 4)
    rest = [jnp.zeros((64, 128), F32)] * 2
    for p in range(8):
        some = jnp.concatenate([lat_rows[pl.ds(p, 80, stride=8), :], jnp.zeros((48, 128), F32)], axis=0).T
        cosine, sine = some[:64], some[64:]
        main = jnp.where(lanes < 64, cosine, pltpu.roll(sine, 64, axis=1))
        g = p // 2
        rest[p % 2] = jnp.where(slot16 == 2 * g, pltpu.roll(cosine, (32 * g + 64) % 128, axis=1), rest[p % 2])
        rest[p % 2] = jnp.where(slot16 == 2 * g + 1, pltpu.roll(sine, (32 * g + 80) % 128, axis=1), rest[p % 2])
        for s in range(NC):
            lat_pack[s, p * 8 : (p + 1) * 8, :] = main[s * 8 : (s + 1) * 8, :]
    for k in range(2):
        for s in range(NC):
            lat_pack[s, 64 + k * 8 : 72 + k * 8, :] = rest[k][s * 8 : (s + 1) * 8, :]
    lat_send[...] = lat_pack[...].astype(BF)
    for i in range(1, NC):
        peer = (c + i) % NC
        send(lat_send.at[peer], lat_recv.at[c], 1, peer, t)
    lat_recv[c] = lat_send[c]

    orders = jnp.concatenate([order_map[r : r + 1, :] for r in range(OWN)], axis=1)
    coarse = jnp.broadcast_to(lax.shift_right_logical(orders, 5).astype(F32).astype(BF), (128, ORDERS))
    fine = jnp.broadcast_to((orders & 31).astype(F32).astype(BF), (128, ORDERS))
    owner_row = lax.broadcasted_iota(jnp.int32, (128, ORDERS), 0) * OWN
    slot_lane = lax.broadcasted_iota(jnp.int32, (128, ORDERS), 1)
    lane = lax.broadcasted_iota(jnp.int32, (128, 128), 1).astype(F32)

    def trig(j, carry):
        hot = jnp.where(owner_row + j == slot_lane, 1.0, 0.0).astype(BF)
        order = 32.0 * mm_nt(hot, coarse) + mm_nt(hot, fine)
        cos_q[j], sin_q[j] = circle(order * lane)
        cosine, sine = circle(order * (lane * 128.0))
        cos_b[j] = cosine * (1.0 / math.sqrt(ORDERS))
        sin_b[j] = sine * (1.0 / math.sqrt(ORDERS))
        return carry

    def make(j, carry):
        cq, sq, cb, sb = cos_q[j], sin_q[j], cos_b[j], sin_b[j]
        for b in range(10):
            ca, sa = cb[:, b : b + 1], sb[:, b : b + 1]
            cols = slice(b * 128, (b + 1) * 128)
            hi, lo = split(ca * cq - sa * sq)
            tab_hi[j, :, cols] = hi
            tab_lo[j, :, cols] = lo
            hi, lo = split(sa * cq + ca * sq)
            tab_hi[OWN + j, :, cols] = hi
            tab_lo[OWN + j, :, cols] = lo
        return carry

    lax.fori_loop(0, 1, lambda j, carry: make(j, trig(j, carry)), 0)
    arrived(part, NT - 1, 0)
    total = part[0]
    for s in range(1, NT):
        total = total + part[s]
    table[t] = total
    for i in range(1, NT):
        peer = (t + i) % NT
        send(table.at[t], table.at[t], 2, c, peer)
    lax.fori_loop(1, OWN, lambda j, carry: make(j, trig(j, carry)), 0)

    arrived(lat_recv, NC - 1, 1)
    slot32 = lax.shift_right_logical(lax.broadcasted_iota(jnp.int32, (16, 128), 1), 5)
    tail = []
    for first in (0, 4):
        parts = [jnp.zeros((16, 128), F32)] * 4
        for k in range(4):
            some = lat_recv[first + k, 64:, :].astype(F32)
            for g in range(4):
                moved = pltpu.roll(some, (32 * (k - g)) % 128, axis=1) if k != g else some
                parts[g] = jnp.where(slot32 == k, moved, parts[g])
        tail.append(jnp.concatenate(parts, axis=0).astype(BF))

    def rows_of(tab, s):
        own = slice(s * NT, (s + 1) * NT)
        return [tab[0:4, own, :].reshape(64, NLON), tab[OWN : OWN + 4, own, :].reshape(64, NLON)]

    def rest_of(tab, s):
        own = slice(s * NT, (s + 1) * NT)
        return [tab[4, own, :], tab[OWN + 4, own, :]]

    grid = jnp.zeros((64, NLON), F32)
    for tab in (tab_hi, tab_lo):
        for s in range(0, NC, 2):
            pair = jnp.concatenate([lat_recv[s, :64, :], lat_recv[s + 1, :64, :]], axis=1)
            grid = grid + mm(pair, jnp.concatenate(rows_of(tab, s) + rows_of(tab, s + 1), axis=0))
        rest_rows = [block for s in range(NC) for block in rest_of(tab, s)]
        grid = grid + mm(jnp.concatenate(tail, axis=1), jnp.concatenate(rest_rows, axis=0))
    arrived(table, NT - 1, 2)
    for b in range(10):
        x = grid[:, b * 128 : (b + 1) * 128]

        def diagonal(d):
            unit = b * 4 + d
            block = table[unit // PIECE, unit % PIECE]
            return jnp.broadcast_to(block[None], (8, 8, 128)).reshape(64, 128)

        adj = diagonal(0) * x
        for d in range(1, 4):
            m = diagonal(d)
            adj = adj + m * pltpu.roll(x, 128 - d, axis=1) + pltpu.roll(m * x, d, axis=1)
        hi, lo = split(adj)
        adj_ref[:64, b * 128 : (b + 1) * 128] = hi
        adj_ref[64:, b * 128 : (b + 1) * 128] = lo
    for i in range(10):
        both = mm_nt(adj_ref[...], tab_hi[i])
        spec_ref[i] = both[:64] + both[64:] + mm_nt(adj_ref[:64, :], tab_lo[i])
    spec_ref[10:] = jnp.zeros((6, 64, 128), F32)
    for p in range(8):
        block = spec_ref[:, p * 8 : (p + 1) * 8, :].reshape(128, 128)
        turn_ref[pl.ds(p, 128, stride=8), :] = block.T
    spec[...] = turn_ref[...].reshape(128, 8, 128).astype(BF)

    pl.semaphore_wait(ready, NT - 1)
    for pc, pt in peers:
        send(spec.at[pc * NT + pt], recv.at[me], 3, pc, pt)
    recv[me] = spec[me]

    same = (lax.broadcasted_iota(jnp.int32, (128, 128), 0) < 64) == (
        lax.broadcasted_iota(jnp.int32, (128, 128), 1) < 64
    )
    for j in range(OWN):
        one = leg[t * OWN + j]
        two = jnp.concatenate([one, one], axis=0)
        hi, lo = split(jnp.where(same, mm_nt(two, two), 0.0))
        normal[j, :128, :] = hi
        normal[j, 128:, :] = lo
    row = lax.broadcasted_iota(jnp.int32, (128, 640), 0)
    col = lax.broadcasted_iota(jnp.int32, (128, 640), 1)
    src_i, src_a = lax.shift_right_logical(row, 3), row & 7
    dst_i = (lax.shift_right_logical(col, 6) & 1) * OWN + lax.shift_right_logical(col, 7)
    dst_band, dst_a = lax.shift_right_logical(col, 3) & 7, col & 7
    hit = (src_a == dst_a) & (src_i == dst_i)
    for s in range(NC):
        perm[s * 128 : (s + 1) * 128, :] = jnp.where(hit & (dst_band == s), 1.0, 0.0).astype(BF)
    arrived(recv, ND - 1, 3)
    blocks = [recv[s * NT : (s + 1) * NT].astype(F32).reshape(128, 128).astype(BF) for s in range(NC)]
    gathered = mm(jnp.concatenate(blocks, axis=1), perm[...])
    left, right = [], []
    for j in range(OWN):
        mine = gathered[:, j * 128 : (j + 1) * 128].astype(BF)
        rows_out[j] = mine
        left += split(mm(jnp.concatenate([mine, mine], axis=1), normal[j]))
        right += [mine, mine]
    gram = mm_nt(jnp.concatenate(left, axis=1), jnp.concatenate(right, axis=1))
    for k in range(GROUP):
        g_part[k] = gram[k * 4 : (k + 1) * 4, :]

    def turn(j):
        one = leg[t * OWN + j]
        turned_out[j] = jnp.concatenate([one, one], axis=0).T

    seat = c * 4 + x_chip
    for d in steps:
        if d[2] == 0 and any(d):
            pc, px = bands[d[:2]], lax.rem(x_chip + d[3], 4)
            send(g_part.at[pc * 4 + px], g_group.at[seat], 4, pc, y_chip * 4 + px)
    g_group[seat] = g_part[seat]
    turn(0)
    turn(1)
    arrived(g_group, GROUP - 1, 4)
    total = g_group[0]
    for k in range(1, GROUP):
        total = total + g_group[k]
    mine_at = y_chip * GROUP + seat
    g_all[mine_at] = total * (1.0 / (2 * ORDERS * NDEG))
    for pc, pt in peers:
        send(g_all.at[mine_at], g_all.at[mine_at], 5, pc, pt)
    turn(2)
    turn(3)
    turn(4)
    arrived(g_all, ND - 1, 5)
    for k in range(GROUP):
        total = g_all[k]
        for q in range(1, 4):
            total = total + g_all[q * GROUP + k]
        gram_out[k * 4 : (k + 1) * 4, :] = total
    for ref, n, k in (
        (part, NT - 1, 0), (lat_send, NC - 1, 1), (table, NT - 1, 2), (spec, ND - 1, 3),
        (g_part, GROUP - 1, 4), (g_all, ND - 1, 5),
    ):
        sent(ref, n, k)


def circle(x):
    quarter = jnp.floor(x * (1.0 / 320.0) + 0.5)
    y = (x - quarter * 320.0) * (2.0 * math.pi / NLON)
    turn = quarter - 4.0 * jnp.floor(quarter * 0.25)
    z = y * y
    sine = y * (1.0 + z * (-1.0 / 6 + z * (1.0 / 120 + z * (-1.0 / 5040 + z * (1.0 / 362880)))))
    cosine = 1.0 + z * (-0.5 + z * (1.0 / 24 + z * (-1.0 / 720 + z * (1.0 / 40320 - z * (1.0 / 3628800)))))
    odd = (turn == 1.0) | (turn == 3.0)
    cos_x = jnp.where(odd, sine, cosine)
    sin_x = jnp.where(odd, cosine, sine)
    cos_x = jnp.where((turn == 1.0) | (turn == 2.0), -cos_x, cos_x)
    sin_x = jnp.where(turn >= 2.0, -sin_x, sin_x)
    return cos_x, sin_x


def front_stage(probes, legendre, orders, index, count, base, coef, weight):
    slots, obs = base.shape
    vm = pltpu.VMEM
    any_space = pl.BlockSpec(memory_space=pl.ANY)
    return pl.pallas_call(
        front_kernel,
        name="front_stage",
        out_shape=(jax.ShapeDtypeStruct((OWN, 128, 128), BF), jax.ShapeDtypeStruct((128, 128), F32),
                   jax.ShapeDtypeStruct((OWN, NDEG, 128), BF)),
        in_specs=[any_space] * 8,
        out_specs=(VM, VM, VM),
        scratch_shapes=[
            vm(legendre.shape, BF), vm(probes.shape, BF),
            vm(base.shape, jnp.int32), vm(coef.shape, BF), vm(weight.shape, F32),
            vm(orders.shape, jnp.int32), vm(index.shape, jnp.int32), vm(count.shape, jnp.int32),
            vm(weight.shape, F32),
            vm((slots, 32, 128), F32),
            vm((NT, PIECE, 8, 128), F32), vm((NT, PIECE, 8, 128), F32), vm((NT, PIECE, 8, 128), F32),
            vm((640, 128), F32),
            vm((NC, 80, 128), F32), vm((NC, 80, 128), BF), vm((NC, 80, 128), BF),
            vm((OWN, 128, 128), F32), vm((OWN, 128, 128), F32), vm((OWN, 128, 128), F32), vm((OWN, 128, 128), F32),
            vm((10, 128, NLON), BF), vm((10, 128, NLON), BF),
            vm((128, NLON), BF), vm((16, 64, 128), F32), vm((1024, 128), F32),
            vm((ND, 8, 128), BF), vm((ND, 8, 128), BF), vm((1024, 640), BF), vm((OWN, 256, 128), BF),
            vm((GROUP, 4, 128), F32), vm((GROUP, 4, 128), F32), vm((ND, 4, 128), F32),
            pltpu.SemaphoreType.DMA((6,)), pltpu.SemaphoreType.DMA((CHUNKS,)),
            pltpu.SemaphoreType.DMA((CHUNKS,)), pltpu.SemaphoreType.DMA((12,)),
            pltpu.SemaphoreType.REGULAR,
        ],
        compiler_params=pltpu.CompilerParams(
            collective_id=0, has_side_effects=True, vmem_limit_bytes=44 * 1024 * 1024
        ),
    )(*(pltpu.with_memory_space_constraint(x, pltpu.HBM) for x in (probes, legendre, orders, index, count, base, coef, weight)))


def exact(a, b, dims):
    return lax.dot_general(a, b, (dims, ((), ())), precision=HIGHEST, preferred_element_type=F32)


NN = ((1,), (0,))


def three(a, b, product):
    a_hi, a_lo = split(a)
    b_hi, b_lo = split(b)
    return product(a_hi, b_hi) + product(a_hi, b_lo) + product(a_lo, b_hi)


def factorize(gram, upper_ref, inv_ref):
    n = gram.shape[0]
    row = lax.broadcasted_iota(jnp.int32, (n, n), 0)
    col = lax.broadcasted_iota(jnp.int32, (n, n), 1)
    eye = jnp.where(row == col, 1.0, 0.0)
    half = jnp.where(row > col, 1.0, 0.5 * eye)
    diag = jnp.where(row == col, gram, 0.0)
    r_col = lax.rsqrt(jnp.sum(diag, axis=1, keepdims=True))
    r_row = lax.rsqrt(jnp.sum(diag, axis=0, keepdims=True))
    inverse = (eye - half * (gram * r_col * r_row - eye)) * r_row
    upper = three(inverse, gram, mm)
    error = eye
    for _ in range(3):
        error = three(upper, inverse, mm_nt) - eye
        step = three(half * error, jnp.concatenate([inverse, upper], axis=1), mm)
        inverse = inverse - step[:, :n]
        upper = upper - step[:, n:]
    inv_ref[...] = inverse
    upper_ref[...] = jnp.where(row <= col, upper, 0.0)
    failed = jnp.max(jnp.where(jnp.abs(error) < 1e-4, 0.0, 1.0))

    @pl.when(failed > 0.5)
    def _():
        def column(j, state):
            left, full, inv = state
            at_row, at_col = row == j, col == j
            line = jnp.sum(jnp.where(at_row, left, 0.0), axis=0, keepdims=True)
            down = jnp.sum(jnp.where(at_col, left, 0.0), axis=1, keepdims=True)
            pivot = jnp.sum(jnp.where(at_row & at_col, left, 0.0), keepdims=True)
            scale = 1.0 / jnp.sqrt(pivot)
            line = jnp.where(col[:1] >= j, line * scale, 0.0)
            below = jnp.where(row[:, :1] > j, down * scale, 0.0)
            inv_line = jnp.sum(jnp.where(at_row, inv, 0.0), axis=0, keepdims=True) * scale
            inv = jnp.where(at_row, inv_line, inv - below * inv_line)
            return left - below * line, jnp.where(at_row, line, full), inv

        _, full, inv = lax.fori_loop(0, n, column, (gram, jnp.zeros_like(gram), eye))
        upper_ref[...] = full
        inv_ref[...] = inv


def panel_kernel(gram_ref, rows_ref, leg_ref, out_ref, upper_ref, inv_ref, block, out_sem):
    factorize(gram_ref[...], upper_ref, inv_ref)
    hi, lo = split(inv_ref[...])
    left = lax.broadcasted_iota(jnp.int32, (128, 128), 1) < 64
    every = jnp.concatenate([rows_ref[j] for j in range(OWN)], axis=1)
    z_hi, z_lo = split(mm(hi, every) + mm(lo, every))
    writes = []
    for j in range(OWN):
        cols = slice(j * 128, (j + 1) * 128)
        hi_f, lo_f = z_hi[:, cols].astype(F32), z_lo[:, cols].astype(F32)
        cosine = jnp.where(left, hi_f, pltpu.roll(lo_f, 64, axis=1))
        sine = jnp.where(left, pltpu.roll(hi_f, 64, axis=1), lo_f)
        weights = jnp.concatenate([cosine, sine], axis=0).astype(BF)
        for start, stop in ((0, 608), (608, NDEG)):
            both = mm_nt(leg_ref[j, start:stop, :], weights)
            block[0, j, start:stop, :] = both[:, :128]
            block[1, j, start:stop, :] = both[:, 128:]
        for half in range(2):
            write = pltpu.make_async_copy(block.at[half, j], out_ref.at[half, j], out_sem.at[half, j])
            write.start()
            writes.append(write)
    for write in writes:
        write.wait()


def panel_stage(gram, rows, turned):
    any_space = pl.BlockSpec(memory_space=pl.ANY)
    return pl.pallas_call(
        panel_kernel,
        name="panel_stage",
        out_shape=(
            jax.ShapeDtypeStruct((2, OWN, NDEG, 128), F32),
            jax.ShapeDtypeStruct((128, 128), F32),
        ),
        in_specs=[VM, VM, VM],
        out_specs=(any_space, VM),
        scratch_shapes=[
            pltpu.VMEM((128, 128), F32),
            pltpu.VMEM((2, OWN, NDEG, 128), F32),
            pltpu.SemaphoreType.DMA((2, OWN)),
        ],
        compiler_params=pltpu.CompilerParams(vmem_limit_bytes=16 * 1024 * 1024),
    )(gram, rows, turned)


def on_device(
    probes, legendre, order_map, tile_index, tile_count, base_offset, stencil_weight, obs_weight
):
    rows, gram, turned = front_stage(
        probes, legendre, order_map.reshape(OWN, 128), tile_index[0], tile_count,
        base_offset[0, 0], stencil_weight[0, 0], obs_weight[0, 0],
    )
    panel, upper = panel_stage(gram, rows, turned)
    return (jnp.swapaxes(panel, 2, 3), upper)


def solution(mesh):
    return jax.shard_map(
        on_device,
        mesh=mesh,
        in_specs=(
            P(None, "coef", "track", None),
            P("coef", None, None),
            P(),
            P("coef", None, None),
            P("coef", None),
            P("coef", "track", None, None),
            P("coef", "track", None, None, None),
            P("coef", "track", None, None),
        ),
        out_specs=(P(None, ("coef", "track"), None, None), P()),
        check_vma=False,
    )
```
